32 devices in a mesh: groups: 2 (over y), trial: 4 (over x, core), dp: 4 (over z).
Axes of the slice: x: 2, y: 2, z: 4, core: 2. Of those that a mesh axis runs over, the one named last changes fastest.
Arguments:
- features: bfloat16 [8, 4, 592, 1536], P(('groups', 'dp'), 'trial'), parts along dimension 0, may hold values from -6 to 6
- owner: int32 [8], P(('groups', 'dp')), parts along dimension 0, may hold values from 0 to 3
- dilation_index: int32 [4], P('trial'), may hold values from 0 to 3
- labels: int32 [8, 592], P(('groups', 'dp')), parts along dimension 0, may hold values from 0 to 149
- input_weight: bfloat16 [4, 1536, 512], P('trial'), may hold values from -0.15625 to 0.15625
- taps: float32 [4, 9, 512], P('trial'), may hold values from -2 to 2
- output_weight: bfloat16 [4, 512, 150], P('trial'), may hold values from -1.0546875 to 1.0546875
Outputs:
- grad_in: float32 [8, 1536, 512], P(('groups', 'trial'), 'dp'), parts along dimension 0
- grad_taps: float32 [8, 9, 512], P(('groups', 'trial')), parts along dimension 0
- grad_out: float32 [8, 512, 150], P(('groups', 'trial'), 'dp'), parts along dimension 0
- noise_norms: float32 [8, 2, 3], P(('groups', 'trial')), parts along dimension 0
The draws below stay inside these ranges and needn't reach their ends.
There are 2 independent parts, one for each index of `groups`. The reference program is written for one: setup_inputs(seed, part) draws one part's arguments, and reference() takes and returns one part's arrays. A program takes and returns all parts, laid end to end along the dimension named above; an argument that names none is the same for every part. Nothing has to cross between parts.
All inputs are finite; a program needn't handle non-finite values.
Results may differ from the reference program's by a relative error of at most 0.0015.
The reference program's roundings to bfloat16 on the way count: a program that leaves them out, or rounds other values in their place, can miss the bound.
Values may be sent and summed in bfloat16 or wider, within the bound.
No kernel may reach another device: no remote copies, remote signals or barrier semaphores. Data moves between devices by JAX's collectives and lax.ppermute only.
A program may use at most 64 MiB of HBM per device.

```python
import jax
import jax.numpy as jnp
from jax import lax

C = 1536
H = 512
K = 150
PC = 37
ROWS = 592
MB = 4
SLOTS = 4
HEAD_TRIALS = 4


def plant(array, stream_key, low, top_value):
    spot = [jax.random.randint(jax.random.fold_in(stream_key, axis), (), 0, length) for axis, length in enumerate(array.shape)]
    longest = array.shape.index(max(array.shape))
    beside = spot[:longest] + [(spot[longest] + 1) % array.shape[longest]] + spot[longest + 1:]
    return array.at[tuple(spot)].set(low).at[tuple(beside)].set(top_value)


def levels(rng, extent, pieces, low, largest):
    factor_of = 1.0
    for position, parts in pieces:
        draws = jax.random.uniform(jax.random.fold_in(jax.random.fold_in(rng, 6), position), (parts,), jnp.float32, low / len(pieces), largest / len(pieces))
        factor_of = factor_of * jnp.repeat(jnp.exp(draws), extent[position] // parts).reshape((-1,) + (1,) * (len(extent) - 1 - position))
    return factor_of


def normal_values(rng, extent, spread, limit, pieces=(), kind=jnp.bfloat16):
    result = jax.random.normal(rng, extent, jnp.float32) * spread
    if len(pieces) > 0:
        result = levels(rng, extent, pieces, -0.22, 0.18) * result
    return jnp.clip(result, min=-limit, max=limit).astype(kind)


def setup_inputs(seed: int = 0, part: int = 0) -> dict:
    seeds = jax.random.split(jax.random.key(seed), 8)
    part_splits = jax.random.split(jax.random.fold_in(seeds[7], part), 8)
    return {
        "features": normal_values(part_splits[0], (MB, SLOTS, ROWS, C), 1.0, 6.0, ((0, 4), (1, 4))),
        "owner": plant(jax.random.randint(part_splits[1], (MB,), 0, SLOTS), jax.random.fold_in(part_splits[1], 1), 0, SLOTS - 1).astype(jnp.int32),
        "dilation_index": plant(jax.random.randint(seeds[2], (HEAD_TRIALS,), 0, 4), jax.random.fold_in(seeds[2], 1), 0, 3).astype(jnp.int32),
        "labels": plant(jax.random.randint(part_splits[3], (MB, ROWS), 0, K), jax.random.fold_in(part_splits[3], 1), 0, K - 1).astype(jnp.int32),
        "input_weight": normal_values(seeds[4], (HEAD_TRIALS, C, H), C ** -0.5, 0.15625, ((0, 4),)),
        "taps": normal_values(seeds[5], (HEAD_TRIALS, 9, H), 9 ** -0.5, 2.0, ((0, 4),), jnp.float32),
        "output_weight": normal_values(seeds[6], (HEAD_TRIALS, H, K), (4.0 / H ** 0.5), 1.0546875, ((0, 4),)),
    }


def gelu_parts(value):
    inner = 0.7978845608 * (value + 0.044715 * value * value * value)
    tanh_val = jnp.tanh(inner)
    out_val = 0.5 * value * (1.0 + tanh_val)
    slope = 0.5 * (1.0 + tanh_val) + 0.5 * value * (1.0 - tanh_val * tanh_val) * 0.7978845608 * (1.0 + 3.0 * 0.044715 * value * value)
    return out_val, slope


def head_backward(xrows, label_row, weight_in, tap_table, weight_out, dilation_rate):
    rows_count = xrows.shape[0]
    hidden_width = weight_in.shape[1]
    classes = weight_out.shape[1]
    slab_rows = rows_count // PC
    pre = jnp.dot(xrows, weight_in, preferred_element_type=jnp.float32).reshape(slab_rows, PC, hidden_width)
    padded = jnp.pad(pre, ((4, 4), (4, 4), (0, 0)))
    zero_idx = jnp.int32(0)
    shifted = []
    for off_a in (-1, 0, 1):
        for off_b in (-1, 0, 1):
            start_a = (4 + dilation_rate * off_a).astype(jnp.int32)
            start_b = (4 + dilation_rate * off_b).astype(jnp.int32)
            shifted.append(lax.dynamic_slice(padded, (start_a, start_b, zero_idx), (slab_rows, PC, hidden_width)))
    yval = shifted[0] * tap_table[0]
    for index in range(1, 9):
        yval = yval + shifted[index] * tap_table[index]
    act, slope = gelu_parts(yval)
    hid = act.astype(jnp.bfloat16).reshape(rows_count, hidden_width)
    logits = jnp.dot(hid, weight_out, preferred_element_type=jnp.float32)
    prob = jax.nn.softmax(logits, axis=-1)
    onehot = (label_row[:, None] == jnp.arange(classes, dtype=jnp.int32)[None, :]).astype(jnp.float32)
    dlog = (prob - onehot).astype(jnp.bfloat16)
    g_out = jnp.dot(hid.T, dlog, preferred_element_type=jnp.float32)
    dhid = jnp.dot(dlog, weight_out.T, preferred_element_type=jnp.float32).reshape(slab_rows, PC, hidden_width)
    dyval = dhid * slope
    g_taps = jnp.stack([jnp.sum(dyval * shifted[index], axis=(0, 1)) for index in range(9)])
    padded_dy = jnp.pad(dyval, ((4, 4), (4, 4), (0, 0)))
    dpre = jnp.zeros((slab_rows, PC, hidden_width), jnp.float32)
    index = 0
    for off_a in (-1, 0, 1):
        for off_b in (-1, 0, 1):
            start_a = (4 - dilation_rate * off_a).astype(jnp.int32)
            start_b = (4 - dilation_rate * off_b).astype(jnp.int32)
            dpre = dpre + tap_table[index] * lax.dynamic_slice(padded_dy, (start_a, start_b, zero_idx), (slab_rows, PC, hidden_width))
            index += 1
    dpre = dpre.astype(jnp.bfloat16).reshape(rows_count, hidden_width)
    return g_taps, g_out, dpre


def reference(features, owner, dilation_index, labels, input_weight, taps, output_weight):
    def trial_values(trial_index):
        weight_in = input_weight[trial_index]
        tap_table = taps[trial_index]
        weight_out = output_weight[trial_index]
        dilation_rate = dilation_index[trial_index] + 1

        def per_batch(carry, batch_position):
            sum_in, sum_taps, sum_out, squares = carry
            slot_row = features[batch_position]
            xrows = lax.dynamic_index_in_dim(slot_row, owner[batch_position], 0, keepdims=False)
            g_taps, g_out, dpre = head_backward(xrows, labels[batch_position], weight_in, tap_table, weight_out, dilation_rate)
            g_in = jnp.dot(xrows.T, dpre, preferred_element_type=jnp.float32)
            local = jnp.stack([jnp.sum(g_in * g_in), jnp.sum(g_taps * g_taps), jnp.sum(g_out * g_out)])
            return (sum_in + g_in, sum_taps + g_taps, sum_out + g_out, squares + local), None

        start = (jnp.zeros((C, H), jnp.float32), jnp.zeros((9, H), jnp.float32), jnp.zeros((H, K), jnp.float32), jnp.zeros((3,), jnp.float32))
        (sum_in, sum_taps, sum_out, squares), _ = lax.scan(per_batch, start, jnp.arange(MB, dtype=jnp.int32))
        totals = jnp.stack([jnp.sum(sum_in * sum_in), jnp.sum(sum_taps * sum_taps), jnp.sum(sum_out * sum_out)])
        norms = jnp.log(1e-12 + jnp.stack([squares, totals]))
        return sum_in, sum_taps, sum_out, norms

    grad_in, grad_taps, grad_out, noise_norms = lax.map(trial_values, jnp.arange(HEAD_TRIALS, dtype=jnp.int32))
    return grad_in, grad_taps, grad_out, noise_norms
```

```python
import jax
import jax.numpy as jnp
from jax import lax
from jax.sharding import PartitionSpec as P

PC = 37


def broadcast(block, axis, size, source):
    if size != 4:
        block = jnp.where(lax.axis_index(axis) == source, block, jnp.zeros_like(block))
        return lax.psum(block, axis)
    me = lax.axis_index(axis)
    core = me % 2
    mate = [(0, 1), (1, 0), (2, 3), (3, 2)]
    across = [(0, 2), (2, 0), (1, 3), (3, 1)]
    width = block.shape[1] // 2
    low, high = block[:, :width], block[:, width:]
    got = lax.ppermute(jnp.where(core == 0, high, low), axis, mate)
    kept = jnp.where(core == 0, low, high)
    held = jnp.where(source % 2 == core, kept, got)
    other = lax.ppermute(held, axis, across)
    here = (source // 2) == (me // 2)
    back_held = lax.ppermute(held, axis, mate)
    back_other = lax.ppermute(other, axis, mate)
    first = jnp.where(here, held, other)
    second = jnp.where(here, back_held, back_other)
    return jnp.where(
        core == 0,
        jnp.concatenate([first, second], axis=1),
        jnp.concatenate([second, first], axis=1),
    )


def gelu_parts(value):
    inner = 0.7978845608 * (value + 0.044715 * value * value * value)
    tanh_val = jnp.tanh(inner)
    out_val = 0.5 * value * (1.0 + tanh_val)
    slope = 0.5 * (1.0 + tanh_val) + 0.5 * value * (1.0 - tanh_val * tanh_val) * 0.7978845608 * (
        1.0 + 3.0 * 0.044715 * value * value
    )
    return (out_val, slope)


def head_backward(xrows, label_row, weight_in, tap_table, weight_out, dilation_rate):
    rows_count = xrows.shape[0]
    hidden_width = weight_in.shape[1]
    classes = weight_out.shape[1]
    slab_rows = rows_count // PC
    pre = jnp.dot(xrows, weight_in, preferred_element_type=jnp.float32).reshape(
        slab_rows, PC, hidden_width
    )
    padded = jnp.pad(pre, ((4, 4), (4, 4), (0, 0)))
    zero_idx = jnp.int32(0)
    shifted = []
    for off_a in (-1, 0, 1):
        for off_b in (-1, 0, 1):
            start_a = 4 + dilation_rate * off_a
            start_b = 4 + dilation_rate * off_b
            shifted.append(
                lax.dynamic_slice(
                    padded, (start_a, start_b, zero_idx), (slab_rows, PC, hidden_width)
                )
            )
    yval = shifted[0] * tap_table[0]
    for index in range(1, 9):
        yval = yval + shifted[index] * tap_table[index]
    act, slope = gelu_parts(yval)
    hid = act.astype(jnp.bfloat16).reshape(rows_count, hidden_width)
    logits = jnp.dot(hid, weight_out, preferred_element_type=jnp.float32)
    prob = jax.nn.softmax(logits, axis=-1)
    onehot = (label_row[:, None] == jnp.arange(classes, dtype=jnp.int32)[None, :]).astype(
        jnp.float32
    )
    dlog = (prob - onehot).astype(jnp.bfloat16)
    g_out = jnp.dot(hid.T, dlog, preferred_element_type=jnp.float32)
    dhid = jnp.dot(dlog, weight_out.T, preferred_element_type=jnp.float32).reshape(
        slab_rows, PC, hidden_width
    )
    dyval = dhid * slope
    g_taps = jnp.stack([jnp.sum(dyval * shifted[index], axis=(0, 1)) for index in range(9)])
    padded_dy = jnp.pad(dyval, ((4, 4), (4, 4), (0, 0)))
    dpre = jnp.zeros((slab_rows, PC, hidden_width), jnp.float32)
    index = 0
    for off_a in (-1, 0, 1):
        for off_b in (-1, 0, 1):
            start_a = 4 - dilation_rate * off_a
            start_b = 4 - dilation_rate * off_b
            dpre = dpre + tap_table[index] * lax.dynamic_slice(
                padded_dy, (start_a, start_b, zero_idx), (slab_rows, PC, hidden_width)
            )
            index += 1
    dpre = dpre.astype(jnp.bfloat16).reshape(rows_count, hidden_width)
    return (g_taps, g_out, dpre)


def shift(value, step, size):
    return lax.ppermute(value, "dp", [(i, (i + step) % size) for i in range(size)])


def per_device(dp, trials, features, owner, dilation_index, labels, input_weight, taps, output_weight):
    xrows = broadcast(features[0, 0], "trial", trials, owner[0])
    dilation_rate = dilation_index[0] + 1
    g_taps, g_out, dpre = head_backward(
        xrows, labels[0], input_weight[0], taps[0], output_weight[0], dilation_rate
    )
    me = lax.axis_index("dp")
    depth = xrows.shape[1] // dp
    depth_out = g_out.shape[0] // dp

    def block(array, index, size, axis):
        return lax.dynamic_slice_in_dim(array, index * size, size, axis)

    share_out = block(g_out, me, depth_out, 0)
    for step in range(1, dp):
        share_out = share_out + shift(block(g_out, (me + step) % dp, depth_out, 0), step, dp)
    share_in = None
    norm_in = 0.0
    got = []
    for step in list(range(1, dp)) + [0]:
        part = jnp.dot(
            block(xrows, (me + step) % dp, depth, 1).T, dpre, preferred_element_type=jnp.float32
        )
        norm_in = norm_in + jnp.sum(part * part)
        if step:
            got.append(shift(part.astype(jnp.bfloat16), step, dp))
        else:
            share_in = part
    local = jnp.stack([norm_in, jnp.sum(g_taps * g_taps), jnp.sum(g_out * g_out)])
    packed = jnp.concatenate([g_taps, jnp.zeros((7, g_taps.shape[1]), jnp.float32)])
    packed = packed.at[9, :3].set(local)
    total = packed
    for step in range(1, dp):
        total = total + shift(packed, step, dp)
    total_taps, squares = total[:9], total[9, :3]
    for value in got:
        share_in = share_in + value.astype(jnp.float32)
    share_sq = jnp.stack([jnp.sum(share_in * share_in), jnp.sum(share_out * share_out)])
    share_sq = jnp.broadcast_to(jnp.pad(share_sq, (0, 126))[None], (8, 128))
    share_total = share_sq
    for step in range(1, dp):
        share_total = share_total + shift(share_sq, step, dp)
    totals = jnp.stack([share_total[0, 0], jnp.sum(total_taps * total_taps), share_total[0, 1]])
    norms = jnp.log(1e-12 + jnp.stack([squares, totals]))
    return (share_in[None], total_taps[None], share_out[None], norms[None])


def solution(mesh):
    dp, trials = mesh.shape["dp"], mesh.shape["trial"]
    placed = (
        P(("groups", "dp"), "trial", None, None),
        P(("groups", "dp")),
        P("trial"),
        P(("groups", "dp"), None),
        P("trial", None, None),
        P("trial", None, None),
        P("trial", None, None),
    )

    def step(*args):
        return per_device(dp, trials, *args)

    return jax.shard_map(
        step,
        mesh=mesh,
        in_specs=placed,
        out_specs=(
            P(("groups", "trial"), "dp", None),
            P(("groups", "trial"), None, None),
            P(("groups", "trial"), "dp", None),
            P(("groups", "trial"), None, None),
        ),
        check_vma=False,
    )
```

```python
import functools

import jax
import jax.numpy as jnp
from jax import lax
from jax.experimental import pallas as pl
from jax.experimental.pallas import tpu as pltpu
from jax.sharding import PartitionSpec as P

PC = 37
LANES = 128
STEP = 32
REACH = 4
OFFSETS = [(a, b) for a in (-1, 0, 1) for b in (-1, 0, 1)]
X_LIMIT = 6.0


def pieces(block, axis, size, source):
    if size != 4:
        block = jnp.where(lax.axis_index(axis) == source, block, jnp.zeros_like(block))
        block = lax.psum(block, axis)
        width = block.shape[1] // 2
        low, high = block[:, :width], block[:, width:]
        zero = jnp.int32(0)
        return zero + 1, zero, (low, low, high, high)
    me = lax.axis_index(axis)
    core = me % 2
    mate = [(0, 1), (1, 0), (2, 3), (3, 2)]
    across = [(0, 2), (2, 0), (1, 3), (3, 1)]
    width = block.shape[1] // 2
    low, high = block[:, :width], block[:, width:]
    got = lax.ppermute(jnp.where(core == 0, high, low), axis, mate)
    kept = jnp.where(core == 0, low, high)
    held = jnp.where(source % 2 == core, kept, got)
    other = lax.ppermute(held, axis, across)
    here = ((source // 2) == (me // 2)).astype(jnp.int32)
    back_held = lax.ppermute(held, axis, mate)
    back_other = lax.ppermute(other, axis, mate)
    return here, core, (held, other, back_held, back_other)


def gelu_parts(value):
    inner = 0.7978845608 * (value + 0.044715 * value * value * value)
    tanh_val = jnp.tanh(inner)
    out_val = 0.5 * value * (1.0 + tanh_val)
    slope = 0.5 * (1.0 + tanh_val) + 0.5 * value * (1.0 - tanh_val * tanh_val) * 0.7978845608 * (
        1.0 + 3.0 * 0.044715 * value * value
    )
    return (out_val, slope)


def head_kernel(
    dp,
    classes,
    scalars,
    held,
    other,
    back_held,
    back_other,
    weight_in,
    taps,
    weight_out,
    onehot,
    after,
    before,
    x_out,
    dpre_out,
    stats_out,
    *rest,
):
    packs = rest[:dp]
    x_vmem, pre, dys, slope, hid, dlog, gout, sem_in, sem_out = rest[dp:]
    rows = x_vmem.shape[0]
    width = x_vmem.shape[1] // 2
    hidden = weight_in.shape[1]
    chunks = hidden // LANES
    guard = REACH * (PC + 1)
    padded = slope.shape[1]
    blocks = padded // STEP
    dil, here, core, me = scalars[0], scalars[1], scalars[2], scalars[3]

    def fetch(source, place, index):
        column = pl.multiple_of(place * width, LANES)
        return pltpu.make_async_copy(source, x_vmem.at[:, pl.ds(column, width)], sem_in.at[index])

    @pl.when(here == 1)
    def _():
        fetch(held, core, 0).start()
        fetch(back_held, 1 - core, 1).start()

    @pl.when(here == 0)
    def _():
        fetch(other, core, 0).start()
        fetch(back_other, 1 - core, 1).start()

    for shift in range(3):
        for c in range(chunks):
            for ref in (pre, dys):
                ref[shift, c, :guard, :] = jnp.zeros((guard, LANES), jnp.float32)
                tail = ref.shape[2] - guard - rows
                ref[shift, c, guard + rows :, :] = jnp.zeros((tail, LANES), jnp.float32)
    fetch(held, core, 0).wait()
    fetch(back_held, 1 - core, 1).wait()
    save = pltpu.make_async_copy(x_vmem, x_out, sem_out)
    save.start()

    masks = (after, None, before)
    for n in range(hidden // 256):
        value = jnp.dot(
            x_vmem[...], weight_in[:, 256 * n : 256 * n + 256], preferred_element_type=jnp.float32
        )
        for h in range(2):
            part = value[:, LANES * h : LANES * h + LANES]
            for shift in range(3):
                mask = (before, None, after)[shift]
                pre[shift, 2 * n + h, guard : guard + rows, :] = (
                    part if mask is None else part * mask[...]
                )

    starts = [dil * (PC * a + b) for a, b in OFFSETS]

    def forward(i, carry):
        row = pl.multiple_of(i * STEP, STEP)
        for c in range(chunks):
            total = None
            for k in range(9):
                term = (
                    pre[k % 3, c, pl.ds(guard + row + starts[k], STEP), :]
                    * taps[k : k + 1, LANES * c : LANES * c + LANES]
                )
                total = term if total is None else total + term
            act, grad = gelu_parts(total)
            slope[c, pl.ds(row, STEP), :] = grad
            hid[pl.ds(row, STEP), LANES * c : LANES * c + LANES] = act.astype(jnp.bfloat16)
        return carry

    lax.fori_loop(0, blocks, forward, 0)

    logits = jnp.dot(hid[:rows, :], weight_out[...], preferred_element_type=jnp.float32)
    lane = lax.broadcasted_iota(jnp.int32, logits.shape, 1)
    logits = jnp.where(lane < classes, logits, -1e30)
    peak = jnp.max(logits, axis=1, keepdims=True)
    power = jnp.exp(logits - peak)
    prob = power / jnp.sum(power, axis=1, keepdims=True)
    dlog[...] = (prob - onehot[...].astype(jnp.float32)).astype(jnp.bfloat16)

    gout[...] = lax.dot_general(
        hid[:rows, :], dlog[...], (((0,), (0,)), ((), ())), preferred_element_type=jnp.float32
    )
    for n in range(hidden // 256):
        value = lax.dot_general(
            dlog[...],
            weight_out[256 * n : 256 * n + 256, :],
            (((1,), (1,)), ((), ())),
            preferred_element_type=jnp.float32,
        )
        for h in range(2):
            c = 2 * n + h
            part = value[:, LANES * h : LANES * h + LANES] * slope[c, :rows, :]
            for shift in range(3):
                mask = (after, None, before)[shift]
                dys[shift, c, guard : guard + rows, :] = part if mask is None else part * mask[...]

    def fold(value):
        return jnp.sum(value.reshape(STEP // 8, 8, LANES), axis=0)

    biggest = jnp.zeros((8, LANES), jnp.float32)
    for c in range(chunks):
        column = slice(LANES * c, LANES * c + LANES)

        def backward(i, carry):
            row = pl.multiple_of(i * STEP, STEP)
            sums, top = carry
            dy = dys[1, c, pl.ds(guard + row, STEP), :]
            total = None
            out = []
            for k in range(9):
                out.append(sums[k] + fold(dy * pre[k % 3, c, pl.ds(guard + row + starts[k], STEP), :]))
                term = (
                    dys[k % 3, c, pl.ds(guard + row - starts[k], STEP), :]
                    * taps[k : k + 1, column]
                )
                total = term if total is None else total + term
            dpre_out[pl.ds(row, STEP), column] = total.astype(jnp.bfloat16)
            size = jnp.max(jnp.abs(total).reshape(STEP // 8, 8, LANES), axis=0)
            return tuple(out), jnp.maximum(top, size)

        zeros = tuple(jnp.zeros((8, LANES), jnp.float32) for _ in range(9))
        sums, biggest = lax.fori_loop(0, blocks, backward, (zeros, biggest))
        square = jnp.zeros((1, LANES), jnp.float32)
        for k in range(9):
            value = jnp.sum(sums[k], axis=0, keepdims=True)
            square = square + value * value
            for pack in packs:
                pack[depth_of(packs) + 2 * k + c // 2, LANES * (c % 2) : LANES * (c % 2) + LANES] = value[0]
        stats_out[0:1, column] = square
    depth = hidden // dp
    top = jnp.full((1, 256), jnp.max(biggest), jnp.float32)
    for s in range(dp):
        place = lax.rem(me + s, dp)
        packs[s][:depth, :] = gout[pl.ds(pl.multiple_of(place * depth, 8), depth), :]
        packs[s][depth + 18 : depth + 19, :] = top
    stats_out[1:2, :256] = jnp.sum(gout[...] * gout[...], axis=0, keepdims=True)
    save.wait()


def depth_of(packs):
    return packs[0].shape[0] - 24


def head_backward(dp, here, core, me, halves, onehot, weight_in, taps, weight_out, dil, masks):
    rows = onehot.shape[0]
    hidden = weight_in.shape[1]
    chunks = hidden // LANES
    padded = pl.cdiv(rows, STEP) * STEP
    guard = REACH * (PC + 1)
    depth = hidden // dp
    scalars = jnp.stack([dil, here, core, me]).astype(jnp.int32)
    vmem = pl.BlockSpec(memory_space=pltpu.VMEM)
    anywhere = pl.BlockSpec(memory_space=pl.ANY)
    classes = weight_out.shape[1]
    weight_out = jnp.pad(weight_out, ((0, 0), (0, 256 - classes)))
    span = 2 * guard + padded
    return pl.pallas_call(
        functools.partial(head_kernel, dp, classes),
        out_shape=[
            jax.ShapeDtypeStruct((rows, weight_in.shape[0]), jnp.bfloat16),
            jax.ShapeDtypeStruct((padded, hidden), jnp.bfloat16),
            jax.ShapeDtypeStruct((8, hidden), jnp.float32),
        ]
        + [jax.ShapeDtypeStruct((depth + 24, 256), jnp.float32)] * dp,
        in_specs=[pl.BlockSpec(memory_space=pltpu.SMEM)] + [anywhere] * 4 + [vmem] * 6,
        out_specs=[anywhere, vmem, vmem] + [vmem] * dp,
        scratch_shapes=[
            pltpu.VMEM((rows, weight_in.shape[0]), jnp.bfloat16),
            pltpu.VMEM((3, chunks, span, LANES), jnp.float32),
            pltpu.VMEM((3, chunks, span, LANES), jnp.float32),
            pltpu.VMEM((chunks, padded, LANES), jnp.float32),
            pltpu.VMEM((padded, hidden), jnp.bfloat16),
            pltpu.VMEM((rows, 256), jnp.bfloat16),
            pltpu.VMEM((hidden, 256), jnp.float32),
            pltpu.SemaphoreType.DMA((2,)),
            pltpu.SemaphoreType.DMA,
        ],
        compiler_params=pltpu.CompilerParams(vmem_limit_bytes=48 * 1024 * 1024),
        name="head",
    )(scalars, *halves, weight_in, taps, weight_out, onehot, *masks)


def shift(value, step, size):
    return lax.ppermute(value, "dp", [(i, (i + step) % size) for i in range(size)])


def per_device(dp, trials, features, owner, dilation_index, labels, input_weight, taps, output_weight):
    here, core, halves = pieces(features[0, 0], "trial", trials, owner[0])
    me = lax.axis_index("dp")
    dil = dilation_index[0] + 1
    rows = features.shape[2]
    onehot = (labels[0][:, None] == jnp.arange(256, dtype=jnp.int32)[None, :]).astype(jnp.bfloat16)
    column = lax.broadcasted_iota(jnp.int32, (rows, LANES), 0) % PC
    before = (column < PC - dil).astype(jnp.float32)
    after = (column >= dil).astype(jnp.float32)
    xrows, dpre, stats, *packs = head_backward(
        dp, here, core, me, halves, onehot, input_weight[0], taps[0], output_weight[0], dil, (after, before)
    )
    dpre = dpre[:rows]
    classes = output_weight.shape[2]
    depth = xrows.shape[1] // dp
    depth_out = input_weight.shape[2] // dp
    sent = [shift(packs[s], s, dp) for s in range(1, dp)]
    limit = X_LIMIT * rows
    room = 32768.0 / limit

    def bound(pack):
        return jnp.maximum(pack[depth_out + 18, 0], 1e-30)

    scale = room / bound(packs[0])
    norm_in = 0.0
    got = []
    share_in = None
    for step in list(range(1, dp)) + [0]:
        place = (me + step) % dp
        part = jnp.dot(
            lax.dynamic_slice_in_dim(xrows, place * depth, depth, 1).T,
            dpre,
            preferred_element_type=jnp.float32,
        )
        norm_in = norm_in + jnp.sum(part * part)
        if step:
            got.append(shift((part * scale).astype(jnp.float16), step, dp))
        else:
            share_in = part
    total = packs[0]
    for pack in sent:
        total = total + pack
    share_out = total[:depth_out, :classes]
    total_taps = total[depth_out : depth_out + 18].reshape(9, -1)
    for value, pack in zip(got, sent):
        share_in = share_in + value.astype(jnp.float32) * (bound(pack) * (1.0 / room))
    line = jnp.stack(
        [
            jnp.sum(share_in * share_in),
            jnp.sum(share_out * share_out),
            norm_in,
            jnp.sum(stats[0]),
            jnp.sum(stats[1, :256]),
        ]
    )
    line = jnp.broadcast_to(jnp.pad(line, (0, 123))[None], (8, 128))
    whole = line
    for step in range(1, dp):
        whole = whole + shift(line, step, dp)
    totals = jnp.stack([whole[0, 0], jnp.sum(total_taps * total_taps), whole[0, 1]])
    norms = jnp.log(1e-12 + jnp.stack([whole[0, 2:5], totals]))
    return (share_in[None], total_taps[None], share_out[None], norms[None])


def solution(mesh):
    dp, trials = mesh.shape["dp"], mesh.shape["trial"]
    placed = (
        P(("groups", "dp"), "trial", None, None),
        P(("groups", "dp")),
        P("trial"),
        P(("groups", "dp"), None),
        P("trial", None, None),
        P("trial", None, None),
        P("trial", None, None),
    )

    def step(*args):
        return per_device(dp, trials, *args)

    return jax.shard_map(
        step,
        mesh=mesh,
        in_specs=placed,
        out_specs=(
            P(("groups", "trial"), "dp", None),
            P(("groups", "trial"), None, None),
            P(("groups", "trial"), "dp", None),
            P(("groups", "trial"), None, None),
        ),
        check_vma=False,
    )
```

```python
import functools

import jax
import jax.numpy as jnp
from jax import lax
from jax.experimental import pallas as pl
from jax.experimental.pallas import tpu as pltpu
from jax.sharding import PartitionSpec as P

PC = 37
LANES = 128
STEP = 32
REACH = 4
OFFSETS = [(a, b) for a in (-1, 0, 1) for b in (-1, 0, 1)]
X_LIMIT = 6.0


def pieces(block, axis, size, source):
    if size != 4:
        block = jnp.where(lax.axis_index(axis) == source, block, jnp.zeros_like(block))
        block = lax.psum(block, axis)
        width = block.shape[1] // 2
        low, high = block[:, :width], block[:, width:]
        zero = jnp.int32(0)
        return zero + 1, zero, (low, low, high, high)
    me = lax.axis_index(axis)
    core = me % 2
    mate = [(0, 1), (1, 0), (2, 3), (3, 2)]
    across = [(0, 2), (2, 0), (1, 3), (3, 1)]
    width = block.shape[1] // 2
    low, high = block[:, :width], block[:, width:]
    got = lax.ppermute(jnp.where(core == 0, high, low), axis, mate)
    kept = jnp.where(core == 0, low, high)
    held = jnp.where(source % 2 == core, kept, got)
    other = lax.ppermute(held, axis, across)
    here = ((source // 2) == (me // 2)).astype(jnp.int32)
    back_held = lax.ppermute(held, axis, mate)
    back_other = lax.ppermute(other, axis, mate)
    return here, core, (held, other, back_held, back_other)


def gelu_parts(value):
    inner = 0.7978845608 * (value + 0.044715 * value * value * value)
    tanh_val = jnp.tanh(inner)
    out_val = 0.5 * value * (1.0 + tanh_val)
    slope = 0.5 * (1.0 + tanh_val) + 0.5 * value * (1.0 - tanh_val * tanh_val) * 0.7978845608 * (
        1.0 + 3.0 * 0.044715 * value * value
    )
    return (out_val, slope)


def head_kernel(
    dp,
    classes,
    scalars,
    held,
    other,
    back_held,
    back_other,
    weight_in,
    taps,
    weight_out,
    onehot,
    after,
    before,
    x_out,
    dpre_out,
    stats_out,
    *rest,
):
    packs = rest[:dp]
    x_vmem, pre, dys, slope, hid, dlog, gout, sem_in, sem_out = rest[dp:]
    rows = x_vmem.shape[0]
    width = x_vmem.shape[1] // 2
    hidden = weight_in.shape[1]
    chunks = hidden // LANES
    guard = REACH * (PC + 1)
    dil, here, core, me = scalars[0], scalars[1], scalars[2], scalars[3]

    def fetch(source, place, index):
        column = pl.multiple_of(place * width, LANES)
        return pltpu.make_async_copy(source, x_vmem.at[:, pl.ds(column, width)], sem_in.at[index])

    @pl.when(here == 1)
    def _():
        fetch(held, core, 0).start()
        fetch(back_held, 1 - core, 1).start()

    @pl.when(here == 0)
    def _():
        fetch(other, core, 0).start()
        fetch(back_other, 1 - core, 1).start()

    for shift in range(3):
        for c in range(chunks):
            for ref in (pre, dys):
                ref[shift, c, :guard, :] = jnp.zeros((guard, LANES), jnp.float32)
                tail = ref.shape[2] - guard - rows
                ref[shift, c, guard + rows :, :] = jnp.zeros((tail, LANES), jnp.float32)
    fetch(held, core, 0).wait()
    fetch(back_held, 1 - core, 1).wait()
    save = pltpu.make_async_copy(x_vmem, x_out, sem_out)
    save.start()

    masks = (after, None, before)
    for n in range(hidden // 256):
        value = jnp.dot(
            x_vmem[...], weight_in[:, 256 * n : 256 * n + 256], preferred_element_type=jnp.float32
        )
        for h in range(2):
            part = value[:, LANES * h : LANES * h + LANES]
            for shift in range(3):
                mask = (before, None, after)[shift]
                pre[shift, 2 * n + h, guard : guard + rows, :] = (
                    part if mask is None else part * mask[...]
                )

    starts = [dil * (PC * a + b) for a, b in OFFSETS]

    def forward(row, count):
        for c in range(chunks):
            total = None
            for k in range(9):
                term = (
                    pre[k % 3, c, pl.ds(guard + row + starts[k], count), :]
                    * taps[k : k + 1, LANES * c : LANES * c + LANES]
                )
                total = term if total is None else total + term
            act, grad = gelu_parts(total)
            slope[c, pl.ds(row, count), :] = grad
            hid[pl.ds(row, count), LANES * c : LANES * c + LANES] = act.astype(jnp.bfloat16)

    whole = rows // STEP
    left = rows - whole * STEP

    @pl.loop(0, whole)
    def _(i):
        forward(pl.multiple_of(i * STEP, STEP), STEP)

    if left:
        forward(whole * STEP, left)

    logits = jnp.dot(hid[...], weight_out[...], preferred_element_type=jnp.float32)
    lane = lax.broadcasted_iota(jnp.int32, logits.shape, 1)
    logits = jnp.where(lane < classes, logits, -1e30)
    peak = jnp.max(logits, axis=1, keepdims=True)
    power = jnp.exp(logits - peak)
    prob = power / jnp.sum(power, axis=1, keepdims=True)
    dlog[...] = (prob - onehot[...].astype(jnp.float32)).astype(jnp.bfloat16)

    gout[...] = lax.dot_general(
        dlog[...], hid[...], (((0,), (0,)), ((), ())), preferred_element_type=jnp.float32
    )
    for n in range(hidden // 256):
        value = lax.dot_general(
            dlog[...],
            weight_out[256 * n : 256 * n + 256, :],
            (((1,), (1,)), ((), ())),
            preferred_element_type=jnp.float32,
        )
        for h in range(2):
            c = 2 * n + h
            part = value[:, LANES * h : LANES * h + LANES] * slope[c]
            for shift in range(3):
                mask = (after, None, before)[shift]
                dys[shift, c, guard : guard + rows, :] = part if mask is None else part * mask[...]

    def fold(value):
        return jnp.sum(value.reshape(-1, 8, LANES), axis=0)

    rows_out = class_rows(classes)
    biggest = jnp.zeros((8, LANES), jnp.float32)
    taps_square = jnp.zeros((1, LANES), jnp.float32)
    for c in range(chunks):
        column = slice(LANES * c, LANES * c + LANES)

        def backward(row, count, carry):
            sums, top = carry
            dy = dys[1, c, pl.ds(guard + row, count), :]
            total = None
            out = []
            for k in range(9):
                out.append(sums[k] + fold(dy * pre[k % 3, c, pl.ds(guard + row + starts[k], count), :]))
                term = (
                    dys[k % 3, c, pl.ds(guard + row - starts[k], count), :] * taps[k : k + 1, column]
                )
                total = term if total is None else total + term
            dpre_out[pl.ds(row, count), column] = total.astype(jnp.bfloat16)
            size = jnp.max(jnp.abs(total).reshape(-1, 8, LANES), axis=0)
            return tuple(out), jnp.maximum(top, size)

        zeros = tuple(jnp.zeros((8, LANES), jnp.float32) for _ in range(9))
        carry = lax.fori_loop(
            0,
            whole,
            lambda i, carry: backward(pl.multiple_of(i * STEP, STEP), STEP, carry),
            (zeros, biggest),
        )
        if left:
            carry = backward(whole * STEP, left, carry)
        sums, biggest = carry
        for k in range(9):
            value = jnp.sum(sums[k], axis=0, keepdims=True)
            taps_square = taps_square + value * value
            row = rows_out + chunks * k + c
            for pack in packs:
                pack[row : row + 1, :] = value
    top = jnp.full((1, LANES), jnp.max(biggest), jnp.float32)
    depth = hidden // dp
    row = rows_out + 9 * chunks
    for s in range(dp):
        packs[s][row : row + 1, :] = top
        if depth % LANES == 0:
            place = pl.multiple_of((me ^ s) * depth, depth)
            packs[s][:rows_out, :] = gout[:rows_out, pl.ds(place, depth)]
    if depth % LANES:
        for at in range(dp):

            @pl.when(me == at)
            def _(at=at):
                for s in range(dp):
                    place = (at ^ s) * depth
                    packs[s][:rows_out, :depth] = gout[:rows_out, place : place + depth]
    stats_out[...] = jnp.zeros(stats_out.shape, jnp.float32)
    stats_out[0:1, :] = taps_square
    square = jnp.sum(gout[...] * gout[...], axis=0, keepdims=True)
    for c in range(chunks):
        stats_out[1 + c : 2 + c, :] = square[:, LANES * c : LANES * c + LANES]
    save.wait()


def class_rows(classes):
    return (classes + 7) // 8 * 8


def pack_rows(classes, chunks):
    return class_rows(classes) + (9 * chunks + 8) // 8 * 8


def head_backward(dp, here, core, me, halves, onehot, weight_in, taps, weight_out, dil, masks):
    rows = onehot.shape[0]
    wide, hidden = weight_in.shape
    chunks = hidden // LANES
    guard = REACH * (PC + 1)
    scalars = jnp.stack([dil, here, core, me]).astype(jnp.int32)
    vmem = pl.BlockSpec(memory_space=pltpu.VMEM)
    anywhere = pl.BlockSpec(memory_space=pl.ANY)
    classes = weight_out.shape[1]
    weight_out = jnp.pad(weight_out, ((0, 0), (0, 256 - classes)))
    span = 2 * guard + rows
    pack = jax.ShapeDtypeStruct((pack_rows(classes, chunks), LANES), jnp.float32)
    return pl.pallas_call(
        functools.partial(head_kernel, dp, classes),
        out_shape=[
            jax.ShapeDtypeStruct((rows, wide), jnp.bfloat16),
            jax.ShapeDtypeStruct((rows, hidden), jnp.bfloat16),
            jax.ShapeDtypeStruct((8, LANES), jnp.float32),
        ]
        + [pack] * dp,
        in_specs=[pl.BlockSpec(memory_space=pltpu.SMEM)] + [anywhere] * 4 + [vmem] * 6,
        out_specs=[anywhere, vmem, vmem] + [vmem] * dp,
        scratch_shapes=[
            pltpu.VMEM((rows, wide), jnp.bfloat16),
            pltpu.VMEM((3, chunks, span, LANES), jnp.float32),
            pltpu.VMEM((3, chunks, span, LANES), jnp.float32),
            pltpu.VMEM((chunks, rows, LANES), jnp.float32),
            pltpu.VMEM((rows, hidden), jnp.bfloat16),
            pltpu.VMEM((rows, 256), jnp.bfloat16),
            pltpu.VMEM((256, hidden), jnp.float32),
            pltpu.SemaphoreType.DMA((2,)),
            pltpu.SemaphoreType.DMA,
        ],
        compiler_params=pltpu.CompilerParams(vmem_limit_bytes=48 * 1024 * 1024),
        name="head",
    )(scalars, *halves, weight_in, taps, weight_out, onehot, *masks)


def sum_kernel(classes, dp, *refs):
    parts, last, stats = refs[0], refs[1], refs[2]
    packs = refs[3 : 3 + dp]
    norms = refs[3 + dp : 3 + 2 * dp]
    share_in, share_out, taps_out, line, turned = refs[3 + 2 * dp :]
    depth = share_out.shape[0]
    chunks = taps_out.shape[1] // LANES
    rows_out = class_rows(classes)

    def fold(value):
        value = jnp.sum(value.reshape(-1, 8, value.shape[1]), axis=0)
        return sum(value[:, LANES * c : LANES * c + LANES] for c in range(value.shape[1] // LANES))

    total = parts[...] + last[...]
    share_in[...] = total
    line[0:8, :] = fold(total * total)
    summed = packs[0][...]
    for pack in packs[1:]:
        summed = summed + pack[...]
    turned[...] = jnp.zeros(turned.shape, jnp.float32)
    turned[:rows_out, :] = summed[:rows_out, :]
    flat = turned[...]
    if depth < LANES:
        keep = lax.broadcasted_iota(jnp.int32, flat.shape, 1) < depth
        flat = jnp.where(keep, flat, 0.0)
    line[8:16, :] = fold(flat * flat)
    share_out[...] = flat.T[:depth, :classes]
    square = jnp.zeros((1, LANES), jnp.float32)
    for k in range(9):
        for c in range(chunks):
            row = rows_out + chunks * k + c
            value = summed[row : row + 1, :]
            taps_out[k : k + 1, LANES * c : LANES * c + LANES] = value
            square = square + value * value
    line[16:24, :] = stats[...]
    line[24:32, :] = jnp.zeros((8, LANES), jnp.float32)
    line[24:25, :] = square
    line[25:26, :] = jnp.full((1, LANES), sum(norm[0] for norm in norms), jnp.float32)


def norm_kernel(dp, chunks, *refs):
    lines, out = refs[:dp], refs[dp]
    total = lines[0][...]
    for line in lines[1:]:
        total = total + line[...]
    values = [
        jnp.max(total[25:26, :]),
        jnp.sum(total[16:17, :]),
        jnp.sum(total[17 : 17 + chunks, :]),
        jnp.sum(total[0:8, :]),
        jnp.sum(lines[0][24:25, :]),
        jnp.sum(total[8:16, :]),
    ]
    row = lax.broadcasted_iota(jnp.int32, (8, LANES), 0)
    lane = lax.broadcasted_iota(jnp.int32, (8, LANES), 1)
    spread = jnp.zeros((8, LANES), jnp.float32)
    for i, value in enumerate(values):
        spread = jnp.where((row == i // 3) & (lane == i % 3), value, spread)
    out[...] = jnp.log(1e-12 + spread)[:2, :3]


def swap(value, step, size):
    return lax.ppermute(value, "dp", [(i, i ^ step) for i in range(size)])


def per_device(dp, trials, features, owner, dilation_index, labels, input_weight, taps, output_weight):
    here, core, halves = pieces(features[0, 0], "trial", trials, owner[0])
    me = lax.axis_index("dp")
    dil = dilation_index[0] + 1
    rows = features.shape[2]
    onehot = (labels[0][:, None] == jnp.arange(256, dtype=jnp.int32)[None, :]).astype(jnp.bfloat16)
    column = lax.broadcasted_iota(jnp.int32, (rows, LANES), 0) % PC
    before = (column < PC - dil).astype(jnp.float32)
    after = (column >= dil).astype(jnp.float32)
    xrows, dpre, stats, *packs = head_backward(
        dp, here, core, me, halves, onehot, input_weight[0], taps[0], output_weight[0], dil, (after, before)
    )
    classes = output_weight.shape[2]
    hidden = input_weight.shape[2]
    chunks = hidden // LANES
    depth = xrows.shape[1] // dp
    packs = packs[:1] + [swap(packs[s], s, dp) for s in range(1, dp)]
    room = 32768.0 / (X_LIMIT * rows)
    mark = class_rows(classes) + 9 * chunks

    def bound(pack):
        return jnp.maximum(pack[mark, 0], 1e-30)

    scale = room / bound(packs[0])
    norms = []
    got = []
    for step in list(range(1, dp)) + [0]:
        part = jnp.dot(
            lax.dynamic_slice_in_dim(xrows, (me ^ step) * depth, depth, 1).T,
            dpre,
            preferred_element_type=jnp.float32,
        )
        norms.append(jnp.sum(part * part).reshape(1))
        if step:
            got.append(swap((part * scale).astype(jnp.float16), step, dp))
    for step in range(1, dp - 1):
        part = part + got[step - 1].astype(jnp.float32) * (bound(packs[step]) * (1.0 / room))
        part = lax.optimization_barrier(part)
    last = got[-1].astype(jnp.float32) * (bound(packs[-1]) * (1.0 / room))
    vmem = pl.BlockSpec(memory_space=pltpu.VMEM)
    smem = pl.BlockSpec(memory_space=pltpu.SMEM)
    share_in, share_out, total_taps, line = pl.pallas_call(
        functools.partial(sum_kernel, classes, dp),
        out_shape=[
            jax.ShapeDtypeStruct((depth, hidden), jnp.float32),
            jax.ShapeDtypeStruct((hidden // dp, classes), jnp.float32),
            jax.ShapeDtypeStruct((9, hidden), jnp.float32),
            jax.ShapeDtypeStruct((32, LANES), jnp.float32),
        ],
        in_specs=[vmem] * (3 + dp) + [smem] * dp,
        out_specs=[vmem] * 4,
        scratch_shapes=[pltpu.VMEM((256, LANES), jnp.float32)],
        name="sums",
    )(part, last, stats, *packs, *norms)
    lines = [line] + [swap(line, s, dp) for s in range(1, dp)]
    norms = pl.pallas_call(
        functools.partial(norm_kernel, dp, chunks),
        out_shape=jax.ShapeDtypeStruct((2, 3), jnp.float32),
        in_specs=[vmem] * dp,
        out_specs=vmem,
        name="norms",
    )(*lines)
    return (share_in[None], total_taps[None], share_out[None], norms[None])


def solution(mesh):
    dp, trials = mesh.shape["dp"], mesh.shape["trial"]
    placed = (
        P(("groups", "dp"), "trial", None, None),
        P(("groups", "dp")),
        P("trial"),
        P(("groups", "dp"), None),
        P("trial", None, None),
        P("trial", None, None),
        P("trial", None, None),
    )

    def step(*args):
        return per_device(dp, trials, *args)

    return jax.shard_map(
        step,
        mesh=mesh,
        in_specs=placed,
        out_specs=(
            P(("groups", "trial"), "dp", None),
            P(("groups", "trial"), None, None),
            P(("groups", "trial"), "dp", None),
            P(("groups", "trial"), None, None),
        ),
        check_vma=False,
    )
```

```python
import functools
import math

import jax
import jax.numpy as jnp
from jax import lax
from jax.experimental import pallas as pl
from jax.experimental.pallas import tpu as pltpu
from jax.sharding import PartitionSpec as P

PC = 37
LANES = 128
STEP = 32
REACH = 4
OFFSETS = [(a, b) for a in (-1, 0, 1) for b in (-1, 0, 1)]
X_LIMIT = 6.0
ROOM = 16384.0


def pieces(block, axis, size, source):
    if size != 4:
        block = jnp.where(lax.axis_index(axis) == source, block, jnp.zeros_like(block))
        block = lax.psum(block, axis)
        width = block.shape[1] // 2
        low, high = block[:, :width], block[:, width:]
        zero = jnp.int32(0)
        return zero + 1, zero, (low, low, high, high)
    me = lax.axis_index(axis)
    core = me % 2
    mate = [(0, 1), (1, 0), (2, 3), (3, 2)]
    across = [(0, 2), (2, 0), (1, 3), (3, 1)]
    width = block.shape[1] // 2
    low, high = block[:, :width], block[:, width:]
    got = lax.ppermute(jnp.where(core == 0, high, low), axis, mate)
    kept = jnp.where(core == 0, low, high)
    held = jnp.where(source % 2 == core, kept, got)
    other = lax.ppermute(held, axis, across)
    here = ((source // 2) == (me // 2)).astype(jnp.int32)
    back_held = lax.ppermute(held, axis, mate)
    back_other = lax.ppermute(other, axis, mate)
    return here, core, (held, other, back_held, back_other)


def gelu_parts(value):
    inner = 0.7978845608 * (value + 0.044715 * value * value * value)
    tanh_val = jnp.tanh(inner)
    out_val = 0.5 * value * (1.0 + tanh_val)
    slope = 0.5 * (1.0 + tanh_val) + 0.5 * value * (1.0 - tanh_val * tanh_val) * 0.7978845608 * (
        1.0 + 3.0 * 0.044715 * value * value
    )
    return (out_val, slope)


def exponent(size):
    size = jnp.maximum(jnp.full((1, LANES), size, jnp.float32), 1e-30)
    return jnp.clip(jnp.floor(jnp.log(ROOM / size) * (1.0 / math.log(2.0))), -100.0, 100.0)


def head_kernel(
    sizes,
    scalars,
    held,
    other,
    back_held,
    back_other,
    weight_in,
    taps,
    weight_out,
    onehot,
    after,
    before,
    x_out,
    dpre_out,
    gout,
    small,
    first,
    x_vmem,
    pre,
    dys,
    slope,
    hid,
    dlog,
    sem_in,
    sem_out,
):
    rows = x_vmem.shape[0]
    width = x_vmem.shape[1] // 2
    hidden = weight_in.shape[1]
    chunks = hidden // LANES
    guard = REACH * (PC + 1)
    dil, here, core = scalars[0], scalars[1], scalars[2]

    def fetch(source, place, index):
        column = pl.multiple_of(place * width, LANES)
        return pltpu.make_async_copy(source, x_vmem.at[:, pl.ds(column, width)], sem_in.at[index])

    @pl.when(here == 1)
    def _():
        fetch(held, core, 0).start()
        fetch(back_held, 1 - core, 1).start()

    @pl.when(here == 0)
    def _():
        fetch(other, core, 0).start()
        fetch(back_other, 1 - core, 1).start()

    for shift in range(3):
        for c in range(chunks):
            for ref in (pre, dys):
                ref[shift, c, :guard, :] = jnp.zeros((guard, LANES), jnp.float32)
                tail = ref.shape[2] - guard - rows
                ref[shift, c, guard + rows :, :] = jnp.zeros((tail, LANES), jnp.float32)
    fetch(held, core, 0).wait()
    fetch(back_held, 1 - core, 1).wait()
    save = pltpu.make_async_copy(x_vmem, x_out, sem_out)
    save.start()

    masks = (after, None, before)
    for n in range(hidden // 256):
        value = jnp.dot(
            x_vmem[...], weight_in[:, 256 * n : 256 * n + 256], preferred_element_type=jnp.float32
        )
        for h in range(2):
            part = value[:, LANES * h : LANES * h + LANES]
            for shift in range(3):
                mask = (before, None, after)[shift]
                pre[shift, 2 * n + h, guard : guard + rows, :] = (
                    part if mask is None else part * mask[...]
                )

    starts = [dil * (PC * a + b) for a, b in OFFSETS]

    def forward(row, count):
        for c in range(chunks):
            total = None
            for k in range(9):
                term = (
                    pre[k % 3, c, pl.ds(guard + row + starts[k], count), :]
                    * taps[k, :, LANES * c : LANES * c + LANES]
                )
                total = term if total is None else total + term
            act, grad = gelu_parts(total)
            slope[c, pl.ds(row, count), :] = grad
            hid[pl.ds(row, count), LANES * c : LANES * c + LANES] = act.astype(jnp.bfloat16)

    whole = rows // STEP
    left = rows - whole * STEP

    @pl.loop(0, whole)
    def _(i):
        forward(pl.multiple_of(i * STEP, STEP), STEP)

    if left:
        forward(whole * STEP, left)

    logits = lax.dot_general(
        hid[...], weight_out[...], (((1,), (1,)), ((), ())), preferred_element_type=jnp.float32
    )
    lane = lax.broadcasted_iota(jnp.int32, logits.shape, 1)
    logits = jnp.where(lane < sizes.classes, logits, -1e30)
    peak = jnp.max(logits, axis=1, keepdims=True)
    power = jnp.exp(logits - peak)
    prob = power / jnp.sum(power, axis=1, keepdims=True)
    dlog[...] = (prob - onehot[...].astype(jnp.float32)).astype(jnp.bfloat16)

    gout[...] = lax.dot_general(
        dlog[...], hid[...], (((0,), (0,)), ((), ())), preferred_element_type=jnp.float32
    )
    for n in range(hidden // 256):
        value = jnp.dot(
            dlog[...], weight_out[:, 256 * n : 256 * n + 256], preferred_element_type=jnp.float32
        )
        for h in range(2):
            c = 2 * n + h
            part = value[:, LANES * h : LANES * h + LANES] * slope[c]
            for shift in range(3):
                mask = (after, None, before)[shift]
                dys[shift, c, guard : guard + rows, :] = part if mask is None else part * mask[...]

    def fold(value):
        return jnp.sum(value.reshape(-1, 8, LANES), axis=0)

    biggest = jnp.zeros((8, LANES), jnp.float32)
    taps_biggest = jnp.zeros((1, LANES), jnp.float32)
    small[...] = jnp.zeros(small.shape, jnp.float32)
    taps_square = jnp.zeros((1, LANES), jnp.float32)
    for c in range(chunks):
        column = slice(LANES * c, LANES * c + LANES)

        def backward(row, count, carry):
            sums, top = carry
            dy = dys[1, c, pl.ds(guard + row, count), :]
            total = None
            out = []
            for k in range(9):
                out.append(sums[k] + fold(dy * pre[k % 3, c, pl.ds(guard + row + starts[k], count), :]))
                term = (
                    dys[k % 3, c, pl.ds(guard + row - starts[k], count), :] * taps[k, :, column]
                )
                total = term if total is None else total + term
            dpre_out[pl.ds(row, count), column] = total.astype(jnp.bfloat16)
            size = jnp.max(jnp.abs(total).reshape(-1, 8, LANES), axis=0)
            return tuple(out), jnp.maximum(top, size)

        zeros = tuple(jnp.zeros((8, LANES), jnp.float32) for _ in range(9))
        carry = lax.fori_loop(
            0,
            whole,
            lambda i, carry: backward(pl.multiple_of(i * STEP, STEP), STEP, carry),
            (zeros, biggest),
        )
        if left:
            carry = backward(whole * STEP, left, carry)
        sums, biggest = carry
        for k in range(9):
            value = jnp.sum(sums[k], axis=0, keepdims=True)
            taps_square = taps_square + value * value
            taps_biggest = jnp.maximum(taps_biggest, jnp.abs(value))
            small[k : k + 1, column] = value
    powers = (
        exponent(jnp.max(biggest) * (X_LIMIT * rows)),
        exponent(jnp.max(jnp.abs(gout[...]))),
        exponent(jnp.max(taps_biggest)),
    )
    for c in range(chunks):
        for i, power in enumerate(powers):
            small[9 + i : 10 + i, LANES * c : LANES * c + LANES] = power
    small[16:17, :LANES] = taps_square
    small[17:18, :] = jnp.sum(gout[...] * gout[...], axis=0, keepdims=True)
    if first.shape[0] == sizes.message:
        norm = message(sizes, scalars[3], x_vmem, dpre_out, gout, small, first, True)
        small[18:19, :LANES] = norm
    save.wait()


def message(sizes, place, x, dpre, gout, small, out, scaled):
    depth, depth_out = sizes.depth, sizes.depth_out
    column = pl.multiple_of(place * depth, LANES)
    block = lax.dot_general(
        x[:, pl.ds(column, depth)], dpre[...], (((0,), (0,)), ((), ())), preferred_element_type=jnp.float32
    )
    hidden = block.shape[1]
    chunks = hidden // LANES
    norm = jnp.sum(block * block, axis=0, keepdims=True)
    norm = sum(norm[:, LANES * c : LANES * c + LANES] for c in range(chunks))
    factors = [jnp.exp2(small[9 + i : 10 + i, :]) if scaled else 1.0 for i in range(3)]
    out[:depth, :] = block * factors[0]
    out[depth:, :] = jnp.zeros((out.shape[0] - depth, hidden), jnp.float32)
    column = pl.multiple_of(place * depth_out, LANES)
    for start, group in sizes.groups:
        value = gout[start : start + group, pl.ds(column, depth_out)]
        lane = start // sizes.group * LANES
        factor = factors[1][:, :LANES] if scaled else 1.0
        out[depth : depth + group, lane : lane + LANES] = value * factor
    row = depth + sizes.group
    out[row : row + 9, :] = small[0:9, :] * factors[2]
    if scaled:
        out[row + 9 : row + 12, :] = small[9:12, :]
    return norm


class Sizes:
    def __init__(self, wide, hidden, classes, dp):
        self.classes = classes
        self.depth = wide // dp
        self.depth_out = hidden // dp
        self.chunks = hidden // LANES
        self.class_rows = (classes + 7) // 8 * 8
        self.group = (self.class_rows // self.chunks + 7) // 8 * 8
        self.groups = [
            (at, min(self.group, self.class_rows - at)) for at in range(0, self.class_rows, self.group)
        ]
        self.message = self.depth + self.group + 16
        self.staged = dp == 4 and self.depth % LANES == 0 and self.depth_out == LANES


def head_backward(sizes, scalars, halves, onehot, weight_in, taps, weight_out, masks):
    rows = onehot.shape[0]
    wide, hidden = weight_in.shape
    chunks = hidden // LANES
    vmem = pl.BlockSpec(memory_space=pltpu.VMEM)
    anywhere = pl.BlockSpec(memory_space=pl.ANY)
    span = 2 * REACH * (PC + 1) + rows
    return pl.pallas_call(
        functools.partial(head_kernel, sizes),
        out_shape=[
            jax.ShapeDtypeStruct((rows, wide), jnp.bfloat16),
            jax.ShapeDtypeStruct((rows, hidden), jnp.bfloat16),
            jax.ShapeDtypeStruct((256, hidden), jnp.float32),
            jax.ShapeDtypeStruct((24, hidden), jnp.float32),
            jax.ShapeDtypeStruct((sizes.message if sizes.staged else 8, hidden), jnp.float32),
        ],
        in_specs=[pl.BlockSpec(memory_space=pltpu.SMEM)] + [anywhere] * 4 + [vmem] * 6,
        out_specs=[anywhere] + [vmem] * 4,
        scratch_shapes=[
            pltpu.VMEM((rows, wide), jnp.bfloat16),
            pltpu.VMEM((3, chunks, span, LANES), jnp.float32),
            pltpu.VMEM((3, chunks, span, LANES), jnp.float32),
            pltpu.VMEM((chunks, rows, LANES), jnp.float32),
            pltpu.VMEM((rows, hidden), jnp.bfloat16),
            pltpu.VMEM((rows, 256), jnp.bfloat16),
            pltpu.SemaphoreType.DMA((2,)),
            pltpu.SemaphoreType.DMA,
        ],
        compiler_params=pltpu.CompilerParams(vmem_limit_bytes=40 * 1024 * 1024),
        name="head",
    )(scalars, *halves, weight_in, taps, weight_out, onehot, *masks)


def blocks_kernel(sizes, scalars, x, dpre, gout, small, second, third, own, stats):
    norm = message(sizes, scalars[4], x, dpre, gout, small, second, True)
    norm = norm + message(sizes, scalars[5], x, dpre, gout, small, third, True)
    norm = norm + message(sizes, scalars[6], x, dpre, gout, small, own, False)
    stats[...] = jnp.zeros(stats.shape, jnp.float32)
    stats[0:1, :] = norm + small[18:19, :LANES]
    stats[1:2, :] = small[16:17, :LANES]
    for c in range(sizes.chunks):
        stats[2 + c : 3 + c, :] = small[17:18, LANES * c : LANES * c + LANES]


def sum_kernel(sizes, parts, last, stats, share_in, share_out, taps_out, line):
    depth, chunks = sizes.depth, sizes.chunks

    def fold(value):
        value = jnp.sum(value.reshape(-1, 8, value.shape[1]), axis=0)
        return sum(value[:, LANES * c : LANES * c + LANES] for c in range(value.shape[1] // LANES))

    mark = depth + sizes.group
    factors = [jnp.exp2(-last[mark + 9 + i : mark + 10 + i, :]) for i in range(3)]
    total = parts[:depth, :] + last[:depth, :] * factors[0]
    share_in[...] = total
    line[0:8, :] = fold(total * total)
    total = parts[depth:mark, :] + last[depth:mark, :] * factors[1]
    line[8:16, :] = fold(total * total)
    for start, group in sizes.groups:
        lane = start // sizes.group * LANES
        count = min(group, sizes.classes - start)
        share_out[start : start + count, 0, :] = total[:count, lane : lane + LANES]
    total = parts[mark : mark + 9, :] + last[mark : mark + 9, :] * factors[2]
    square = jnp.sum(total * total, axis=0, keepdims=True)
    for k in range(9):
        taps_out[k, :, :] = total[k : k + 1, :]
    line[16:24, :] = stats[...]
    line[24:32, :] = jnp.zeros((8, LANES), jnp.float32)
    line[24:25, :] = sum(square[:, LANES * c : LANES * c + LANES] for c in range(chunks))


def norm_kernel(dp, chunks, *refs):
    lines, out = refs[:dp], refs[dp]
    total = lines[0][...]
    for line in lines[1:]:
        total = total + line[...]
    values = [
        jnp.sum(total[16:17, :]),
        jnp.sum(total[17:18, :]),
        jnp.sum(total[18 : 18 + chunks, :]),
        jnp.sum(total[0:8, :]),
        jnp.sum(lines[0][24:25, :]),
        jnp.sum(total[8:16, :]),
    ]
    row = lax.broadcasted_iota(jnp.int32, (8, LANES), 0)
    lane = lax.broadcasted_iota(jnp.int32, (8, LANES), 1)
    spread = jnp.zeros((8, LANES), jnp.float32)
    for i, value in enumerate(values):
        spread = jnp.where((row == i // 3) & (lane == i % 3), value, spread)
    out[...] = jnp.log(1e-12 + spread)[:2, :3]


def permute(value, pairs):
    return lax.ppermute(value, "dp", pairs)


def by_row(sizes, shape, three):
    row = lax.broadcasted_iota(jnp.int32, shape, 0)
    return jnp.where(
        row < sizes.depth, three[0], jnp.where(row < sizes.depth + sizes.group, three[1], three[2])
    )


def staged_sums(sizes, me, scalars, xrows, dpre, gout, small, first):
    vmem = pl.BlockSpec(memory_space=pltpu.VMEM)
    smem = pl.BlockSpec(memory_space=pltpu.SMEM)
    hidden = dpre.shape[1]
    shape = (sizes.message, hidden)
    full = jax.ShapeDtypeStruct(shape, jnp.float32)
    lines = jax.ShapeDtypeStruct((8, LANES), jnp.float32)
    half = jnp.float16
    near = permute(first.astype(half), [(0, 1), (1, 0), (2, 3), (3, 2)])
    second, third, own, stats = pl.pallas_call(
        functools.partial(blocks_kernel, sizes),
        out_shape=[full, full, full, lines],
        in_specs=[smem] + [vmem] * 4,
        out_specs=[vmem] * 4,
        compiler_params=pltpu.CompilerParams(vmem_limit_bytes=16 * 1024 * 1024),
        name="blocks",
    )(scalars, xrows, dpre, gout, small)
    second = second.astype(half)
    middle = permute(second, [(1, 2), (2, 1)])
    end = (me == 0) | (me == 3)
    mark = sizes.depth + sizes.group + 9
    row = lax.broadcasted_iota(jnp.int32, shape, 0)

    def split(value):
        return [value[mark + i : mark + i + 1] for i in range(3)]

    mine, theirs = split(third), split(near.astype(jnp.float32))
    theirs = [jnp.where(end, a, b) for a, b in zip(mine, theirs)]
    common = [jnp.minimum(a, b) for a, b in zip(mine, theirs)]
    both = third * by_row(sizes, shape, [jnp.exp2(c - a) for a, c in zip(mine, common)])
    both = both + jnp.where(end, 0.0, near.astype(jnp.float32)) * by_row(
        sizes, shape, [jnp.exp2(c - b) for b, c in zip(theirs, common)]
    )
    for i in range(3):
        both = jnp.where(row == mark + i, common[i], both)
    far = permute(both.astype(half), [(0, 2), (2, 0), (1, 3), (3, 1)])
    edge = permute(second, [(0, 1), (3, 2)])

    def decode(value):
        value = value.astype(jnp.float32)
        return value * by_row(sizes, shape, [jnp.exp2(-v) for v in split(value)])

    parts = own + decode(jnp.where(end, near, middle)) + decode(edge)
    return parts, far.astype(jnp.float32), stats


def per_device(sizes, dp, trials, features, owner, dilation_index, labels, input_weight, taps, output_weight):
    here, core, halves = pieces(features[0, 0], "trial", trials, owner[0])
    me = lax.axis_index("dp")
    dil = dilation_index[0] + 1
    rows = features.shape[2]
    onehot = (labels[0][:, None] == jnp.arange(256, dtype=jnp.int32)[None, :]).astype(jnp.bfloat16)
    column = lax.broadcasted_iota(jnp.int32, (rows, LANES), 0) % PC
    before = (column < PC - dil).astype(jnp.float32)
    after = (column >= dil).astype(jnp.float32)
    classes, chunks = sizes.classes, sizes.chunks
    weight_out = jnp.pad(output_weight[0].T, ((0, 256 - classes), (0, 0)))
    high = me >= 2
    odd = me % 2
    to = [3 * (1 - odd), jnp.where(odd == 0, 1, 2), jnp.where(high, me - 2, me + 2), me]
    scalars = jnp.stack([dil, here, core] + to).astype(jnp.int32)
    xrows, dpre, gout, small, first = head_backward(
        sizes,
        scalars,
        halves,
        onehot,
        input_weight[0],
        taps[0][:, None, :],
        weight_out,
        (after, before),
    )
    if not sizes.staged:
        return general_sums(sizes, xrows, dpre, gout, small)
    parts, last, stats = staged_sums(sizes, me, scalars, xrows, dpre, gout, small, first)
    vmem = pl.BlockSpec(memory_space=pltpu.VMEM)
    hidden = dpre.shape[1]
    share_in, share_out, total_taps, line = pl.pallas_call(
        functools.partial(sum_kernel, sizes),
        out_shape=[
            jax.ShapeDtypeStruct((sizes.depth, hidden), jnp.float32),
            jax.ShapeDtypeStruct((classes, 1, sizes.depth_out), jnp.float32),
            jax.ShapeDtypeStruct((9, 1, hidden), jnp.float32),
            jax.ShapeDtypeStruct((32, LANES), jnp.float32),
        ],
        in_specs=[vmem] * 3,
        out_specs=[vmem] * 4,
        compiler_params=pltpu.CompilerParams(vmem_limit_bytes=8 * 1024 * 1024),
        name="sums",
    )(parts, last, stats)
    lines = [line] + [permute(line, [(i, i ^ s) for i in range(dp)]) for s in range(1, dp)]
    norms = pl.pallas_call(
        functools.partial(norm_kernel, dp, chunks),
        out_shape=jax.ShapeDtypeStruct((2, 3), jnp.float32),
        in_specs=[vmem] * dp,
        out_specs=vmem,
        compiler_params=pltpu.CompilerParams(vmem_limit_bytes=4 * 1024 * 1024),
        name="norms",
    )(*lines)
    share_out = jnp.transpose(share_out, (1, 2, 0))
    return (share_in[None], jnp.transpose(total_taps, (1, 0, 2)), share_out, norms[None])


def general_sums(sizes, xrows, dpre, gout, small):
    g_in = jnp.dot(xrows.T, dpre, preferred_element_type=jnp.float32)
    g_out = gout[: sizes.classes].T
    g_taps = small[:9]
    share_in = lax.psum_scatter(g_in, "dp", scatter_dimension=0, tiled=True)
    share_out = lax.psum_scatter(g_out, "dp", scatter_dimension=0, tiled=True)
    local = jnp.stack([jnp.sum(g_in * g_in), jnp.sum(g_taps * g_taps), jnp.sum(g_out * g_out)])
    share_sq = jnp.stack([jnp.sum(share_in * share_in), jnp.sum(share_out * share_out)])
    total_taps, squares, share_total = lax.psum((g_taps, local, share_sq), "dp")
    totals = jnp.stack([share_total[0], jnp.sum(total_taps * total_taps), share_total[1]])
    norms = jnp.log(1e-12 + jnp.stack([squares, totals]))
    return (share_in[None], total_taps[None], share_out[None], norms[None])


def solution(mesh):
    dp, trials = mesh.shape["dp"], mesh.shape["trial"]
    placed = (
        P(("groups", "dp"), "trial", None, None),
        P(("groups", "dp")),
        P("trial"),
        P(("groups", "dp"), None),
        P("trial", None, None),
        P("trial", None, None),
        P("trial", None, None),
    )

    def step(*args):
        (wide, hidden), classes = args[4].shape[1:], args[6].shape[2]
        return per_device(Sizes(wide, hidden, classes, dp), dp, trials, *args)

    return jax.shard_map(
        step,
        mesh=mesh,
        in_specs=placed,
        out_specs=(
            P(("groups", "trial"), "dp", None),
            P(("groups", "trial"), None, None),
            P(("groups", "trial"), "dp", None),
            P(("groups", "trial"), None, None),
        ),
        check_vma=False,
    )
```

```python
import functools
import math

import jax
import jax.numpy as jnp
from jax import lax
from jax.experimental import pallas as pl
from jax.experimental.pallas import tpu as pltpu
from jax.sharding import PartitionSpec as P

PC = 37
LANES = 128
STEP = 32
REACH = 4
OFFSETS = [(a, b) for a in (-1, 0, 1) for b in (-1, 0, 1)]
X_LIMIT = 6.0
ROOM = 16384.0


def pieces(block, axis, size, source):
    width = block.shape[1] // 2
    if size != 4:
        block = jnp.where(lax.axis_index(axis) == source, block, jnp.zeros_like(block))
        block = lax.psum(block, axis)
        low, high = block[:, :width], block[:, width:]
        zero = jnp.int32(0)
        return zero + 1, zero, (width,), (low, low, high, high)
    me = lax.axis_index(axis)
    core = me % 2
    mate = [(0, 1), (1, 0), (2, 3), (3, 2)]
    across = [(0, 2), (2, 0), (1, 3), (3, 1)]
    here = ((source // 2) == (me // 2)).astype(jnp.int32)
    widths = split_width(width)
    rows = block.shape[0]
    switches = jnp.stack([core, (source % 2 == core).astype(jnp.int32)]).astype(jnp.int32)
    smem = pl.BlockSpec(memory_space=pltpu.SMEM)
    vmem = pl.BlockSpec(memory_space=pltpu.VMEM)
    anywhere = pl.BlockSpec(memory_space=pl.ANY)
    hbm = pl.BlockSpec(memory_space=pltpu.MemorySpace.HBM)
    sent = pl.pallas_call(
        give_kernel,
        out_shape=jax.ShapeDtypeStruct((rows, width), block.dtype),
        in_specs=[smem, hbm],
        out_specs=vmem,
        scratch_shapes=[pltpu.SemaphoreType.DMA],
        compiler_params=pltpu.CompilerParams(vmem_limit_bytes=4 * 1024 * 1024),
        name="give",
    )(switches, block)
    got = lax.ppermute(sent, axis, mate)
    held = pl.pallas_call(
        functools.partial(hold_kernel, widths),
        out_shape=[jax.ShapeDtypeStruct((rows, piece), block.dtype) for piece in widths],
        in_specs=[smem, hbm, anywhere],
        out_specs=[vmem] * len(widths),
        scratch_shapes=[pltpu.SemaphoreType.DMA((len(widths),))],
        compiler_params=pltpu.CompilerParams(vmem_limit_bytes=4 * 1024 * 1024),
        name="hold",
    )(switches, block, got)
    values = []
    for piece in held:
        other = lax.ppermute(piece, axis, across)
        back_held = lax.ppermute(piece, axis, mate)
        back_other = lax.ppermute(other, axis, mate)
        values += [piece, other, back_held, back_other]
    return here, core, widths, tuple(values)


def give_kernel(switches, block, out, sem):
    width = out.shape[1]
    column = pl.multiple_of((1 - switches[0]) * width, LANES)
    copy = pltpu.make_async_copy(block.at[:, pl.ds(column, width)], out, sem)
    copy.start()
    copy.wait()


def hold_kernel(widths, switches, block, got, *rest):
    outs, sem = rest[:-1], rest[-1]
    width = got.shape[1]
    column = switches[0] * width
    starts = [sum(widths[:i]) for i in range(len(widths))]

    def copy(i, own):
        if own:
            source = block.at[:, pl.ds(pl.multiple_of(column + starts[i], LANES), widths[i])]
        else:
            source = got.at[:, pl.ds(starts[i], widths[i])]
        return pltpu.make_async_copy(source, outs[i], sem.at[i])

    @pl.when(switches[1] == 1)
    def _():
        for i in range(len(widths)):
            copy(i, True).start()

    @pl.when(switches[1] == 0)
    def _():
        for i in range(len(widths)):
            copy(i, False).start()

    for i in range(len(widths)):
        copy(i, False).wait()


def split_width(width):
    tiles = width // LANES
    last = max(tiles // 3, 1)
    return tuple(LANES * n for n in (tiles - last, last) if n > 0)


def gelu_parts(value):
    inner = 0.7978845608 * (value + 0.044715 * value * value * value)
    tanh_val = jnp.tanh(inner)
    out_val = 0.5 * value * (1.0 + tanh_val)
    slope = 0.5 * (1.0 + tanh_val) + 0.5 * value * (1.0 - tanh_val * tanh_val) * 0.7978845608 * (
        1.0 + 3.0 * 0.044715 * value * value
    )
    return (out_val, slope)


def exponent(size):
    size = jnp.maximum(jnp.full((1, LANES), size, jnp.float32), 1e-30)
    return jnp.clip(jnp.floor(jnp.log(ROOM / size) * (1.0 / math.log(2.0))), -100.0, 100.0)


def head_kernel(
    sizes,
    widths,
    scalars,
    *refs,
):
    halves, refs = refs[: 4 * len(widths)], refs[4 * len(widths) :]
    weight_in, taps, weight_out, onehot, after, before = refs[:6]
    x_out, dpre_out, gout, small, first, early = refs[6:12]
    x_vmem, pre, dys, slope, hid, dlog, sem_in, sem_out = refs[12:]
    rows = x_vmem.shape[0]
    width = x_vmem.shape[1] // 2
    hidden = weight_in.shape[1]
    chunks = hidden // LANES
    guard = REACH * (PC + 1)
    dil, here, core = scalars[0], scalars[1], scalars[2]

    def fetch(kind, index):
        place = core if kind < 2 else 1 - core
        column = pl.multiple_of(place * width + sum(widths[:index]), LANES)
        target = x_vmem.at[:, pl.ds(column, widths[index])]
        return pltpu.make_async_copy(halves[4 * index + kind], target, sem_in.at[index, kind // 2])

    @pl.when(here == 1)
    def _():
        for index in range(len(widths)):
            fetch(0, index).start()
            fetch(2, index).start()

    @pl.when(here == 0)
    def _():
        for index in range(len(widths)):
            fetch(1, index).start()
            fetch(3, index).start()

    for shift in range(3):
        for c in range(chunks):
            for ref in (pre, dys):
                ref[shift, c, :guard, :] = jnp.zeros((guard, LANES), jnp.float32)
                tail = ref.shape[2] - guard - rows
                ref[shift, c, guard + rows :, :] = jnp.zeros((tail, LANES), jnp.float32)
    for index in range(len(widths)):
        fetch(0, index).wait()
        fetch(2, index).wait()
    save = pltpu.make_async_copy(x_vmem, x_out, sem_out)
    save.start()

    masks = (after, None, before)
    for n in range(hidden // 256):
        value = jnp.dot(
            x_vmem[...], weight_in[:, 256 * n : 256 * n + 256], preferred_element_type=jnp.float32
        )
        for h in range(2):
            part = value[:, LANES * h : LANES * h + LANES]
            for shift in range(3):
                mask = (before, None, after)[shift]
                pre[shift, 2 * n + h, guard : guard + rows, :] = (
                    part if mask is None else part * mask[...]
                )

    starts = [dil * (PC * a + b) for a, b in OFFSETS]

    def forward(row, count):
        for c in range(chunks):
            total = None
            for k in range(9):
                term = (
                    pre[k % 3, c, pl.ds(guard + row + starts[k], count), :]
                    * taps[k, :, LANES * c : LANES * c + LANES]
                )
                total = term if total is None else total + term
            act, grad = gelu_parts(total)
            slope[c, pl.ds(row, count), :] = grad
            hid[pl.ds(row, count), LANES * c : LANES * c + LANES] = act.astype(jnp.bfloat16)

    whole = rows // STEP
    left = rows - whole * STEP

    @pl.loop(0, whole)
    def _(i):
        forward(pl.multiple_of(i * STEP, STEP), STEP)

    if left:
        forward(whole * STEP, left)

    logits = lax.dot_general(
        hid[...], weight_out[...], (((1,), (1,)), ((), ())), preferred_element_type=jnp.float32
    )
    lane = lax.broadcasted_iota(jnp.int32, logits.shape, 1)
    logits = jnp.where(lane < sizes.classes, logits, -1e30)
    peak = jnp.max(logits, axis=1, keepdims=True)
    power = jnp.exp(logits - peak)
    prob = power / jnp.sum(power, axis=1, keepdims=True)
    dlog[...] = (prob - onehot[...].astype(jnp.float32)).astype(jnp.bfloat16)

    gout[...] = lax.dot_general(
        dlog[...], hid[...], (((0,), (0,)), ((), ())), preferred_element_type=jnp.float32
    )
    for n in range(hidden // 256):
        value = jnp.dot(
            dlog[...], weight_out[:, 256 * n : 256 * n + 256], preferred_element_type=jnp.float32
        )
        for h in range(2):
            c = 2 * n + h
            part = value[:, LANES * h : LANES * h + LANES] * slope[c]
            for shift in range(3):
                mask = (after, None, before)[shift]
                dys[shift, c, guard : guard + rows, :] = part if mask is None else part * mask[...]

    def fold(value):
        return jnp.sum(value.reshape(-1, 8, LANES), axis=0)

    biggest = jnp.zeros((8, LANES), jnp.float32)
    taps_biggest = jnp.zeros((1, LANES), jnp.float32)
    small[...] = jnp.zeros(small.shape, jnp.float32)
    taps_square = jnp.zeros((1, LANES), jnp.float32)
    for c in range(chunks):
        column = slice(LANES * c, LANES * c + LANES)

        def backward(row, count, carry):
            sums, top = carry
            dy = dys[1, c, pl.ds(guard + row, count), :]
            total = None
            out = []
            for k in range(9):
                out.append(sums[k] + fold(dy * pre[k % 3, c, pl.ds(guard + row + starts[k], count), :]))
                term = (
                    dys[k % 3, c, pl.ds(guard + row - starts[k], count), :] * taps[k, :, column]
                )
                total = term if total is None else total + term
            dpre_out[pl.ds(row, count), column] = total.astype(jnp.bfloat16)
            size = jnp.max(jnp.abs(total).reshape(-1, 8, LANES), axis=0)
            return tuple(out), jnp.maximum(top, size)

        zeros = tuple(jnp.zeros((8, LANES), jnp.float32) for _ in range(9))
        carry = lax.fori_loop(
            0,
            whole,
            lambda i, carry: backward(pl.multiple_of(i * STEP, STEP), STEP, carry),
            (zeros, biggest),
        )
        if left:
            carry = backward(whole * STEP, left, carry)
        sums, biggest = carry
        for k in range(9):
            value = jnp.sum(sums[k], axis=0, keepdims=True)
            taps_square = taps_square + value * value
            taps_biggest = jnp.maximum(taps_biggest, jnp.abs(value))
            small[k : k + 1, column] = value
    powers = (
        exponent(jnp.max(biggest) * (X_LIMIT * rows)),
        exponent(jnp.max(jnp.abs(gout[...]))),
        exponent(jnp.max(taps_biggest)),
    )
    for c in range(chunks):
        for i, power in enumerate(powers):
            small[9 + i : 10 + i, LANES * c : LANES * c + LANES] = power
    small[16:17, :LANES] = taps_square
    small[17:18, :] = jnp.sum(gout[...] * gout[...], axis=0, keepdims=True)
    if first.shape[0] == sizes.message:
        norm = message(sizes, scalars[3], x_vmem, dpre_out, gout, small, first, True)
        norm = norm + message(sizes, scalars[4], x_vmem, dpre_out, gout, small, early, True)
        small[18:19, :LANES] = norm
    save.wait()


def message(sizes, place, x, dpre, gout, small, out, scaled):
    depth, depth_out = sizes.depth, sizes.depth_out
    column = pl.multiple_of(place * depth, LANES)
    block = lax.dot_general(
        x[:, pl.ds(column, depth)], dpre[...], (((0,), (0,)), ((), ())), preferred_element_type=jnp.float32
    )
    hidden = block.shape[1]
    chunks = hidden // LANES
    norm = jnp.sum(block * block, axis=0, keepdims=True)
    norm = sum(norm[:, LANES * c : LANES * c + LANES] for c in range(chunks))
    factors = [jnp.exp2(small[9 + i : 10 + i, :]) if scaled else 1.0 for i in range(3)]
    out[:depth, :] = block * factors[0]
    out[depth:, :] = jnp.zeros((out.shape[0] - depth, hidden), jnp.float32)
    column = pl.multiple_of(place * depth_out, LANES)
    for start, group in sizes.groups:
        value = gout[start : start + group, pl.ds(column, depth_out)]
        lane = start // sizes.group * LANES
        factor = factors[1][:, :LANES] if scaled else 1.0
        out[depth : depth + group, lane : lane + LANES] = value * factor
    row = depth + sizes.group
    out[row : row + 9, :] = small[0:9, :] * factors[2]
    if scaled:
        out[row + 9 : row + 12, :] = small[9:12, :]
    return norm


class Sizes:
    def __init__(self, wide, hidden, classes, dp):
        self.classes = classes
        self.depth = wide // dp
        self.depth_out = hidden // dp
        self.chunks = hidden // LANES
        self.class_rows = (classes + 7) // 8 * 8
        self.group = (self.class_rows // self.chunks + 7) // 8 * 8
        self.groups = [
            (at, min(self.group, self.class_rows - at)) for at in range(0, self.class_rows, self.group)
        ]
        self.message = self.depth + self.group + 16
        self.staged = dp == 4 and self.depth % LANES == 0 and self.depth_out == LANES


def head_backward(sizes, widths, scalars, halves, onehot, weight_in, taps, weight_out, masks):
    rows = onehot.shape[0]
    wide, hidden = weight_in.shape
    chunks = hidden // LANES
    vmem = pl.BlockSpec(memory_space=pltpu.VMEM)
    anywhere = pl.BlockSpec(memory_space=pl.ANY)
    span = 2 * REACH * (PC + 1) + rows
    return pl.pallas_call(
        functools.partial(head_kernel, sizes, widths),
        out_shape=[
            jax.ShapeDtypeStruct((rows, wide), jnp.bfloat16),
            jax.ShapeDtypeStruct((rows, hidden), jnp.bfloat16),
            jax.ShapeDtypeStruct((256, hidden), jnp.float32),
            jax.ShapeDtypeStruct((24, hidden), jnp.float32),
        ]
        + [jax.ShapeDtypeStruct((sizes.message if sizes.staged else 8, hidden), jnp.float32)] * 2,
        in_specs=[pl.BlockSpec(memory_space=pltpu.SMEM)] + [anywhere] * len(halves) + [vmem] * 6,
        out_specs=[anywhere] + [vmem] * 5,
        scratch_shapes=[
            pltpu.VMEM((rows, wide), jnp.bfloat16),
            pltpu.VMEM((3, chunks, span, LANES), jnp.float32),
            pltpu.VMEM((3, chunks, span, LANES), jnp.float32),
            pltpu.VMEM((chunks, rows, LANES), jnp.float32),
            pltpu.VMEM((rows, hidden), jnp.bfloat16),
            pltpu.VMEM((rows, 256), jnp.bfloat16),
            pltpu.SemaphoreType.DMA((len(widths), 2)),
            pltpu.SemaphoreType.DMA,
        ],
        compiler_params=pltpu.CompilerParams(vmem_limit_bytes=30 * 1024 * 1024),
        name="head",
    )(scalars, *halves, weight_in, taps, weight_out, onehot, *masks)


def blocks_kernel(sizes, scalars, x, dpre, gout, small, late, own, stats):
    norm = message(sizes, scalars[5], x, dpre, gout, small, late, True)
    norm = norm + message(sizes, scalars[6], x, dpre, gout, small, own, False)
    stats[...] = jnp.zeros(stats.shape, jnp.float32)
    stats[0:1, :] = norm + small[18:19, :LANES]
    stats[1:2, :] = small[16:17, :LANES]
    for c in range(sizes.chunks):
        stats[2 + c : 3 + c, :] = small[17:18, LANES * c : LANES * c + LANES]


def sum_kernel(sizes, parts, last, stats, share_in, share_out, taps_out, line):
    depth, chunks = sizes.depth, sizes.chunks

    def fold(value):
        value = jnp.sum(value.reshape(-1, 8, value.shape[1]), axis=0)
        return sum(value[:, LANES * c : LANES * c + LANES] for c in range(value.shape[1] // LANES))

    mark = depth + sizes.group
    factors = [jnp.exp2(-last[mark + 9 + i : mark + 10 + i, :]) for i in range(3)]
    total = parts[:depth, :] + last[:depth, :] * factors[0]
    share_in[...] = total
    line[0:8, :] = fold(total * total)
    total = parts[depth:mark, :] + last[depth:mark, :] * factors[1]
    line[8:16, :] = fold(total * total)
    for start, group in sizes.groups:
        lane = start // sizes.group * LANES
        count = min(group, sizes.classes - start)
        share_out[start : start + count, 0, :] = total[:count, lane : lane + LANES]
    total = parts[mark : mark + 9, :] + last[mark : mark + 9, :] * factors[2]
    square = jnp.sum(total * total, axis=0, keepdims=True)
    for k in range(9):
        taps_out[k, :, :] = total[k : k + 1, :]
    line[16:24, :] = stats[...]
    line[24:32, :] = jnp.zeros((8, LANES), jnp.float32)
    line[24:25, :] = sum(square[:, LANES * c : LANES * c + LANES] for c in range(chunks))


def norm_kernel(dp, chunks, *refs):
    lines, out = refs[:dp], refs[dp]
    total = lines[0][...]
    for line in lines[1:]:
        total = total + line[...]
    values = [
        jnp.sum(total[16:17, :]),
        jnp.sum(total[17:18, :]),
        jnp.sum(total[18 : 18 + chunks, :]),
        jnp.sum(total[0:8, :]),
        jnp.sum(lines[0][24:25, :]),
        jnp.sum(total[8:16, :]),
    ]
    row = lax.broadcasted_iota(jnp.int32, (8, LANES), 0)
    lane = lax.broadcasted_iota(jnp.int32, (8, LANES), 1)
    spread = jnp.zeros((8, LANES), jnp.float32)
    for i, value in enumerate(values):
        spread = jnp.where((row == i // 3) & (lane == i % 3), value, spread)
    out[...] = jnp.log(1e-12 + spread)[:2, :3]


def permute(value, pairs):
    return lax.ppermute(value, "dp", pairs)


def add_kernel(sizes, scalars, mine, theirs, out):
    depth, group = sizes.depth, sizes.group
    mark = depth + group
    end = (scalars[6] == 0) | (scalars[6] == 3)

    @pl.when(end)
    def _():
        out[...] = mine[...]

    @pl.when(jnp.logical_not(end))
    def _():
        for i, (start, stop) in enumerate(((0, depth), (depth, mark), (mark, mark + 9))):
            at = mark + 9 + i
            a, b = mine[at : at + 1, :], theirs[at : at + 1, :]
            common = jnp.minimum(a, b)
            out[start:stop, :] = mine[start:stop, :] * jnp.exp2(common - a) + theirs[
                start:stop, :
            ] * jnp.exp2(common - b)
            out[at : at + 1, :] = common
        out[mark + 12 :, :] = mine[mark + 12 :, :]


def by_row(sizes, shape, three):
    row = lax.broadcasted_iota(jnp.int32, shape, 0)
    return jnp.where(
        row < sizes.depth, three[0], jnp.where(row < sizes.depth + sizes.group, three[1], three[2])
    )


def staged_sums(sizes, me, scalars, xrows, dpre, gout, small, first, early):
    vmem = pl.BlockSpec(memory_space=pltpu.VMEM)
    smem = pl.BlockSpec(memory_space=pltpu.SMEM)
    hidden = dpre.shape[1]
    shape = (sizes.message, hidden)
    full = jax.ShapeDtypeStruct(shape, jnp.float32)
    lines = jax.ShapeDtypeStruct((8, LANES), jnp.float32)
    half = jnp.float16
    near = permute(first.astype(half), [(0, 1), (1, 0), (2, 3), (3, 2)])
    early = early.astype(half)
    middle = permute(early, [(1, 2), (2, 1)])
    skip = permute(early, [(0, 2), (3, 1)])
    late, own, stats = pl.pallas_call(
        functools.partial(blocks_kernel, sizes),
        out_shape=[full, full, lines],
        in_specs=[smem] + [vmem] * 4,
        out_specs=[vmem] * 3,
        compiler_params=pltpu.CompilerParams(vmem_limit_bytes=16 * 1024 * 1024),
        cost_estimate=pl.CostEstimate(
            flops=4 * sizes.depth * dpre.shape[0] * hidden,
            bytes_accessed=2 * xrows.size + 2 * dpre.size + 8 * sizes.message * hidden,
            transcendentals=0,
        ),
        name="blocks",
    )(scalars, xrows, dpre, gout, small)
    end = (me == 0) | (me == 3)
    mark = sizes.depth + sizes.group + 9
    both = pl.pallas_call(
        functools.partial(add_kernel, sizes),
        out_shape=full,
        in_specs=[smem, vmem, vmem],
        out_specs=vmem,
        compiler_params=pltpu.CompilerParams(vmem_limit_bytes=8 * 1024 * 1024),
        name="add",
    )(scalars, late, near.astype(jnp.float32))
    both = both.astype(half)
    near, skip, middle, _ = lax.optimization_barrier((near, skip, middle, both))
    far = permute(both, [(0, 1), (3, 2), (1, 3), (2, 0)])

    def split(value):
        return [value[mark + i : mark + i + 1] for i in range(3)]


    def decode(value):
        value = value.astype(jnp.float32)
        return value * by_row(sizes, shape, [jnp.exp2(-v) for v in split(value)])

    parts = own + decode(jnp.where(end, near, skip)) + decode(middle)
    return parts, far.astype(jnp.float32), stats


def per_device(sizes, dp, trials, features, owner, dilation_index, labels, input_weight, taps, output_weight):
    here, core, widths, halves = pieces(features[0, 0], "trial", trials, owner[0])
    me = lax.axis_index("dp")
    dil = dilation_index[0] + 1
    rows = features.shape[2]
    onehot = (labels[0][:, None] == jnp.arange(256, dtype=jnp.int32)[None, :]).astype(jnp.bfloat16)
    column = lax.broadcasted_iota(jnp.int32, (rows, LANES), 0) % PC
    before = (column < PC - dil).astype(jnp.float32)
    after = (column >= dil).astype(jnp.float32)
    classes, chunks = sizes.classes, sizes.chunks
    weight_out = jnp.pad(output_weight[0].T, ((0, 256 - classes), (0, 0)))
    high = me >= 2
    odd = me % 2
    end = (me == 0) | (me == 3)
    step, jump = jnp.where(odd == 0, 1, 2), jnp.where(high, me - 2, me + 2)
    to = [3 * (1 - odd), jnp.where(end, jump, step), jnp.where(end, step, jump), me]
    scalars = jnp.stack([dil, here, core] + to).astype(jnp.int32)
    xrows, dpre, gout, small, first, early = head_backward(
        sizes,
        widths,
        scalars,
        halves,
        onehot,
        input_weight[0],
        taps[0][:, None, :],
        weight_out,
        (after, before),
    )
    if not sizes.staged:
        return general_sums(sizes, xrows, dpre, gout, small)
    parts, last, stats = staged_sums(sizes, me, scalars, xrows, dpre, gout, small, first, early)
    vmem = pl.BlockSpec(memory_space=pltpu.VMEM)
    hidden = dpre.shape[1]
    share_in, share_out, total_taps, line = pl.pallas_call(
        functools.partial(sum_kernel, sizes),
        out_shape=[
            jax.ShapeDtypeStruct((sizes.depth, hidden), jnp.float32),
            jax.ShapeDtypeStruct((classes, 1, sizes.depth_out), jnp.float32),
            jax.ShapeDtypeStruct((9, 1, hidden), jnp.float32),
            jax.ShapeDtypeStruct((32, LANES), jnp.float32),
        ],
        in_specs=[vmem] * 3,
        out_specs=[vmem] * 4,
        compiler_params=pltpu.CompilerParams(vmem_limit_bytes=8 * 1024 * 1024),
        name="sums",
    )(parts, last, stats)
    lines = [line] + [permute(line, [(i, i ^ s) for i in range(dp)]) for s in range(1, dp)]
    norms = pl.pallas_call(
        functools.partial(norm_kernel, dp, chunks),
        out_shape=jax.ShapeDtypeStruct((2, 3), jnp.float32),
        in_specs=[vmem] * dp,
        out_specs=vmem,
        compiler_params=pltpu.CompilerParams(vmem_limit_bytes=4 * 1024 * 1024),
        name="norms",
    )(*lines)
    share_out = jnp.transpose(share_out, (1, 2, 0))
    return (share_in[None], jnp.transpose(total_taps, (1, 0, 2)), share_out, norms[None])


def general_sums(sizes, xrows, dpre, gout, small):
    g_in = jnp.dot(xrows.T, dpre, preferred_element_type=jnp.float32)
    g_out = gout[: sizes.classes].T
    g_taps = small[:9]
    share_in = lax.psum_scatter(g_in, "dp", scatter_dimension=0, tiled=True)
    share_out = lax.psum_scatter(g_out, "dp", scatter_dimension=0, tiled=True)
    local = jnp.stack([jnp.sum(g_in * g_in), jnp.sum(g_taps * g_taps), jnp.sum(g_out * g_out)])
    share_sq = jnp.stack([jnp.sum(share_in * share_in), jnp.sum(share_out * share_out)])
    total_taps, squares, share_total = lax.psum((g_taps, local, share_sq), "dp")
    totals = jnp.stack([share_total[0], jnp.sum(total_taps * total_taps), share_total[1]])
    norms = jnp.log(1e-12 + jnp.stack([squares, totals]))
    return (share_in[None], total_taps[None], share_out[None], norms[None])


def solution(mesh):
    dp, trials = mesh.shape["dp"], mesh.shape["trial"]
    placed = (
        P(("groups", "dp"), "trial", None, None),
        P(("groups", "dp")),
        P("trial"),
        P(("groups", "dp"), None),
        P("trial", None, None),
        P("trial", None, None),
        P("trial", None, None),
    )

    def step(*args):
        (wide, hidden), classes = args[4].shape[1:], args[6].shape[2]
        return per_device(Sizes(wide, hidden, classes, dp), dp, trials, *args)

    return jax.shard_map(
        step,
        mesh=mesh,
        in_specs=placed,
        out_specs=(
            P(("groups", "trial"), "dp", None),
            P(("groups", "trial"), None, None),
            P(("groups", "trial"), "dp", None),
            P(("groups", "trial"), None, None),
        ),
        check_vma=False,
    )
```

```python
import functools
import math

import jax
import jax.numpy as jnp
from jax import lax
from jax.experimental import pallas as pl
from jax.experimental.pallas import tpu as pltpu
from jax.sharding import PartitionSpec as P

PC = 37
LANES = 128
STEP = 32
REACH = 4
OFFSETS = [(a, b) for a in (-1, 0, 1) for b in (-1, 0, 1)]
X_LIMIT = 6.0
ROOM = 16384.0


def pieces(block, axis, size, source):
    width = block.shape[1] // 2
    if size != 4:
        block = jnp.where(lax.axis_index(axis) == source, block, jnp.zeros_like(block))
        block = lax.psum(block, axis)
        low, high = block[:, :width], block[:, width:]
        zero = jnp.int32(0)
        return zero + 1, zero, (width,), (low, low, high, high)
    me = lax.axis_index(axis)
    core = me % 2
    mate = [(0, 1), (1, 0), (2, 3), (3, 2)]
    across = [(0, 2), (2, 0), (1, 3), (3, 1)]
    here = ((source // 2) == (me // 2)).astype(jnp.int32)
    widths = split_width(width)
    rows = block.shape[0]
    switches = jnp.stack([core, (source % 2 == core).astype(jnp.int32)]).astype(jnp.int32)
    smem = pl.BlockSpec(memory_space=pltpu.SMEM)
    vmem = pl.BlockSpec(memory_space=pltpu.VMEM)
    anywhere = pl.BlockSpec(memory_space=pl.ANY)
    hbm = pl.BlockSpec(memory_space=pltpu.MemorySpace.HBM)
    sent = pl.pallas_call(
        give_kernel,
        out_shape=jax.ShapeDtypeStruct((rows, width), block.dtype),
        in_specs=[smem, hbm],
        out_specs=vmem,
        scratch_shapes=[pltpu.SemaphoreType.DMA],
        compiler_params=pltpu.CompilerParams(vmem_limit_bytes=60 * 1024 * 1024),
        name="give",
    )(switches, block)
    got = lax.ppermute(sent, axis, mate)
    held = pl.pallas_call(
        functools.partial(hold_kernel, widths),
        out_shape=[jax.ShapeDtypeStruct((rows, piece), block.dtype) for piece in widths],
        in_specs=[smem, hbm, anywhere],
        out_specs=[vmem] * len(widths),
        scratch_shapes=[pltpu.SemaphoreType.DMA((len(widths),))],
        compiler_params=pltpu.CompilerParams(vmem_limit_bytes=4 * 1024 * 1024),
        name="hold",
    )(switches, block, got)
    values = []
    for piece in held:
        other = lax.ppermute(piece, axis, across)
        back_held = lax.ppermute(piece, axis, mate)
        back_other = lax.ppermute(other, axis, mate)
        values += [piece, other, back_held, back_other]
    return here, core, widths, tuple(values)


def give_kernel(switches, block, out, sem):
    width = out.shape[1]
    column = pl.multiple_of((1 - switches[0]) * width, LANES)
    copy = pltpu.make_async_copy(block.at[:, pl.ds(column, width)], out, sem)
    copy.start()
    copy.wait()


def hold_kernel(widths, switches, block, got, *rest):
    outs, sem = rest[:-1], rest[-1]
    width = got.shape[1]
    column = switches[0] * width
    starts = [sum(widths[:i]) for i in range(len(widths))]

    def copy(i, own):
        if own:
            source = block.at[:, pl.ds(pl.multiple_of(column + starts[i], LANES), widths[i])]
        else:
            source = got.at[:, pl.ds(starts[i], widths[i])]
        return pltpu.make_async_copy(source, outs[i], sem.at[i])

    @pl.when(switches[1] == 1)
    def _():
        for i in range(len(widths)):
            copy(i, True).start()

    @pl.when(switches[1] == 0)
    def _():
        for i in range(len(widths)):
            copy(i, False).start()

    for i in range(len(widths)):
        copy(i, False).wait()


def split_width(width):
    tiles = width // LANES
    last = max(tiles // 3, 1)
    return tuple(LANES * n for n in (tiles - last, last) if n > 0)


def gelu_parts(value):
    inner = 0.7978845608 * (value + 0.044715 * value * value * value)
    tanh_val = jnp.tanh(inner)
    out_val = 0.5 * value * (1.0 + tanh_val)
    slope = 0.5 * (1.0 + tanh_val) + 0.5 * value * (1.0 - tanh_val * tanh_val) * 0.7978845608 * (
        1.0 + 3.0 * 0.044715 * value * value
    )
    return (out_val, slope)


def exponent(size):
    size = jnp.maximum(jnp.full((1, LANES), size, jnp.float32), 1e-30)
    return jnp.clip(jnp.floor(jnp.log(ROOM / size) * (1.0 / math.log(2.0))), -100.0, 100.0)


def head_kernel(
    sizes,
    widths,
    scalars,
    *refs,
):
    halves, refs = refs[: 4 * len(widths)], refs[4 * len(widths) :]
    weight_in, taps, weight_out, onehot, after, before = refs[:6]
    x_out, dpre_out, gout, small, first = refs[6:11]
    x_vmem, pre, dys, slope, hid, dlog, sem_in, sem_out = refs[11:]
    rows = x_vmem.shape[0]
    width = x_vmem.shape[1] // 2
    hidden = weight_in.shape[1]
    chunks = hidden // LANES
    guard = REACH * (PC + 1)
    dil, here, core = scalars[0], scalars[1], scalars[2]

    def fetch(kind, index):
        place = core if kind < 2 else 1 - core
        column = pl.multiple_of(place * width + sum(widths[:index]), LANES)
        target = x_vmem.at[:, pl.ds(column, widths[index])]
        return pltpu.make_async_copy(halves[4 * index + kind], target, sem_in.at[index, kind // 2])

    @pl.when(here == 1)
    def _():
        for index in range(len(widths)):
            fetch(0, index).start()
            fetch(2, index).start()

    @pl.when(here == 0)
    def _():
        for index in range(len(widths)):
            fetch(1, index).start()
            fetch(3, index).start()

    for shift in range(3):
        for c in range(chunks):
            for ref in (pre, dys):
                ref[shift, c, :guard, :] = jnp.zeros((guard, LANES), jnp.float32)
                tail = ref.shape[2] - guard - rows
                ref[shift, c, guard + rows :, :] = jnp.zeros((tail, LANES), jnp.float32)
    for index in range(len(widths)):
        fetch(0, index).wait()
        fetch(2, index).wait()
    save = pltpu.make_async_copy(x_vmem, x_out, sem_out)
    save.start()

    masks = (after, None, before)
    for n in range(hidden // 256):
        value = jnp.dot(
            x_vmem[...], weight_in[:, 256 * n : 256 * n + 256], preferred_element_type=jnp.float32
        )
        for h in range(2):
            part = value[:, LANES * h : LANES * h + LANES]
            for shift in range(3):
                mask = (before, None, after)[shift]
                pre[shift, 2 * n + h, guard : guard + rows, :] = (
                    part if mask is None else part * mask[...]
                )

    starts = [dil * (PC * a + b) for a, b in OFFSETS]

    def forward(row, count):
        for c in range(chunks):
            total = None
            for k in range(9):
                term = (
                    pre[k % 3, c, pl.ds(guard + row + starts[k], count), :]
                    * taps[k, :, LANES * c : LANES * c + LANES]
                )
                total = term if total is None else total + term
            act, grad = gelu_parts(total)
            slope[c, pl.ds(row, count), :] = grad
            hid[pl.ds(row, count), LANES * c : LANES * c + LANES] = act.astype(jnp.bfloat16)

    whole = rows // STEP
    left = rows - whole * STEP

    @pl.loop(0, whole)
    def _(i):
        forward(pl.multiple_of(i * STEP, STEP), STEP)

    if left:
        forward(whole * STEP, left)

    logits = lax.dot_general(
        hid[...], weight_out[...], (((1,), (1,)), ((), ())), preferred_element_type=jnp.float32
    )
    lane = lax.broadcasted_iota(jnp.int32, logits.shape, 1)
    logits = jnp.where(lane < sizes.classes, logits, -1e30)
    peak = jnp.max(logits, axis=1, keepdims=True)
    power = jnp.exp(logits - peak)
    prob = power / jnp.sum(power, axis=1, keepdims=True)
    dlog[...] = (prob - onehot[...].astype(jnp.float32)).astype(jnp.bfloat16)

    gout[...] = lax.dot_general(
        dlog[...], hid[...], (((0,), (0,)), ((), ())), preferred_element_type=jnp.float32
    )
    for n in range(hidden // 256):
        value = jnp.dot(
            dlog[...], weight_out[:, 256 * n : 256 * n + 256], preferred_element_type=jnp.float32
        )
        for h in range(2):
            c = 2 * n + h
            part = value[:, LANES * h : LANES * h + LANES] * slope[c]
            for shift in range(3):
                mask = (after, None, before)[shift]
                dys[shift, c, guard : guard + rows, :] = part if mask is None else part * mask[...]

    def fold(value):
        return jnp.sum(value.reshape(-1, 8, LANES), axis=0)

    biggest = jnp.zeros((8, LANES), jnp.float32)
    taps_biggest = jnp.zeros((1, LANES), jnp.float32)
    small[...] = jnp.zeros(small.shape, jnp.float32)
    taps_square = jnp.zeros((1, LANES), jnp.float32)
    for c in range(chunks):
        column = slice(LANES * c, LANES * c + LANES)

        def backward(row, count, carry):
            sums, top = carry
            dy = dys[1, c, pl.ds(guard + row, count), :]
            total = None
            out = []
            for k in range(9):
                out.append(sums[k] + fold(dy * pre[k % 3, c, pl.ds(guard + row + starts[k], count), :]))
                term = (
                    dys[k % 3, c, pl.ds(guard + row - starts[k], count), :] * taps[k, :, column]
                )
                total = term if total is None else total + term
            dpre_out[pl.ds(row, count), column] = total.astype(jnp.bfloat16)
            size = jnp.max(jnp.abs(total).reshape(-1, 8, LANES), axis=0)
            return tuple(out), jnp.maximum(top, size)

        zeros = tuple(jnp.zeros((8, LANES), jnp.float32) for _ in range(9))
        carry = lax.fori_loop(
            0,
            whole,
            lambda i, carry: backward(pl.multiple_of(i * STEP, STEP), STEP, carry),
            (zeros, biggest),
        )
        if left:
            carry = backward(whole * STEP, left, carry)
        sums, biggest = carry
        for k in range(9):
            value = jnp.sum(sums[k], axis=0, keepdims=True)
            taps_square = taps_square + value * value
            taps_biggest = jnp.maximum(taps_biggest, jnp.abs(value))
            small[k : k + 1, column] = value
    powers = (
        exponent(jnp.max(biggest) * (X_LIMIT * rows)),
        exponent(jnp.max(jnp.abs(gout[...]))),
        exponent(jnp.max(taps_biggest)),
    )
    for c in range(chunks):
        for i, power in enumerate(powers):
            small[9 + i : 10 + i, LANES * c : LANES * c + LANES] = power
    small[16:17, :LANES] = taps_square
    small[17:18, :] = jnp.sum(gout[...] * gout[...], axis=0, keepdims=True)
    if first.shape[0] == sizes.message:
        norm = message(sizes, scalars[3], x_vmem, dpre_out, gout, small, first, True)
        small[18:19, :LANES] = norm
    save.wait()


def message(sizes, place, x, dpre, gout, small, out, scaled):
    depth, depth_out = sizes.depth, sizes.depth_out
    column = pl.multiple_of(place * depth, LANES)
    block = lax.dot_general(
        x[:, pl.ds(column, depth)], dpre[...], (((0,), (0,)), ((), ())), preferred_element_type=jnp.float32
    )
    hidden = block.shape[1]
    chunks = hidden // LANES
    norm = jnp.sum(block * block, axis=0, keepdims=True)
    norm = sum(norm[:, LANES * c : LANES * c + LANES] for c in range(chunks))
    factors = [jnp.exp2(small[9 + i : 10 + i, :]) if scaled else 1.0 for i in range(3)]
    out[:depth, :] = block * factors[0]
    out[depth:, :] = jnp.zeros((out.shape[0] - depth, hidden), jnp.float32)
    column = pl.multiple_of(place * depth_out, LANES)
    for start, group in sizes.groups:
        value = gout[start : start + group, pl.ds(column, depth_out)]
        lane = start // sizes.group * LANES
        factor = factors[1][:, :LANES] if scaled else 1.0
        out[depth : depth + group, lane : lane + LANES] = value * factor
    row = depth + sizes.group
    out[row : row + 9, :] = small[0:9, :] * factors[2]
    if scaled:
        out[row + 9 : row + 12, :] = small[9:12, :]
    return norm


class Sizes:
    def __init__(self, wide, hidden, classes, dp):
        self.classes = classes
        self.depth = wide // dp
        self.depth_out = hidden // dp
        self.chunks = hidden // LANES
        self.class_rows = (classes + 7) // 8 * 8
        self.group = (self.class_rows // self.chunks + 7) // 8 * 8
        self.groups = [
            (at, min(self.group, self.class_rows - at)) for at in range(0, self.class_rows, self.group)
        ]
        self.message = self.depth + self.group + 16
        self.staged = dp == 4 and self.depth % LANES == 0 and self.depth_out == LANES


def head_backward(sizes, widths, scalars, halves, onehot, weight_in, taps, weight_out, masks):
    rows = onehot.shape[0]
    wide, hidden = weight_in.shape
    chunks = hidden // LANES
    vmem = pl.BlockSpec(memory_space=pltpu.VMEM)
    anywhere = pl.BlockSpec(memory_space=pl.ANY)
    span = 2 * REACH * (PC + 1) + rows
    return pl.pallas_call(
        functools.partial(head_kernel, sizes, widths),
        out_shape=[
            jax.ShapeDtypeStruct((rows, wide), jnp.bfloat16),
            jax.ShapeDtypeStruct((rows, hidden), jnp.bfloat16),
            jax.ShapeDtypeStruct((256, hidden), jnp.float32),
            jax.ShapeDtypeStruct((24, hidden), jnp.float32),
            jax.ShapeDtypeStruct((sizes.message if sizes.staged else 8, hidden), jnp.float32),
        ],
        in_specs=[pl.BlockSpec(memory_space=pltpu.SMEM)] + [anywhere] * len(halves) + [vmem] * 6,
        out_specs=[anywhere] + [vmem] * 4,
        scratch_shapes=[
            pltpu.VMEM((rows, wide), jnp.bfloat16),
            pltpu.VMEM((3, chunks, span, LANES), jnp.float32),
            pltpu.VMEM((3, chunks, span, LANES), jnp.float32),
            pltpu.VMEM((chunks, rows, LANES), jnp.float32),
            pltpu.VMEM((rows, hidden), jnp.bfloat16),
            pltpu.VMEM((rows, 256), jnp.bfloat16),
            pltpu.SemaphoreType.DMA((len(widths), 2)),
            pltpu.SemaphoreType.DMA,
        ],
        compiler_params=pltpu.CompilerParams(vmem_limit_bytes=30 * 1024 * 1024),
        name="head",
    )(scalars, *halves, weight_in, taps, weight_out, onehot, *masks)


def blocks_kernel(sizes, scalars, x, dpre, gout, small, early, late, own, stats):
    norm = message(sizes, scalars[4], x, dpre, gout, small, early, True)
    norm = norm + message(sizes, scalars[5], x, dpre, gout, small, late, True)
    norm = norm + message(sizes, scalars[6], x, dpre, gout, small, own, False)
    stats[...] = jnp.zeros(stats.shape, jnp.float32)
    stats[0:1, :] = norm + small[18:19, :LANES]
    stats[1:2, :] = small[16:17, :LANES]
    for c in range(sizes.chunks):
        stats[2 + c : 3 + c, :] = small[17:18, LANES * c : LANES * c + LANES]


def sum_kernel(sizes, parts, last, stats, share_in, share_out, taps_out, line):
    depth, chunks = sizes.depth, sizes.chunks

    def fold(value):
        value = jnp.sum(value.reshape(-1, 8, value.shape[1]), axis=0)
        return sum(value[:, LANES * c : LANES * c + LANES] for c in range(value.shape[1] // LANES))

    mark = depth + sizes.group
    factors = [jnp.exp2(-last[mark + 9 + i : mark + 10 + i, :]) for i in range(3)]
    total = parts[:depth, :] + last[:depth, :] * factors[0]
    share_in[...] = total
    line[0:8, :] = fold(total * total)
    total = parts[depth:mark, :] + last[depth:mark, :] * factors[1]
    line[8:16, :] = fold(total * total)
    for start, group in sizes.groups:
        lane = start // sizes.group * LANES
        count = min(group, sizes.classes - start)
        share_out[start : start + count, 0, :] = total[:count, lane : lane + LANES]
    total = parts[mark : mark + 9, :] + last[mark : mark + 9, :] * factors[2]
    square = jnp.sum(total * total, axis=0, keepdims=True)
    for k in range(9):
        taps_out[k, :, :] = total[k : k + 1, :]
    line[16:24, :] = stats[...]
    line[24:32, :] = jnp.zeros((8, LANES), jnp.float32)
    line[24:25, :] = sum(square[:, LANES * c : LANES * c + LANES] for c in range(chunks))


def norm_kernel(dp, chunks, *refs):
    lines, out = refs[:dp], refs[dp]
    total = lines[0][...]
    for line in lines[1:]:
        total = total + line[...]
    values = [
        jnp.sum(total[16:17, :]),
        jnp.sum(total[17:18, :]),
        jnp.sum(total[18 : 18 + chunks, :]),
        jnp.sum(total[0:8, :]),
        jnp.sum(lines[0][24:25, :]),
        jnp.sum(total[8:16, :]),
    ]
    row = lax.broadcasted_iota(jnp.int32, (8, LANES), 0)
    lane = lax.broadcasted_iota(jnp.int32, (8, LANES), 1)
    spread = jnp.zeros((8, LANES), jnp.float32)
    for i, value in enumerate(values):
        spread = jnp.where((row == i // 3) & (lane == i % 3), value, spread)
    out[...] = jnp.log(1e-12 + spread)[:2, :3]


def permute(value, pairs):
    return lax.ppermute(value, "dp", pairs)


def add_kernel(sizes, scalars, mine, theirs, own, middle, out, parts):
    depth, group = sizes.depth, sizes.group
    mark = depth + group
    end = (scalars[6] == 0) | (scalars[6] == 3)
    spans = tuple(enumerate(((0, depth), (depth, mark), (mark, mark + 9))))

    @pl.when(end)
    def _():
        out[...] = mine[...]
        parts[...] = own[...]

    @pl.when(jnp.logical_not(end))
    def _():
        for i, (start, stop) in spans:
            at = mark + 9 + i
            a, b = mine[at : at + 1, :], theirs[at : at + 1, :]
            common = jnp.minimum(a, b)
            out[start:stop, :] = mine[start:stop, :] * jnp.exp2(common - a) + theirs[
                start:stop, :
            ] * jnp.exp2(common - b)
            out[at : at + 1, :] = common
            parts[start:stop, :] = own[start:stop, :] + middle[start:stop, :] * jnp.exp2(
                -middle[at : at + 1, :]
            )
        out[mark + 12 :, :] = mine[mark + 12 :, :]
        parts[mark + 9 :, :] = own[mark + 9 :, :]


def by_row(sizes, shape, three):
    row = lax.broadcasted_iota(jnp.int32, shape, 0)
    return jnp.where(
        row < sizes.depth, three[0], jnp.where(row < sizes.depth + sizes.group, three[1], three[2])
    )


def staged_sums(sizes, me, scalars, xrows, dpre, gout, small, first):
    vmem = pl.BlockSpec(memory_space=pltpu.VMEM)
    smem = pl.BlockSpec(memory_space=pltpu.SMEM)
    hidden = dpre.shape[1]
    shape = (sizes.message, hidden)
    full = jax.ShapeDtypeStruct(shape, jnp.float32)
    lines = jax.ShapeDtypeStruct((8, LANES), jnp.float32)
    half = jnp.float16
    first = first.astype(half)
    near = permute(first, [(0, 1), (3, 2)])
    middle = permute(first, [(1, 2), (2, 1)])
    early, late, own, stats = pl.pallas_call(
        functools.partial(blocks_kernel, sizes),
        out_shape=[full, full, full, lines],
        in_specs=[smem] + [vmem] * 4,
        out_specs=[vmem] * 4,
        compiler_params=pltpu.CompilerParams(vmem_limit_bytes=16 * 1024 * 1024),
        cost_estimate=pl.CostEstimate(
            flops=6 * sizes.depth * dpre.shape[0] * hidden,
            bytes_accessed=2 * xrows.size + 2 * dpre.size + 12 * sizes.message * hidden,
            transcendentals=0,
        ),
        name="blocks",
    )(scalars, xrows, dpre, gout, small)
    outer = permute(early.astype(half), [(0, 2), (3, 1), (1, 0), (2, 3)])
    both, parts = pl.pallas_call(
        functools.partial(add_kernel, sizes),
        out_shape=[full, full],
        in_specs=[smem] + [vmem] * 4,
        out_specs=[vmem] * 2,
        compiler_params=pltpu.CompilerParams(vmem_limit_bytes=8 * 1024 * 1024),
        name="add",
    )(scalars, late, near.astype(jnp.float32), own, middle.astype(jnp.float32))
    both = both.astype(half)
    far = permute(both, [(0, 1), (3, 2), (1, 3), (2, 0)])
    outer, _ = lax.optimization_barrier((outer, both))
    outer = outer.astype(jnp.float32)
    mark = sizes.depth + sizes.group + 9
    parts = parts + outer * by_row(
        sizes, shape, [jnp.exp2(-outer[mark + i : mark + i + 1]) for i in range(3)]
    )
    return parts, far.astype(jnp.float32), stats


def per_device(sizes, dp, trials, features, owner, dilation_index, labels, input_weight, taps, output_weight):
    here, core, widths, halves = pieces(features[0, 0], "trial", trials, owner[0])
    me = lax.axis_index("dp")
    dil = dilation_index[0] + 1
    rows = features.shape[2]
    onehot = (labels[0][:, None] == jnp.arange(256, dtype=jnp.int32)[None, :]).astype(jnp.bfloat16)
    column = lax.broadcasted_iota(jnp.int32, (rows, LANES), 0) % PC
    before = (column < PC - dil).astype(jnp.float32)
    after = (column >= dil).astype(jnp.float32)
    classes, chunks = sizes.classes, sizes.chunks
    weight_out = jnp.pad(output_weight[0].T, ((0, 256 - classes), (0, 0)))
    high = me >= 2
    odd = me % 2
    end = (me == 0) | (me == 3)
    step, jump = jnp.where(odd == 0, 1, 2), jnp.where(high, me - 2, me + 2)
    edge = 3 * (1 - odd)
    to = [jnp.where(end, edge, step), jnp.where(end, jump, edge), jnp.where(end, step, jump), me]
    scalars = jnp.stack([dil, here, core] + to).astype(jnp.int32)
    xrows, dpre, gout, small, first = head_backward(
        sizes,
        widths,
        scalars,
        halves,
        onehot,
        input_weight[0],
        taps[0][:, None, :],
        weight_out,
        (after, before),
    )
    if not sizes.staged:
        return general_sums(sizes, xrows, dpre, gout, small)
    parts, last, stats = staged_sums(sizes, me, scalars, xrows, dpre, gout, small, first)
    vmem = pl.BlockSpec(memory_space=pltpu.VMEM)
    hidden = dpre.shape[1]
    share_in, share_out, total_taps, line = pl.pallas_call(
        functools.partial(sum_kernel, sizes),
        out_shape=[
            jax.ShapeDtypeStruct((sizes.depth, hidden), jnp.float32),
            jax.ShapeDtypeStruct((classes, 1, sizes.depth_out), jnp.float32),
            jax.ShapeDtypeStruct((9, 1, hidden), jnp.float32),
            jax.ShapeDtypeStruct((32, LANES), jnp.float32),
        ],
        in_specs=[vmem] * 3,
        out_specs=[vmem] * 4,
        compiler_params=pltpu.CompilerParams(vmem_limit_bytes=8 * 1024 * 1024),
        name="sums",
    )(parts, last, stats)
    lines = [line] + [permute(line, [(i, i ^ s) for i in range(dp)]) for s in range(1, dp)]
    norms = pl.pallas_call(
        functools.partial(norm_kernel, dp, chunks),
        out_shape=jax.ShapeDtypeStruct((2, 3), jnp.float32),
        in_specs=[vmem] * dp,
        out_specs=vmem,
        compiler_params=pltpu.CompilerParams(vmem_limit_bytes=4 * 1024 * 1024),
        name="norms",
    )(*lines)
    share_out = jnp.transpose(share_out, (1, 2, 0))
    return (share_in[None], jnp.transpose(total_taps, (1, 0, 2)), share_out, norms[None])


def general_sums(sizes, xrows, dpre, gout, small):
    g_in = jnp.dot(xrows.T, dpre, preferred_element_type=jnp.float32)
    g_out = gout[: sizes.classes].T
    g_taps = small[:9]
    share_in = lax.psum_scatter(g_in, "dp", scatter_dimension=0, tiled=True)
    share_out = lax.psum_scatter(g_out, "dp", scatter_dimension=0, tiled=True)
    local = jnp.stack([jnp.sum(g_in * g_in), jnp.sum(g_taps * g_taps), jnp.sum(g_out * g_out)])
    share_sq = jnp.stack([jnp.sum(share_in * share_in), jnp.sum(share_out * share_out)])
    total_taps, squares, share_total = lax.psum((g_taps, local, share_sq), "dp")
    totals = jnp.stack([share_total[0], jnp.sum(total_taps * total_taps), share_total[1]])
    norms = jnp.log(1e-12 + jnp.stack([squares, totals]))
    return (share_in[None], total_taps[None], share_out[None], norms[None])


def solution(mesh):
    dp, trials = mesh.shape["dp"], mesh.shape["trial"]
    placed = (
        P(("groups", "dp"), "trial", None, None),
        P(("groups", "dp")),
        P("trial"),
        P(("groups", "dp"), None),
        P("trial", None, None),
        P("trial", None, None),
        P("trial", None, None),
    )

    def step(*args):
        (wide, hidden), classes = args[4].shape[1:], args[6].shape[2]
        return per_device(Sizes(wide, hidden, classes, dp), dp, trials, *args)

    return jax.shard_map(
        step,
        mesh=mesh,
        in_specs=placed,
        out_specs=(
            P(("groups", "trial"), "dp", None),
            P(("groups", "trial"), None, None),
            P(("groups", "trial"), "dp", None),
            P(("groups", "trial"), None, None),
        ),
        check_vma=False,
    )
```

```python
import functools
import math

import jax
import jax.numpy as jnp
from jax import lax
from jax.experimental import pallas as pl
from jax.experimental.pallas import tpu as pltpu
from jax.sharding import PartitionSpec as P

PC = 37
LANES = 128
STEP = 32
REACH = 4
OFFSETS = [(a, b) for a in (-1, 0, 1) for b in (-1, 0, 1)]
X_LIMIT = 6.0
ROOM = 16384.0


def pieces(block, axis, size, source):
    width = block.shape[1] // 2
    if size != 4:
        block = jnp.where(lax.axis_index(axis) == source, block, jnp.zeros_like(block))
        block = lax.psum(block, axis)
        low, high = block[:, :width], block[:, width:]
        zero = jnp.int32(0)
        return zero + 1, zero, (width,), (low, low, high, high)
    me = lax.axis_index(axis)
    core = me % 2
    mate = [(0, 1), (1, 0), (2, 3), (3, 2)]
    across = [(0, 2), (2, 0), (1, 3), (3, 1)]
    here = ((source // 2) == (me // 2)).astype(jnp.int32)
    widths = split_width(width)
    got = lax.ppermute(jnp.where(core == 0, block[:, width:], block[:, :width]), axis, mate)
    values = []
    at = 0
    for piece in widths:
        low, high = block[:, at : at + piece], block[:, width + at : width + at + piece]
        kept = jnp.where(core == 0, low, high)
        held = jnp.where(source % 2 == core, kept, got[:, at : at + piece])
        other = lax.ppermute(held, axis, across)
        values += [held, other, lax.ppermute(held, axis, mate), lax.ppermute(other, axis, mate)]
        at += piece
    return here, core, widths, tuple(values)


def split_width(width):
    tiles = width // LANES
    last = max(tiles // 3, 1)
    return tuple(LANES * n for n in (tiles - last, last) if n > 0)


def gelu_parts(value):
    square = value * value
    half = 0.5 + 0.5 * jnp.tanh(value * (0.7978845608 + (0.7978845608 * 0.044715) * square))
    out_val = value * half
    rate = 2.0 * 0.7978845608 + (6.0 * 0.7978845608 * 0.044715) * square
    return (out_val, half + out_val * (1.0 - half) * rate)


def exponent(size):
    size = jnp.maximum(jnp.full((1, LANES), size, jnp.float32), 1e-30)
    return jnp.clip(jnp.floor(jnp.log(ROOM / size) * (1.0 / math.log(2.0))), -100.0, 100.0)


def head_kernel(
    sizes,
    widths,
    scalars,
    *refs,
):
    halves, refs = refs[: 4 * len(widths)], refs[4 * len(widths) :]
    weight_in, taps, weight_out, onehot, after, before = refs[:6]
    x_out, dpre_out, gout, small, first, early = refs[6:12]
    x_vmem, pre, dys, slope, hid, dlog, sem_in, sem_out = refs[12:]
    rows = x_vmem.shape[0]
    width = x_vmem.shape[1] // 2
    hidden = weight_in.shape[1]
    chunks = hidden // LANES
    guard = REACH * (PC + 1)
    dil, here, core = scalars[0], scalars[1], scalars[2]

    def fetch(kind, index):
        column = (core if kind < 2 else 1 - core) * width + sum(widths[:index])
        target = x_vmem.at[:, pl.ds(pl.multiple_of(column, LANES), widths[index])]
        return pltpu.make_async_copy(halves[4 * index + kind], target, sem_in.at[index, kind // 2])

    for away in (0, 1):

        @pl.when(here == 1 - away)
        def _(away=away):
            for index in range(len(widths)):
                fetch(away, index).start()
                fetch(2 + away, index).start()

    for c in range(chunks):
        for ref in (pre, dys):
            ref[c, :guard, :] = jnp.zeros((guard, LANES), jnp.float32)
            ref[c, guard + rows :, :] = jnp.zeros((guard, LANES), jnp.float32)
    for index in range(len(widths)):
        fetch(0, index).wait()
        fetch(2, index).wait()
    save = pltpu.make_async_copy(x_vmem, x_out, sem_out)
    save.start()

    for n in range(hidden // 256):
        value = jnp.dot(
            x_vmem[...], weight_in[:, 256 * n : 256 * n + 256], preferred_element_type=jnp.float32
        )
        for h in range(2):
            pre[2 * n + h, guard : guard + rows, :] = value[:, LANES * h : LANES * h + LANES]

    starts = [dil * (PC * a + b) for a, b in OFFSETS]

    def column_sums(source, c, row, count, sign):
        column = slice(LANES * c, LANES * c + LANES)
        sums = []
        for b in range(3):
            total = None
            for k in (b, 3 + b, 6 + b):
                at = guard + row + sign * starts[k]
                term = source[c, pl.ds(at, count), :] * taps[k, :, column]
                total = term if total is None else total + term
            sums.append(total)
        return sums

    def forward(row, count):
        low, high = after[pl.ds(row, count), :], before[pl.ds(row, count), :]
        for c in range(chunks):
            sums = column_sums(pre, c, row, count, 1)
            act, grad = gelu_parts(sums[1] + low * sums[0] + high * sums[2])
            slope[c, pl.ds(row, count), :] = grad
            hid[pl.ds(row, count), LANES * c : LANES * c + LANES] = act.astype(jnp.bfloat16)

    whole = rows // STEP
    left = rows - whole * STEP

    @pl.loop(0, whole)
    def _(i):
        forward(pl.multiple_of(i * STEP, STEP), STEP)

    if left:
        forward(whole * STEP, left)

    logits = lax.dot_general(
        hid[...], weight_out[...], (((1,), (1,)), ((), ())), preferred_element_type=jnp.float32
    )
    lane = lax.broadcasted_iota(jnp.int32, logits.shape, 1)
    logits = jnp.where(lane < sizes.classes, logits, -1e30)
    peak = jnp.max(logits, axis=1, keepdims=True)
    power = jnp.exp(logits - peak)
    prob = power / jnp.sum(power, axis=1, keepdims=True)
    dlog[...] = (prob - onehot[...].astype(jnp.float32)).astype(jnp.bfloat16)

    gout[...] = lax.dot_general(
        dlog[...], hid[...], (((0,), (0,)), ((), ())), preferred_element_type=jnp.float32
    )
    for n in range(hidden // 256):
        value = jnp.dot(
            dlog[...], weight_out[:, 256 * n : 256 * n + 256], preferred_element_type=jnp.float32
        )
        for h in range(2):
            c = 2 * n + h
            dys[c, guard : guard + rows, :] = value[:, LANES * h : LANES * h + LANES] * slope[c]

    def fold(value):
        return jnp.sum(value.reshape(-1, 8, LANES), axis=0)

    biggest = jnp.zeros((8, LANES), jnp.float32)
    taps_biggest = jnp.zeros((1, LANES), jnp.float32)
    small[...] = jnp.zeros(small.shape, jnp.float32)
    taps_square = jnp.zeros((1, LANES), jnp.float32)
    for c in range(chunks):
        column = slice(LANES * c, LANES * c + LANES)

        def backward(row, count, carry):
            sums, top = carry
            low, high = after[pl.ds(row, count), :], before[pl.ds(row, count), :]
            dy = dys[c, pl.ds(guard + row, count), :]
            masked = (dy * low, dy, dy * high)
            out = [
                sums[k] + fold(masked[k % 3] * pre[c, pl.ds(guard + row + starts[k], count), :])
                for k in range(9)
            ]
            back = column_sums(dys, c, row, count, -1)
            total = back[1] + high * back[0] + low * back[2]
            dpre_out[pl.ds(row, count), column] = total.astype(jnp.bfloat16)
            size = jnp.max(jnp.abs(total).reshape(-1, 8, LANES), axis=0)
            return tuple(out), jnp.maximum(top, size)

        zeros = tuple(jnp.zeros((8, LANES), jnp.float32) for _ in range(9))
        carry = lax.fori_loop(
            0,
            whole,
            lambda i, carry: backward(pl.multiple_of(i * STEP, STEP), STEP, carry),
            (zeros, biggest),
        )
        if left:
            carry = backward(whole * STEP, left, carry)
        sums, biggest = carry
        for k in range(9):
            value = jnp.sum(sums[k], axis=0, keepdims=True)
            taps_square = taps_square + value * value
            taps_biggest = jnp.maximum(taps_biggest, jnp.abs(value))
            small[k : k + 1, column] = value
    powers = (
        exponent(jnp.max(biggest) * (X_LIMIT * rows)),
        exponent(jnp.max(jnp.abs(gout[...]))),
        exponent(jnp.max(taps_biggest)),
    )
    for c in range(chunks):
        for i, power in enumerate(powers):
            small[9 + i : 10 + i, LANES * c : LANES * c + LANES] = power
    small[16:17, :LANES] = taps_square
    small[17:18, :] = jnp.sum(gout[...] * gout[...], axis=0, keepdims=True)
    if first.shape[0] == sizes.message:
        norm = message(sizes, scalars[3], x_vmem, dpre_out, gout, small, first, True)
        norm = norm + message(sizes, scalars[4], x_vmem, dpre_out, gout, small, early, True)
        small[18:19, :LANES] = norm
    save.wait()


def message(sizes, place, x, dpre, gout, small, out, scaled):
    depth, depth_out = sizes.depth, sizes.depth_out
    column = pl.multiple_of(place * depth, LANES)
    block = lax.dot_general(
        x[:, pl.ds(column, depth)], dpre[...], (((0,), (0,)), ((), ())), preferred_element_type=jnp.float32
    )
    hidden = block.shape[1]
    chunks = hidden // LANES
    norm = jnp.sum(block * block, axis=0, keepdims=True)
    norm = sum(norm[:, LANES * c : LANES * c + LANES] for c in range(chunks))
    factors = [jnp.exp2(small[9 + i : 10 + i, :]) if scaled else 1.0 for i in range(3)]
    out[:depth, :] = block * factors[0]
    out[depth:, :] = jnp.zeros((out.shape[0] - depth, hidden), jnp.float32)
    column = pl.multiple_of(place * depth_out, LANES)
    for start, group in sizes.groups:
        value = gout[start : start + group, pl.ds(column, depth_out)]
        lane = start // sizes.group * LANES
        factor = factors[1][:, :LANES] if scaled else 1.0
        out[depth : depth + group, lane : lane + LANES] = value * factor
    row = depth + sizes.group
    out[row : row + 9, :] = small[0:9, :] * factors[2]
    if scaled:
        out[row + 9 : row + 12, :] = small[9:12, :]
    return norm


class Sizes:
    def __init__(self, wide, hidden, classes, dp):
        self.classes = classes
        self.depth = wide // dp
        self.depth_out = hidden // dp
        self.chunks = hidden // LANES
        self.class_rows = (classes + 7) // 8 * 8
        self.group = (self.class_rows // self.chunks + 7) // 8 * 8
        self.groups = [
            (at, min(self.group, self.class_rows - at)) for at in range(0, self.class_rows, self.group)
        ]
        self.message = self.depth + self.group + 16
        self.staged = dp == 4 and self.depth % LANES == 0 and self.depth_out == LANES


def head_backward(sizes, widths, scalars, halves, onehot, weight_in, taps, weight_out, masks):
    rows = onehot.shape[0]
    wide, hidden = weight_in.shape
    chunks = hidden // LANES
    vmem = pl.BlockSpec(memory_space=pltpu.VMEM)
    anywhere = pl.BlockSpec(memory_space=pl.ANY)
    span = 2 * REACH * (PC + 1) + rows
    return pl.pallas_call(
        functools.partial(head_kernel, sizes, widths),
        out_shape=[
            jax.ShapeDtypeStruct((rows, wide), jnp.bfloat16),
            jax.ShapeDtypeStruct((rows, hidden), jnp.bfloat16),
            jax.ShapeDtypeStruct((256, hidden), jnp.float32),
            jax.ShapeDtypeStruct((24, hidden), jnp.float32),
        ]
        + [jax.ShapeDtypeStruct((sizes.message if sizes.staged else 8, hidden), jnp.float32)] * 2,
        in_specs=[pl.BlockSpec(memory_space=pltpu.SMEM)] + [anywhere] * len(halves) + [vmem] * 6,
        out_specs=[anywhere] + [vmem] * 5,
        scratch_shapes=[
            pltpu.VMEM((rows, wide), jnp.bfloat16),
            pltpu.VMEM((chunks, span, LANES), jnp.float32),
            pltpu.VMEM((chunks, span, LANES), jnp.float32),
            pltpu.VMEM((chunks, rows, LANES), jnp.float32),
            pltpu.VMEM((rows, hidden), jnp.bfloat16),
            pltpu.VMEM((rows, 256), jnp.bfloat16),
            pltpu.SemaphoreType.DMA((len(widths), 2)),
            pltpu.SemaphoreType.DMA,
        ],
        compiler_params=pltpu.CompilerParams(vmem_limit_bytes=24 * 1024 * 1024),
        name="head",
    )(scalars, *halves, weight_in, taps, weight_out, onehot, *masks)


def blocks_kernel(sizes, scalars, x, dpre, gout, small, late, own, stats):
    norm = message(sizes, scalars[5], x, dpre, gout, small, late, True)
    norm = norm + message(sizes, scalars[6], x, dpre, gout, small, own, False)
    stats[...] = jnp.zeros(stats.shape, jnp.float32)
    stats[0:1, :] = norm + small[18:19, :LANES]
    stats[1:2, :] = small[16:17, :LANES]
    for c in range(sizes.chunks):
        stats[2 + c : 3 + c, :] = small[17:18, LANES * c : LANES * c + LANES]


def sum_kernel(sizes, parts, last, stats, share_in, share_out, taps_out, line):
    depth, chunks = sizes.depth, sizes.chunks

    def fold(value):
        value = jnp.sum(value.reshape(-1, 8, value.shape[1]), axis=0)
        return sum(value[:, LANES * c : LANES * c + LANES] for c in range(value.shape[1] // LANES))

    mark = depth + sizes.group
    factors = [jnp.exp2(-last[mark + 9 + i : mark + 10 + i, :]) for i in range(3)]
    total = parts[:depth, :] + last[:depth, :] * factors[0]
    share_in[...] = total
    line[0:8, :] = fold(total * total)
    total = parts[depth:mark, :] + last[depth:mark, :] * factors[1]
    line[8:16, :] = fold(total * total)
    for start, group in sizes.groups:
        lane = start // sizes.group * LANES
        count = min(group, sizes.classes - start)
        share_out[start : start + count, 0, :] = total[:count, lane : lane + LANES]
    total = parts[mark : mark + 9, :] + last[mark : mark + 9, :] * factors[2]
    square = jnp.sum(total * total, axis=0, keepdims=True)
    for k in range(9):
        taps_out[k, :, :] = total[k : k + 1, :]
    line[16:24, :] = stats[...]
    line[24:32, :] = jnp.zeros((8, LANES), jnp.float32)
    line[24:25, :] = sum(square[:, LANES * c : LANES * c + LANES] for c in range(chunks))


def norm_kernel(chunks, line, total, out):
    values = [
        jnp.sum(total[16:17, :]),
        jnp.sum(total[17:18, :]),
        jnp.sum(total[18 : 18 + chunks, :]),
        jnp.sum(total[0:8, :]),
        jnp.sum(line[24:25, :]),
        jnp.sum(total[8:16, :]),
    ]
    row = lax.broadcasted_iota(jnp.int32, (8, LANES), 0)
    lane = lax.broadcasted_iota(jnp.int32, (8, LANES), 1)
    spread = jnp.zeros((8, LANES), jnp.float32)
    for i, value in enumerate(values):
        spread = jnp.where((row == i // 3) & (lane == i % 3), value, spread)
    out[...] = jnp.log(1e-12 + spread)[:2, :3]


def permute(value, pairs):
    return lax.ppermute(value, "dp", pairs)


def add_kernel(sizes, scalars, mine, theirs, out):
    depth, group = sizes.depth, sizes.group
    mark = depth + group
    end = (scalars[6] == 0) | (scalars[6] == 3)

    @pl.when(end)
    def _():
        out[...] = mine[...]

    @pl.when(jnp.logical_not(end))
    def _():
        for i, (start, stop) in enumerate(((0, depth), (depth, mark), (mark, mark + 9))):
            at = mark + 9 + i
            a, b = mine[at : at + 1, :], theirs[at : at + 1, :]
            common = jnp.minimum(a, b)
            out[start:stop, :] = mine[start:stop, :] * jnp.exp2(common - a) + theirs[
                start:stop, :
            ] * jnp.exp2(common - b)
            out[at : at + 1, :] = common
        out[mark + 12 :, :] = mine[mark + 12 :, :]


def by_row(sizes, shape, three):
    row = lax.broadcasted_iota(jnp.int32, shape, 0)
    return jnp.where(
        row < sizes.depth, three[0], jnp.where(row < sizes.depth + sizes.group, three[1], three[2])
    )


def staged_sums(sizes, me, scalars, xrows, dpre, gout, small, first, early):
    vmem = pl.BlockSpec(memory_space=pltpu.VMEM)
    smem = pl.BlockSpec(memory_space=pltpu.SMEM)
    hidden = dpre.shape[1]
    shape = (sizes.message, hidden)
    full = jax.ShapeDtypeStruct(shape, jnp.float32)
    lines = jax.ShapeDtypeStruct((8, LANES), jnp.float32)
    half = jnp.float16
    near = permute(first.astype(half), [(0, 1), (1, 0), (2, 3), (3, 2)])
    early = early.astype(half)
    middle = permute(early, [(1, 2), (2, 1)])
    skip = permute(early, [(0, 2), (3, 1)])
    late, own, stats = pl.pallas_call(
        functools.partial(blocks_kernel, sizes),
        out_shape=[full, full, lines],
        in_specs=[smem] + [vmem] * 4,
        out_specs=[vmem] * 3,
        compiler_params=pltpu.CompilerParams(vmem_limit_bytes=16 * 1024 * 1024),
        cost_estimate=pl.CostEstimate(
            flops=4 * sizes.depth * dpre.shape[0] * hidden,
            bytes_accessed=2 * xrows.size + 2 * dpre.size + 8 * sizes.message * hidden,
            transcendentals=0,
        ),
        name="blocks",
    )(scalars, xrows, dpre, gout, small)
    end = (me == 0) | (me == 3)
    mark = sizes.depth + sizes.group + 9
    both = pl.pallas_call(
        functools.partial(add_kernel, sizes),
        out_shape=full,
        in_specs=[smem, vmem, vmem],
        out_specs=vmem,
        compiler_params=pltpu.CompilerParams(vmem_limit_bytes=8 * 1024 * 1024),
        name="add",
    )(scalars, late, near.astype(jnp.float32))
    both = both.astype(half)
    near, skip, middle, _ = lax.optimization_barrier((near, skip, middle, both))
    far = permute(both, [(0, 1), (3, 2), (1, 3), (2, 0)])

    def split(value):
        return [value[mark + i : mark + i + 1] for i in range(3)]


    def decode(value):
        value = value.astype(jnp.float32)
        return value * by_row(sizes, shape, [jnp.exp2(-v) for v in split(value)])

    parts = own + decode(jnp.where(end, near, skip)) + decode(middle)
    return parts, far.astype(jnp.float32), stats


def per_device(sizes, dp, trials, features, owner, dilation_index, labels, input_weight, taps, output_weight):
    here, core, widths, halves = pieces(features[0, 0], "trial", trials, owner[0])
    me = lax.axis_index("dp")
    dil = dilation_index[0] + 1
    rows = features.shape[2]
    onehot = (labels[0][:, None] == jnp.arange(256, dtype=jnp.int32)[None, :]).astype(jnp.bfloat16)
    column = lax.broadcasted_iota(jnp.int32, (rows, LANES), 0) % PC
    before = (column < PC - dil).astype(jnp.float32)
    after = (column >= dil).astype(jnp.float32)
    classes, chunks = sizes.classes, sizes.chunks
    weight_out = jnp.pad(output_weight[0].T, ((0, 256 - classes), (0, 0)))
    high = me >= 2
    odd = me % 2
    end = (me == 0) | (me == 3)
    step, jump = jnp.where(odd == 0, 1, 2), jnp.where(high, me - 2, me + 2)
    to = [3 * (1 - odd), jnp.where(end, jump, step), jnp.where(end, step, jump), me]
    scalars = jnp.stack([dil, here, core] + to).astype(jnp.int32)
    xrows, dpre, gout, small, first, early = head_backward(
        sizes,
        widths,
        scalars,
        halves,
        onehot,
        input_weight[0],
        taps[0][:, None, :],
        weight_out,
        (after, before),
    )
    if not sizes.staged:
        return general_sums(sizes, xrows, dpre, gout, small)
    parts, last, stats = staged_sums(sizes, me, scalars, xrows, dpre, gout, small, first, early)
    vmem = pl.BlockSpec(memory_space=pltpu.VMEM)
    hidden = dpre.shape[1]
    share_in, share_out, total_taps, line = pl.pallas_call(
        functools.partial(sum_kernel, sizes),
        out_shape=[
            jax.ShapeDtypeStruct((sizes.depth, hidden), jnp.float32),
            jax.ShapeDtypeStruct((classes, 1, sizes.depth_out), jnp.float32),
            jax.ShapeDtypeStruct((9, 1, hidden), jnp.float32),
            jax.ShapeDtypeStruct((32, LANES), jnp.float32),
        ],
        in_specs=[vmem] * 3,
        out_specs=[vmem] * 4,
        compiler_params=pltpu.CompilerParams(vmem_limit_bytes=8 * 1024 * 1024),
        name="sums",
    )(parts, last, stats)
    total = line
    for step in (1, 2):
        total = total + permute(total, [(i, i ^ step) for i in range(dp)])
    norms = pl.pallas_call(
        functools.partial(norm_kernel, chunks),
        out_shape=jax.ShapeDtypeStruct((2, 3), jnp.float32),
        in_specs=[vmem] * 2,
        out_specs=vmem,
        compiler_params=pltpu.CompilerParams(vmem_limit_bytes=4 * 1024 * 1024),
        name="norms",
    )(line, total)
    share_out = jnp.transpose(share_out, (1, 2, 0))
    return (share_in[None], jnp.transpose(total_taps, (1, 0, 2)), share_out, norms[None])


def general_sums(sizes, xrows, dpre, gout, small):
    g_in = jnp.dot(xrows.T, dpre, preferred_element_type=jnp.float32)
    g_out = gout[: sizes.classes].T
    g_taps = small[:9]
    share_in = lax.psum_scatter(g_in, "dp", scatter_dimension=0, tiled=True)
    share_out = lax.psum_scatter(g_out, "dp", scatter_dimension=0, tiled=True)
    local = jnp.stack([jnp.sum(g_in * g_in), jnp.sum(g_taps * g_taps), jnp.sum(g_out * g_out)])
    share_sq = jnp.stack([jnp.sum(share_in * share_in), jnp.sum(share_out * share_out)])
    total_taps, squares, share_total = lax.psum((g_taps, local, share_sq), "dp")
    totals = jnp.stack([share_total[0], jnp.sum(total_taps * total_taps), share_total[1]])
    norms = jnp.log(1e-12 + jnp.stack([squares, totals]))
    return (share_in[None], total_taps[None], share_out[None], norms[None])


def solution(mesh):
    dp, trials = mesh.shape["dp"], mesh.shape["trial"]
    placed = (
        P(("groups", "dp"), "trial", None, None),
        P(("groups", "dp")),
        P("trial"),
        P(("groups", "dp"), None),
        P("trial", None, None),
        P("trial", None, None),
        P("trial", None, None),
    )

    def step(*args):
        (wide, hidden), classes = args[4].shape[1:], args[6].shape[2]
        return per_device(Sizes(wide, hidden, classes, dp), dp, trials, *args)

    return jax.shard_map(
        step,
        mesh=mesh,
        in_specs=placed,
        out_specs=(
            P(("groups", "trial"), "dp", None),
            P(("groups", "trial"), None, None),
            P(("groups", "trial"), "dp", None),
            P(("groups", "trial"), None, None),
        ),
        check_vma=False,
    )
```

```python
import functools
import math

import jax
import jax.numpy as jnp
from jax import lax
from jax.experimental import pallas as pl
from jax.experimental.pallas import tpu as pltpu
from jax.sharding import PartitionSpec as P

PC = 37
LANES = 128
FORWARD_STEP = 64
BACKWARD_STEP = 64
REACH = 4
OFFSETS = [(a, b) for a in (-1, 0, 1) for b in (-1, 0, 1)]
X_LIMIT = 6.0
ROOM = 16384.0


def pieces(block, axis, size, source):
    width = block.shape[1] // 2
    if size != 4:
        block = jnp.where(lax.axis_index(axis) == source, block, jnp.zeros_like(block))
        block = lax.psum(block, axis)
        low, high = block[:, :width], block[:, width:]
        zero = jnp.int32(0)
        return zero + 1, zero, (width,), (low, low, high, high)
    me = lax.axis_index(axis)
    core = me % 2
    mate = [(0, 1), (1, 0), (2, 3), (3, 2)]
    across = [(0, 2), (2, 0), (1, 3), (3, 1)]
    here = ((source // 2) == (me // 2)).astype(jnp.int32)
    widths = split_width(width)
    got = lax.ppermute(jnp.where(core == 0, block[:, width:], block[:, :width]), axis, mate)
    values = []
    at = 0
    for piece in widths:
        low, high = block[:, at : at + piece], block[:, width + at : width + at + piece]
        kept = jnp.where(core == 0, low, high)
        held = jnp.where(source % 2 == core, kept, got[:, at : at + piece])
        other = lax.ppermute(held, axis, across)
        values += [held, other, lax.ppermute(held, axis, mate), lax.ppermute(other, axis, mate)]
        at += piece
    return here, core, widths, tuple(values)


def split_width(width):
    tiles = width // LANES
    last = max(tiles // 3, 1)
    return tuple(LANES * n for n in (tiles - last, last) if n > 0)


def gelu_parts(value):
    square = value * value
    half = 0.5 + 0.5 * jnp.tanh(value * (0.7978845608 + (0.7978845608 * 0.044715) * square))
    out_val = value * half
    rate = 2.0 * 0.7978845608 + (6.0 * 0.7978845608 * 0.044715) * square
    return (out_val, half + out_val * (1.0 - half) * rate)


def exponent(size):
    size = jnp.maximum(jnp.full((1, LANES), size, jnp.float32), 1e-30)
    return jnp.clip(jnp.floor(jnp.log(ROOM / size) * (1.0 / math.log(2.0))), -100.0, 100.0)


def head_kernel(
    sizes,
    widths,
    scalars,
    *refs,
):
    halves, refs = refs[: 4 * len(widths)], refs[4 * len(widths) :]
    weight_in, taps, weight_out, onehot, after, before = refs[:6]
    x_vmem, dpre_out, gout, small, first, early = refs[6:12]
    pre, dys, slope, hid, dlog, sem_in = refs[12:]
    rows = x_vmem.shape[0]
    width = x_vmem.shape[1] // 2
    hidden = weight_in.shape[1]
    chunks = hidden // LANES
    guard = REACH * (PC + 1)
    dil, here, core = scalars[0], scalars[1], scalars[2]

    def fetch(kind, index):
        column = (core if kind < 2 else 1 - core) * width + sum(widths[:index])
        target = x_vmem.at[:, pl.ds(pl.multiple_of(column, LANES), widths[index])]
        return pltpu.make_async_copy(halves[4 * index + kind], target, sem_in.at[index, kind // 2])

    for away in (0, 1):

        @pl.when(here == 1 - away)
        def _(away=away):
            for index in range(len(widths)):
                fetch(away, index).start()
                fetch(2 + away, index).start()

    for c in range(chunks):
        for ref in (pre, dys):
            ref[c, :guard, :] = jnp.zeros((guard, LANES), jnp.float32)
            ref[c, guard + rows :, :] = jnp.zeros((guard, LANES), jnp.float32)
    for index in range(len(widths)):
        fetch(0, index).wait()
        fetch(2, index).wait()

    for n in range(hidden // 256):
        value = jnp.dot(
            x_vmem[...], weight_in[:, 256 * n : 256 * n + 256], preferred_element_type=jnp.float32
        )
        for h in range(2):
            pre[2 * n + h, guard : guard + rows, :] = value[:, LANES * h : LANES * h + LANES]

    starts = [dil * (PC * a + b) for a, b in OFFSETS]

    def column_sums(source, c, row, count, sign):
        column = slice(LANES * c, LANES * c + LANES)
        sums = []
        for b in range(3):
            total = None
            for k in (b, 3 + b, 6 + b):
                at = guard + row + sign * starts[k]
                term = source[c, pl.ds(at, count), :] * taps[k, :, column]
                total = term if total is None else total + term
            sums.append(total)
        return sums

    def forward(row, count):
        low, high = after[pl.ds(row, count), :], before[pl.ds(row, count), :]
        for c in range(chunks):
            sums = column_sums(pre, c, row, count, 1)
            act, grad = gelu_parts(sums[1] + low * sums[0] + high * sums[2])
            slope[c, pl.ds(row, count), :] = grad
            hid[pl.ds(row, count), LANES * c : LANES * c + LANES] = act.astype(jnp.bfloat16)

    def run(step, body):
        whole = rows // step

        @pl.loop(0, whole)
        def _(i):
            body(pl.multiple_of(i * step, step), step)

        if rows > whole * step:
            body(whole * step, rows - whole * step)

    run(FORWARD_STEP, forward)

    logits = lax.dot_general(
        hid[...], weight_out[...], (((1,), (1,)), ((), ())), preferred_element_type=jnp.float32
    )
    lane = lax.broadcasted_iota(jnp.int32, logits.shape, 1)
    logits = jnp.where(lane < sizes.classes, logits, -1e30)
    peak = jnp.max(logits, axis=1, keepdims=True)
    power = jnp.exp(logits - peak)
    prob = power / jnp.sum(power, axis=1, keepdims=True)
    dlog[...] = (prob - onehot[...].astype(jnp.float32)).astype(jnp.bfloat16)

    gout[...] = lax.dot_general(
        dlog[...], hid[...], (((0,), (0,)), ((), ())), preferred_element_type=jnp.float32
    )
    for n in range(hidden // 256):
        value = jnp.dot(
            dlog[...], weight_out[:, 256 * n : 256 * n + 256], preferred_element_type=jnp.float32
        )
        for h in range(2):
            c = 2 * n + h
            dys[c, guard : guard + rows, :] = value[:, LANES * h : LANES * h + LANES] * slope[c]

    def fold(value):
        return jnp.sum(value.reshape(-1, 8, LANES), axis=0)

    biggest = jnp.zeros((8, LANES), jnp.float32)
    taps_biggest = jnp.zeros((1, LANES), jnp.float32)
    small[...] = jnp.zeros(small.shape, jnp.float32)
    taps_square = jnp.zeros((1, LANES), jnp.float32)
    for c in range(chunks):
        column = slice(LANES * c, LANES * c + LANES)

        def backward(row, count, carry):
            sums, top = carry
            low, high = after[pl.ds(row, count), :], before[pl.ds(row, count), :]
            dy = dys[c, pl.ds(guard + row, count), :]
            masked = (dy * low, dy, dy * high)
            out = [
                sums[k] + fold(masked[k % 3] * pre[c, pl.ds(guard + row + starts[k], count), :])
                for k in range(9)
            ]
            back = column_sums(dys, c, row, count, -1)
            total = back[1] + high * back[0] + low * back[2]
            dpre_out[pl.ds(row, count), column] = total.astype(jnp.bfloat16)
            size = jnp.max(jnp.abs(total).reshape(-1, 8, LANES), axis=0)
            return tuple(out), jnp.maximum(top, size)

        zeros = tuple(jnp.zeros((8, LANES), jnp.float32) for _ in range(9))
        step = BACKWARD_STEP
        whole = rows // step
        carry = lax.fori_loop(
            0,
            whole,
            lambda i, carry, step=step: backward(pl.multiple_of(i * step, step), step, carry),
            (zeros, biggest),
        )
        if rows > whole * step:
            carry = backward(whole * step, rows - whole * step, carry)
        sums, biggest = carry
        for k in range(9):
            value = jnp.sum(sums[k], axis=0, keepdims=True)
            taps_square = taps_square + value * value
            taps_biggest = jnp.maximum(taps_biggest, jnp.abs(value))
            small[k : k + 1, column] = value
    powers = (
        exponent(jnp.max(biggest) * (X_LIMIT * rows)),
        exponent(jnp.max(jnp.abs(gout[...]))),
        exponent(jnp.max(taps_biggest)),
    )
    for c in range(chunks):
        for i, power in enumerate(powers):
            small[9 + i : 10 + i, LANES * c : LANES * c + LANES] = power
    small[16:17, :LANES] = taps_square
    small[17:18, :] = jnp.sum(gout[...] * gout[...], axis=0, keepdims=True)
    if first.shape[0] == sizes.message:
        norm = message(sizes, scalars[3], x_vmem, dpre_out, gout, small, first, True)
        norm = norm + message(sizes, scalars[4], x_vmem, dpre_out, gout, small, early, True)
        small[18:19, :LANES] = norm


def message(sizes, place, x, dpre, gout, small, out, scaled):
    depth, depth_out = sizes.depth, sizes.depth_out
    column = pl.multiple_of(place * depth, LANES)
    block = lax.dot_general(
        x[:, pl.ds(column, depth)], dpre[...], (((0,), (0,)), ((), ())), preferred_element_type=jnp.float32
    )
    hidden = block.shape[1]
    chunks = hidden // LANES
    norm = jnp.sum(block * block, axis=0, keepdims=True)
    norm = sum(norm[:, LANES * c : LANES * c + LANES] for c in range(chunks))
    factors = [jnp.exp2(small[9 + i : 10 + i, :]) if scaled else 1.0 for i in range(3)]
    out[:depth, :] = block * factors[0]
    out[depth:, :] = jnp.zeros((out.shape[0] - depth, hidden), jnp.float32)
    column = pl.multiple_of(place * depth_out, LANES)
    for start, group in sizes.groups:
        value = gout[start : start + group, pl.ds(column, depth_out)]
        lane = start // sizes.group * LANES
        factor = factors[1][:, :LANES] if scaled else 1.0
        out[depth : depth + group, lane : lane + LANES] = value * factor
    row = depth + sizes.group
    out[row : row + 9, :] = small[0:9, :] * factors[2]
    if scaled:
        out[row + 9 : row + 12, :] = small[9:12, :]
    return norm


class Sizes:
    def __init__(self, wide, hidden, classes, dp):
        self.classes = classes
        self.depth = wide // dp
        self.depth_out = hidden // dp
        self.chunks = hidden // LANES
        self.class_rows = (classes + 7) // 8 * 8
        self.group = (self.class_rows // self.chunks + 7) // 8 * 8
        self.groups = [
            (at, min(self.group, self.class_rows - at)) for at in range(0, self.class_rows, self.group)
        ]
        self.message = self.depth + self.group + 16
        self.staged = dp == 4 and self.depth % LANES == 0 and self.depth_out == LANES


def head_backward(sizes, widths, scalars, halves, onehot, weight_in, taps, weight_out, masks):
    rows = onehot.shape[0]
    wide, hidden = weight_in.shape
    chunks = hidden // LANES
    vmem = pl.BlockSpec(memory_space=pltpu.VMEM)
    anywhere = pl.BlockSpec(memory_space=pl.ANY)
    span = 2 * REACH * (PC + 1) + rows
    return pl.pallas_call(
        functools.partial(head_kernel, sizes, widths),
        out_shape=[
            jax.ShapeDtypeStruct((rows, wide), jnp.bfloat16),
            jax.ShapeDtypeStruct((rows, hidden), jnp.bfloat16),
            jax.ShapeDtypeStruct((256, hidden), jnp.float32),
            jax.ShapeDtypeStruct((24, hidden), jnp.float32),
        ]
        + [jax.ShapeDtypeStruct((sizes.message if sizes.staged else 8, hidden), jnp.float32)] * 2,
        in_specs=[pl.BlockSpec(memory_space=pltpu.SMEM)] + [anywhere] * len(halves) + [vmem] * 6,
        out_specs=[vmem] * 6,
        scratch_shapes=[
            pltpu.VMEM((chunks, span, LANES), jnp.float32),
            pltpu.VMEM((chunks, span, LANES), jnp.float32),
            pltpu.VMEM((chunks, rows, LANES), jnp.float32),
            pltpu.VMEM((rows, hidden), jnp.bfloat16),
            pltpu.VMEM((rows, 256), jnp.bfloat16),
            pltpu.SemaphoreType.DMA((len(widths), 2)),
        ],
        compiler_params=pltpu.CompilerParams(vmem_limit_bytes=24 * 1024 * 1024),
        name="head",
    )(scalars, *halves, weight_in, taps, weight_out, onehot, *masks)


def blocks_kernel(sizes, scalars, x, dpre, gout, small, late, own, stats):
    norm = message(sizes, scalars[5], x, dpre, gout, small, late, True)
    norm = norm + message(sizes, scalars[6], x, dpre, gout, small, own, False)
    stats[...] = jnp.zeros(stats.shape, jnp.float32)
    stats[0:1, :] = norm + small[18:19, :LANES]
    stats[1:2, :] = small[16:17, :LANES]
    for c in range(sizes.chunks):
        stats[2 + c : 3 + c, :] = small[17:18, LANES * c : LANES * c + LANES]


def totals(sizes, parts, last):
    mark = sizes.depth + sizes.group
    spans = ((0, sizes.depth), (sizes.depth, mark), (mark, mark + 9))
    return [
        parts[start:stop, :] + last[start:stop, :] * jnp.exp2(-last[mark + 9 + i : mark + 10 + i, :])
        for i, (start, stop) in enumerate(spans)
    ]


def line_kernel(sizes, parts, last, stats, line):
    def fold(value):
        value = jnp.sum(value.reshape(-1, 8, value.shape[1]), axis=0)
        return sum(value[:, LANES * c : LANES * c + LANES] for c in range(sizes.chunks))

    sum_in, sum_out, sum_taps = totals(sizes, parts, last)
    line[0:8, :] = fold(sum_in * sum_in)
    line[8:16, :] = fold(sum_out * sum_out)
    line[16:24, :] = stats[...]
    line[24:32, :] = jnp.zeros((8, LANES), jnp.float32)
    square = jnp.sum(sum_taps * sum_taps, axis=0, keepdims=True)
    line[24:25, :] = sum(square[:, LANES * c : LANES * c + LANES] for c in range(sizes.chunks))


def sum_kernel(sizes, parts, last, share_in, share_out, taps_out):
    sum_in, sum_out, sum_taps = totals(sizes, parts, last)
    share_in[...] = sum_in
    for start, group in sizes.groups:
        lane = start // sizes.group * LANES
        count = min(group, sizes.classes - start)
        share_out[start : start + count, 0, :] = sum_out[:count, lane : lane + LANES]
    for k in range(9):
        taps_out[k, :, :] = sum_taps[k : k + 1, :]


def norm_kernel(chunks, *refs):
    lines, out = refs[:-1], refs[-1]
    total = sum(line[...] for line in lines)
    line = lines[0]
    values = [
        jnp.sum(total[16:17, :]),
        jnp.sum(total[17:18, :]),
        jnp.sum(total[18 : 18 + chunks, :]),
        jnp.sum(total[0:8, :]),
        jnp.sum(line[24:25, :]),
        jnp.sum(total[8:16, :]),
    ]
    row = lax.broadcasted_iota(jnp.int32, (8, LANES), 0)
    lane = lax.broadcasted_iota(jnp.int32, (8, LANES), 1)
    spread = jnp.zeros((8, LANES), jnp.float32)
    for i, value in enumerate(values):
        spread = jnp.where((row == i // 3) & (lane == i % 3), value, spread)
    out[...] = jnp.log(1e-12 + spread)[:2, :3]


def permute(value, pairs):
    return lax.ppermute(value, "dp", pairs)


def add_kernel(sizes, scalars, mine, theirs, out):
    depth, group = sizes.depth, sizes.group
    mark = depth + group
    end = (scalars[6] == 0) | (scalars[6] == 3)

    @pl.when(end)
    def _():
        out[...] = mine[...]

    @pl.when(jnp.logical_not(end))
    def _():
        for i, (start, stop) in enumerate(((0, depth), (depth, mark), (mark, mark + 9))):
            at = mark + 9 + i
            a, b = mine[at : at + 1, :], theirs[at : at + 1, :]
            common = jnp.minimum(a, b)
            out[start:stop, :] = mine[start:stop, :] * jnp.exp2(common - a) + theirs[
                start:stop, :
            ] * jnp.exp2(common - b)
            out[at : at + 1, :] = common
        out[mark + 12 :, :] = mine[mark + 12 :, :]


def by_row(sizes, shape, three):
    row = lax.broadcasted_iota(jnp.int32, shape, 0)
    return jnp.where(
        row < sizes.depth, three[0], jnp.where(row < sizes.depth + sizes.group, three[1], three[2])
    )


def staged_sums(sizes, me, scalars, xrows, dpre, gout, small, first, early):
    vmem = pl.BlockSpec(memory_space=pltpu.VMEM)
    smem = pl.BlockSpec(memory_space=pltpu.SMEM)
    hidden = dpre.shape[1]
    shape = (sizes.message, hidden)
    full = jax.ShapeDtypeStruct(shape, jnp.float32)
    lines = jax.ShapeDtypeStruct((8, LANES), jnp.float32)
    half = jnp.float16
    near = permute(first.astype(half), [(0, 1), (1, 0), (2, 3), (3, 2)])
    early = early.astype(half)
    middle = permute(early, [(1, 2), (2, 1)])
    skip = permute(early, [(0, 2), (3, 1)])
    late, own, stats = pl.pallas_call(
        functools.partial(blocks_kernel, sizes),
        out_shape=[full, full, lines],
        in_specs=[smem] + [vmem] * 4,
        out_specs=[vmem] * 3,
        compiler_params=pltpu.CompilerParams(vmem_limit_bytes=16 * 1024 * 1024),
        cost_estimate=pl.CostEstimate(
            flops=4 * sizes.depth * dpre.shape[0] * hidden,
            bytes_accessed=2 * xrows.size + 2 * dpre.size + 8 * sizes.message * hidden,
            transcendentals=0,
        ),
        name="blocks",
    )(scalars, xrows, dpre, gout, small)
    end = (me == 0) | (me == 3)
    mark = sizes.depth + sizes.group + 9
    both = pl.pallas_call(
        functools.partial(add_kernel, sizes),
        out_shape=full,
        in_specs=[smem, vmem, vmem],
        out_specs=vmem,
        compiler_params=pltpu.CompilerParams(vmem_limit_bytes=8 * 1024 * 1024),
        name="add",
    )(scalars, late, near.astype(jnp.float32))
    both = both.astype(half)
    near, skip, middle, _ = lax.optimization_barrier((near, skip, middle, both))
    far = permute(both, [(0, 1), (3, 2), (1, 3), (2, 0)])

    def split(value):
        return [value[mark + i : mark + i + 1] for i in range(3)]


    def decode(value):
        value = value.astype(jnp.float32)
        return value * by_row(sizes, shape, [jnp.exp2(-v) for v in split(value)])

    parts = own + decode(jnp.where(end, near, skip)) + decode(middle)
    return parts, far.astype(jnp.float32), stats


def per_device(sizes, dp, trials, features, owner, dilation_index, labels, input_weight, taps, output_weight):
    here, core, widths, halves = pieces(features[0, 0], "trial", trials, owner[0])
    me = lax.axis_index("dp")
    dil = dilation_index[0] + 1
    rows = features.shape[2]
    onehot = (labels[0][:, None] == jnp.arange(256, dtype=jnp.int32)[None, :]).astype(jnp.bfloat16)
    column = lax.broadcasted_iota(jnp.int32, (rows, LANES), 0) % PC
    before = (column < PC - dil).astype(jnp.float32)
    after = (column >= dil).astype(jnp.float32)
    classes, chunks = sizes.classes, sizes.chunks
    weight_out = jnp.pad(output_weight[0].T, ((0, 256 - classes), (0, 0)))
    high = me >= 2
    odd = me % 2
    end = (me == 0) | (me == 3)
    step, jump = jnp.where(odd == 0, 1, 2), jnp.where(high, me - 2, me + 2)
    to = [3 * (1 - odd), jnp.where(end, jump, step), jnp.where(end, step, jump), me]
    scalars = jnp.stack([dil, here, core] + to).astype(jnp.int32)
    xrows, dpre, gout, small, first, early = head_backward(
        sizes,
        widths,
        scalars,
        halves,
        onehot,
        input_weight[0],
        taps[0][:, None, :],
        weight_out,
        (after, before),
    )
    if not sizes.staged:
        return general_sums(sizes, xrows, dpre, gout, small)
    parts, last, stats = staged_sums(sizes, me, scalars, xrows, dpre, gout, small, first, early)
    vmem = pl.BlockSpec(memory_space=pltpu.VMEM)
    hidden = dpre.shape[1]
    small = pltpu.CompilerParams(vmem_limit_bytes=8 * 1024 * 1024)
    line = pl.pallas_call(
        functools.partial(line_kernel, sizes),
        out_shape=jax.ShapeDtypeStruct((32, LANES), jnp.float32),
        in_specs=[vmem] * 3,
        out_specs=vmem,
        compiler_params=small,
        name="line",
    )(parts, last, stats)
    lines = [line] + [permute(line, [(i, i ^ s) for i in range(dp)]) for s in range(1, dp)]
    share_in, share_out, total_taps = pl.pallas_call(
        functools.partial(sum_kernel, sizes),
        out_shape=[
            jax.ShapeDtypeStruct((sizes.depth, hidden), jnp.float32),
            jax.ShapeDtypeStruct((classes, 1, sizes.depth_out), jnp.float32),
            jax.ShapeDtypeStruct((9, 1, hidden), jnp.float32),
        ],
        in_specs=[vmem] * 2,
        out_specs=[vmem] * 3,
        compiler_params=small,
        cost_estimate=pl.CostEstimate(
            flops=2 * parts.size, bytes_accessed=16 * parts.size, transcendentals=0
        ),
        name="sums",
    )(parts, last)
    norms = pl.pallas_call(
        functools.partial(norm_kernel, chunks),
        out_shape=jax.ShapeDtypeStruct((2, 3), jnp.float32),
        in_specs=[vmem] * dp,
        out_specs=vmem,
        compiler_params=pltpu.CompilerParams(vmem_limit_bytes=4 * 1024 * 1024),
        name="norms",
    )(*lines)
    share_out = jnp.transpose(share_out, (1, 2, 0))
    return (share_in[None], jnp.transpose(total_taps, (1, 0, 2)), share_out, norms[None])


def general_sums(sizes, xrows, dpre, gout, small):
    g_in = jnp.dot(xrows.T, dpre, preferred_element_type=jnp.float32)
    g_out = gout[: sizes.classes].T
    g_taps = small[:9]
    share_in = lax.psum_scatter(g_in, "dp", scatter_dimension=0, tiled=True)
    share_out = lax.psum_scatter(g_out, "dp", scatter_dimension=0, tiled=True)
    local = jnp.stack([jnp.sum(g_in * g_in), jnp.sum(g_taps * g_taps), jnp.sum(g_out * g_out)])
    share_sq = jnp.stack([jnp.sum(share_in * share_in), jnp.sum(share_out * share_out)])
    total_taps, squares, share_total = lax.psum((g_taps, local, share_sq), "dp")
    totals = jnp.stack([share_total[0], jnp.sum(total_taps * total_taps), share_total[1]])
    norms = jnp.log(1e-12 + jnp.stack([squares, totals]))
    return (share_in[None], total_taps[None], share_out[None], norms[None])


def solution(mesh):
    dp, trials = mesh.shape["dp"], mesh.shape["trial"]
    placed = (
        P(("groups", "dp"), "trial", None, None),
        P(("groups", "dp")),
        P("trial"),
        P(("groups", "dp"), None),
        P("trial", None, None),
        P("trial", None, None),
        P("trial", None, None),
    )

    def step(*args):
        (wide, hidden), classes = args[4].shape[1:], args[6].shape[2]
        return per_device(Sizes(wide, hidden, classes, dp), dp, trials, *args)

    return jax.shard_map(
        step,
        mesh=mesh,
        in_specs=placed,
        out_specs=(
            P(("groups", "trial"), "dp", None),
            P(("groups", "trial"), None, None),
            P(("groups", "trial"), "dp", None),
            P(("groups", "trial"), None, None),
        ),
        check_vma=False,
    )
```

```python
import functools
import math

import jax
import jax.numpy as jnp
from jax import lax
from jax.experimental import pallas as pl
from jax.experimental.pallas import tpu as pltpu
from jax.sharding import PartitionSpec as P

PC = 37
LANES = 128
FORWARD_STEP = 64
BACKWARD_STEP = 64
REACH = 4
OFFSETS = [(a, b) for a in (-1, 0, 1) for b in (-1, 0, 1)]
X_LIMIT = 6.0
ROOM = 16384.0


def pieces(block, axis, size, source):
    width = block.shape[1] // 2
    if size != 4:
        block = jnp.where(lax.axis_index(axis) == source, block, jnp.zeros_like(block))
        block = lax.psum(block, axis)
        low, high = block[:, :width], block[:, width:]
        zero = jnp.int32(0)
        return zero + 1, zero, (width,), (low, low, high, high)
    me = lax.axis_index(axis)
    core = me % 2
    mate = [(0, 1), (1, 0), (2, 3), (3, 2)]
    across = [(0, 2), (2, 0), (1, 3), (3, 1)]
    here = ((source // 2) == (me // 2)).astype(jnp.int32)
    widths = split_width(width)
    got = lax.ppermute(jnp.where(core == 0, block[:, width:], block[:, :width]), axis, mate)
    values = []
    at = 0
    for piece in widths:
        low, high = block[:, at : at + piece], block[:, width + at : width + at + piece]
        kept = jnp.where(core == 0, low, high)
        held = jnp.where(source % 2 == core, kept, got[:, at : at + piece])
        other = lax.ppermute(held, axis, across)
        values += [held, other, lax.ppermute(held, axis, mate), lax.ppermute(other, axis, mate)]
        at += piece
    return here, core, widths, tuple(values)


def split_width(width):
    tiles = width // LANES
    last = max(tiles // 3, 1)
    return tuple(LANES * n for n in (tiles - last, last) if n > 0)


def gelu_parts(value):
    square = value * value
    half = 0.5 + 0.5 * jnp.tanh(value * (0.7978845608 + (0.7978845608 * 0.044715) * square))
    out_val = value * half
    rate = 2.0 * 0.7978845608 + (6.0 * 0.7978845608 * 0.044715) * square
    return (out_val, half + out_val * (1.0 - half) * rate)


def exponent(size):
    size = jnp.maximum(jnp.full((1, LANES), size, jnp.float32), 1e-30)
    return jnp.clip(jnp.floor(jnp.log(ROOM / size) * (1.0 / math.log(2.0))), -100.0, 100.0)


def head_kernel(
    sizes,
    widths,
    scalars,
    *refs,
):
    halves, refs = refs[: 4 * len(widths)], refs[4 * len(widths) :]
    weight_in, taps, weight_out, onehot, after, before = refs[:6]
    x_vmem, dpre_out, gout, small, first, early = refs[6:12]
    pre, dys, slope, hid, dlog, sem_in = refs[12:]
    rows = x_vmem.shape[0]
    width = x_vmem.shape[1] // 2
    hidden = weight_in.shape[1]
    chunks = hidden // LANES
    guard = REACH * (PC + 1)
    dil, here, core = scalars[0], scalars[1], scalars[2]

    def fetch(kind, index):
        column = (core if kind < 2 else 1 - core) * width + sum(widths[:index])
        target = x_vmem.at[:, pl.ds(pl.multiple_of(column, LANES), widths[index])]
        return pltpu.make_async_copy(halves[4 * index + kind], target, sem_in.at[index, kind // 2])

    for away in (0, 1):

        @pl.when(here == 1 - away)
        def _(away=away):
            for index in range(len(widths)):
                fetch(away, index).start()
                fetch(2 + away, index).start()

    for c in range(chunks):
        for ref in (pre, dys):
            ref[c, :guard, :] = jnp.zeros((guard, LANES), jnp.float32)
            ref[c, guard + rows :, :] = jnp.zeros((guard, LANES), jnp.float32)
    for index in range(len(widths)):
        fetch(0, index).wait()
        fetch(2, index).wait()

    for n in range(hidden // 256):
        value = jnp.dot(
            x_vmem[...], weight_in[:, 256 * n : 256 * n + 256], preferred_element_type=jnp.float32
        )
        for h in range(2):
            pre[2 * n + h, guard : guard + rows, :] = value[:, LANES * h : LANES * h + LANES]

    starts = [dil * (PC * a + b) for a, b in OFFSETS]

    def column_sums(source, c, row, count, sign):
        column = slice(LANES * c, LANES * c + LANES)
        sums = []
        for b in range(3):
            total = None
            for k in (b, 3 + b, 6 + b):
                at = guard + row + sign * starts[k]
                term = source[c, pl.ds(at, count), :] * taps[k, :, column]
                total = term if total is None else total + term
            sums.append(total)
        return sums

    def forward(row, count):
        low, high = after[pl.ds(row, count), :], before[pl.ds(row, count), :]
        for c in range(chunks):
            sums = column_sums(pre, c, row, count, 1)
            act, grad = gelu_parts(sums[1] + low * sums[0] + high * sums[2])
            slope[c, pl.ds(row, count), :] = grad
            hid[pl.ds(row, count), LANES * c : LANES * c + LANES] = act.astype(jnp.bfloat16)

    def run(step, body):
        whole = rows // step

        @pl.loop(0, whole)
        def _(i):
            body(pl.multiple_of(i * step, step), step)

        if rows > whole * step:
            body(whole * step, rows - whole * step)

    run(FORWARD_STEP, forward)

    logits = lax.dot_general(
        hid[...], weight_out[...], (((1,), (1,)), ((), ())), preferred_element_type=jnp.float32
    )
    lane = lax.broadcasted_iota(jnp.int32, logits.shape, 1)
    logits = jnp.where(lane < sizes.classes, logits, -1e30)
    peak = jnp.max(logits, axis=1, keepdims=True)
    power = jnp.exp(logits - peak)
    prob = power / jnp.sum(power, axis=1, keepdims=True)
    dlog[...] = (prob - onehot[...].astype(jnp.float32)).astype(jnp.bfloat16)

    gout[...] = lax.dot_general(
        dlog[...], hid[...], (((0,), (0,)), ((), ())), preferred_element_type=jnp.float32
    )
    for n in range(hidden // 256):
        value = jnp.dot(
            dlog[...], weight_out[:, 256 * n : 256 * n + 256], preferred_element_type=jnp.float32
        )
        for h in range(2):
            c = 2 * n + h
            dys[c, guard : guard + rows, :] = value[:, LANES * h : LANES * h + LANES] * slope[c]

    def fold(value):
        return jnp.sum(value.reshape(-1, 8, LANES), axis=0)

    biggest = jnp.zeros((8, LANES), jnp.float32)
    taps_biggest = jnp.zeros((1, LANES), jnp.float32)
    small[...] = jnp.zeros(small.shape, jnp.float32)
    taps_square = jnp.zeros((1, LANES), jnp.float32)
    for c in range(chunks):
        column = slice(LANES * c, LANES * c + LANES)

        def backward(row, count, carry):
            sums, top = carry
            low, high = after[pl.ds(row, count), :], before[pl.ds(row, count), :]
            dy = dys[c, pl.ds(guard + row, count), :]
            masked = (dy * low, dy, dy * high)
            out = [
                sums[k] + fold(masked[k % 3] * pre[c, pl.ds(guard + row + starts[k], count), :])
                for k in range(9)
            ]
            back = column_sums(dys, c, row, count, -1)
            total = back[1] + high * back[0] + low * back[2]
            dpre_out[pl.ds(row, count), column] = total.astype(jnp.bfloat16)
            size = jnp.max(jnp.abs(total).reshape(-1, 8, LANES), axis=0)
            return tuple(out), jnp.maximum(top, size)

        zeros = tuple(jnp.zeros((8, LANES), jnp.float32) for _ in range(9))
        step = BACKWARD_STEP
        whole = rows // step
        carry = lax.fori_loop(
            0,
            whole,
            lambda i, carry, step=step: backward(pl.multiple_of(i * step, step), step, carry),
            (zeros, biggest),
        )
        if rows > whole * step:
            carry = backward(whole * step, rows - whole * step, carry)
        sums, biggest = carry
        for k in range(9):
            value = jnp.sum(sums[k], axis=0, keepdims=True)
            taps_square = taps_square + value * value
            taps_biggest = jnp.maximum(taps_biggest, jnp.abs(value))
            small[k : k + 1, column] = value
    powers = (
        exponent(jnp.max(biggest) * (X_LIMIT * rows)),
        exponent(jnp.max(jnp.abs(gout[...]))),
        exponent(jnp.max(taps_biggest)),
    )
    for c in range(chunks):
        for i, power in enumerate(powers):
            small[9 + i : 10 + i, LANES * c : LANES * c + LANES] = power
    small[16:17, :LANES] = taps_square
    small[17:18, :] = jnp.sum(gout[...] * gout[...], axis=0, keepdims=True)
    if first.shape[0] == sizes.message:
        norm = message(sizes, scalars[3], x_vmem, dpre_out, gout, small, first, True)
        norm = norm + message(sizes, scalars[4], x_vmem, dpre_out, gout, small, early, True)
        small[18:19, :LANES] = norm


def message(sizes, place, x, dpre, gout, small, out, scaled):
    depth, depth_out = sizes.depth, sizes.depth_out
    column = pl.multiple_of(place * depth, LANES)
    block = lax.dot_general(
        x[:, pl.ds(column, depth)], dpre[...], (((0,), (0,)), ((), ())), preferred_element_type=jnp.float32
    )
    hidden = block.shape[1]
    chunks = hidden // LANES
    norm = jnp.sum(block * block, axis=0, keepdims=True)
    norm = sum(norm[:, LANES * c : LANES * c + LANES] for c in range(chunks))
    factors = [jnp.exp2(small[9 + i : 10 + i, :]) if scaled else 1.0 for i in range(3)]
    out[:depth, :] = block * factors[0]
    out[depth:, :] = jnp.zeros((out.shape[0] - depth, hidden), jnp.float32)
    column = pl.multiple_of(place * depth_out, LANES)
    for start, group in sizes.groups:
        value = gout[start : start + group, pl.ds(column, depth_out)]
        lane = start // sizes.group * LANES
        factor = factors[1][:, :LANES] if scaled else 1.0
        out[depth : depth + group, lane : lane + LANES] = value * factor
    row = depth + sizes.group
    out[row : row + 9, :] = small[0:9, :] * factors[2]
    if scaled:
        out[row + 9 : row + 12, :] = small[9:12, :]
    return norm


class Sizes:
    def __init__(self, wide, hidden, classes, dp):
        self.classes = classes
        self.depth = wide // dp
        self.depth_out = hidden // dp
        self.chunks = hidden // LANES
        self.class_rows = (classes + 7) // 8 * 8
        self.group = (self.class_rows // self.chunks + 7) // 8 * 8
        self.groups = [
            (at, min(self.group, self.class_rows - at)) for at in range(0, self.class_rows, self.group)
        ]
        self.message = self.depth + self.group + 16
        self.staged = dp == 4 and self.depth % LANES == 0 and self.depth_out == LANES


def head_backward(sizes, widths, scalars, halves, onehot, weight_in, taps, weight_out, masks):
    rows = onehot.shape[0]
    wide, hidden = weight_in.shape
    chunks = hidden // LANES
    vmem = pl.BlockSpec(memory_space=pltpu.VMEM)
    anywhere = pl.BlockSpec(memory_space=pl.ANY)
    span = 2 * REACH * (PC + 1) + rows
    return pl.pallas_call(
        functools.partial(head_kernel, sizes, widths),
        out_shape=[
            jax.ShapeDtypeStruct((rows, wide), jnp.bfloat16),
            jax.ShapeDtypeStruct((rows, hidden), jnp.bfloat16),
            jax.ShapeDtypeStruct((256, hidden), jnp.float32),
            jax.ShapeDtypeStruct((24, hidden), jnp.float32),
        ]
        + [jax.ShapeDtypeStruct((sizes.message if sizes.staged else 8, hidden), jnp.float32)] * 2,
        in_specs=[pl.BlockSpec(memory_space=pltpu.SMEM)] + [anywhere] * len(halves) + [vmem] * 6,
        out_specs=[vmem] * 6,
        scratch_shapes=[
            pltpu.VMEM((chunks, span, LANES), jnp.float32),
            pltpu.VMEM((chunks, span, LANES), jnp.float32),
            pltpu.VMEM((chunks, rows, LANES), jnp.float32),
            pltpu.VMEM((rows, hidden), jnp.bfloat16),
            pltpu.VMEM((rows, 256), jnp.bfloat16),
            pltpu.SemaphoreType.DMA((len(widths), 2)),
        ],
        compiler_params=pltpu.CompilerParams(vmem_limit_bytes=24 * 1024 * 1024),
        name="head",
    )(scalars, *halves, weight_in, taps, weight_out, onehot, *masks)


def blocks_kernel(sizes, scalars, x, dpre, gout, small, late, own, stats):
    norm = message(sizes, scalars[5], x, dpre, gout, small, late, True)
    norm = norm + message(sizes, scalars[6], x, dpre, gout, small, own, False)
    stats[...] = jnp.zeros(stats.shape, jnp.float32)
    stats[0:1, :] = norm + small[18:19, :LANES]
    stats[1:2, :] = small[16:17, :LANES]
    for c in range(sizes.chunks):
        stats[2 + c : 3 + c, :] = small[17:18, LANES * c : LANES * c + LANES]


def totals(sizes, parts, messages):
    mark = sizes.depth + sizes.group
    spans = ((0, sizes.depth), (sizes.depth, mark), (mark, mark + 9))
    sums = []
    for i, (start, stop) in enumerate(spans):
        total = parts[start:stop, :]
        for value in messages:
            total = total + value[start:stop, :] * jnp.exp2(-value[mark + 9 + i : mark + 10 + i, :])
        sums.append(total)
    return sums


def line_kernel(sizes, parts, far, edge, stats, line):
    def fold(value):
        value = jnp.sum(value.reshape(-1, 8, value.shape[1]), axis=0)
        return sum(value[:, LANES * c : LANES * c + LANES] for c in range(sizes.chunks))

    sum_in, sum_out, sum_taps = totals(sizes, parts, (far, edge))
    line[0:8, :] = fold(sum_in * sum_in)
    line[8:16, :] = fold(sum_out * sum_out)
    line[16:24, :] = stats[...]
    line[24:32, :] = jnp.zeros((8, LANES), jnp.float32)
    square = jnp.sum(sum_taps * sum_taps, axis=0, keepdims=True)
    line[24:25, :] = sum(square[:, LANES * c : LANES * c + LANES] for c in range(sizes.chunks))


def sum_kernel(sizes, parts, far, edge, share_in, share_out, taps_out):
    sum_in, sum_out, sum_taps = totals(sizes, parts, (far, edge))
    share_in[...] = sum_in
    for start, group in sizes.groups:
        lane = start // sizes.group * LANES
        count = min(group, sizes.classes - start)
        share_out[start : start + count, 0, :] = sum_out[:count, lane : lane + LANES]
    for k in range(9):
        taps_out[k, :, :] = sum_taps[k : k + 1, :]


def norm_kernel(chunks, *refs):
    lines, out = refs[:-1], refs[-1]
    total = sum(line[...] for line in lines)
    line = lines[0]
    values = [
        jnp.sum(total[16:17, :]),
        jnp.sum(total[17:18, :]),
        jnp.sum(total[18 : 18 + chunks, :]),
        jnp.sum(total[0:8, :]),
        jnp.sum(line[24:25, :]),
        jnp.sum(total[8:16, :]),
    ]
    row = lax.broadcasted_iota(jnp.int32, (8, LANES), 0)
    lane = lax.broadcasted_iota(jnp.int32, (8, LANES), 1)
    spread = jnp.zeros((8, LANES), jnp.float32)
    for i, value in enumerate(values):
        spread = jnp.where((row == i // 3) & (lane == i % 3), value, spread)
    out[...] = jnp.log(1e-12 + spread)[:2, :3]


def permute(value, pairs):
    return lax.ppermute(value, "dp", pairs)


def add_kernel(sizes, scalars, mine, theirs, out):
    depth, group = sizes.depth, sizes.group
    mark = depth + group
    end = (scalars[6] == 0) | (scalars[6] == 3)

    @pl.when(end)
    def _():
        out[...] = mine[...]

    @pl.when(jnp.logical_not(end))
    def _():
        for i, (start, stop) in enumerate(((0, depth), (depth, mark), (mark, mark + 9))):
            at = mark + 9 + i
            a, b = mine[at : at + 1, :], theirs[at : at + 1, :]
            common = jnp.minimum(a, b)
            out[start:stop, :] = mine[start:stop, :] * jnp.exp2(common - a) + theirs[
                start:stop, :
            ] * jnp.exp2(common - b)
            out[at : at + 1, :] = common
        out[mark + 12 :, :] = mine[mark + 12 :, :]


def by_row(sizes, shape, three):
    row = lax.broadcasted_iota(jnp.int32, shape, 0)
    return jnp.where(
        row < sizes.depth, three[0], jnp.where(row < sizes.depth + sizes.group, three[1], three[2])
    )


def staged_sums(sizes, me, scalars, xrows, dpre, gout, small, first, early):
    vmem = pl.BlockSpec(memory_space=pltpu.VMEM)
    smem = pl.BlockSpec(memory_space=pltpu.SMEM)
    hidden = dpre.shape[1]
    shape = (sizes.message, hidden)
    full = jax.ShapeDtypeStruct(shape, jnp.float32)
    lines = jax.ShapeDtypeStruct((8, LANES), jnp.float32)
    half = jnp.float16
    near = permute(first.astype(half), [(0, 1), (1, 0), (2, 3), (3, 2)])
    early = early.astype(half)
    middle = permute(early, [(1, 2), (2, 1)])
    late, own, stats = pl.pallas_call(
        functools.partial(blocks_kernel, sizes),
        out_shape=[full, full, lines],
        in_specs=[smem] + [vmem] * 4,
        out_specs=[vmem] * 3,
        compiler_params=pltpu.CompilerParams(vmem_limit_bytes=16 * 1024 * 1024),
        cost_estimate=pl.CostEstimate(
            flops=4 * sizes.depth * dpre.shape[0] * hidden,
            bytes_accessed=2 * xrows.size + 2 * dpre.size + 8 * sizes.message * hidden,
            transcendentals=0,
        ),
        name="blocks",
    )(scalars, xrows, dpre, gout, small)
    end = (me == 0) | (me == 3)
    mark = sizes.depth + sizes.group + 9
    both = pl.pallas_call(
        functools.partial(add_kernel, sizes),
        out_shape=full,
        in_specs=[smem, vmem, vmem],
        out_specs=vmem,
        compiler_params=pltpu.CompilerParams(vmem_limit_bytes=8 * 1024 * 1024),
        name="add",
    )(scalars, late, near.astype(jnp.float32))
    both = both.astype(half)
    far = permute(both, [(0, 2), (2, 0), (1, 3), (3, 1)])
    early, _ = lax.optimization_barrier((early, both))
    near, middle, _ = lax.optimization_barrier((near, middle, both))
    edge = permute(early, [(0, 1), (3, 2)])
    value = jnp.where(end, near, middle).astype(jnp.float32)
    parts = own + value * by_row(
        sizes, shape, [jnp.exp2(-value[mark + i : mark + i + 1]) for i in range(3)]
    )
    return parts, far.astype(jnp.float32), edge.astype(jnp.float32), stats


def per_device(sizes, dp, trials, features, owner, dilation_index, labels, input_weight, taps, output_weight):
    here, core, widths, halves = pieces(features[0, 0], "trial", trials, owner[0])
    me = lax.axis_index("dp")
    dil = dilation_index[0] + 1
    rows = features.shape[2]
    onehot = (labels[0][:, None] == jnp.arange(256, dtype=jnp.int32)[None, :]).astype(jnp.bfloat16)
    column = lax.broadcasted_iota(jnp.int32, (rows, LANES), 0) % PC
    before = (column < PC - dil).astype(jnp.float32)
    after = (column >= dil).astype(jnp.float32)
    classes, chunks = sizes.classes, sizes.chunks
    weight_out = jnp.pad(output_weight[0].T, ((0, 256 - classes), (0, 0)))
    high = me >= 2
    odd = me % 2
    step, jump = jnp.where(odd == 0, 1, 2), jnp.where(high, me - 2, me + 2)
    to = [3 * (1 - odd), step, jump, me]
    scalars = jnp.stack([dil, here, core] + to).astype(jnp.int32)
    xrows, dpre, gout, small, first, early = head_backward(
        sizes,
        widths,
        scalars,
        halves,
        onehot,
        input_weight[0],
        taps[0][:, None, :],
        weight_out,
        (after, before),
    )
    if not sizes.staged:
        return general_sums(sizes, xrows, dpre, gout, small)
    parts, far, edge, stats = staged_sums(sizes, me, scalars, xrows, dpre, gout, small, first, early)
    vmem = pl.BlockSpec(memory_space=pltpu.VMEM)
    hidden = dpre.shape[1]
    small = pltpu.CompilerParams(vmem_limit_bytes=8 * 1024 * 1024)
    line = pl.pallas_call(
        functools.partial(line_kernel, sizes),
        out_shape=jax.ShapeDtypeStruct((32, LANES), jnp.float32),
        in_specs=[vmem] * 4,
        out_specs=vmem,
        compiler_params=small,
        name="line",
    )(parts, far, edge, stats)
    lines = [line] + [permute(line, [(i, i ^ s) for i in range(dp)]) for s in range(1, dp)]
    share_in, share_out, total_taps = pl.pallas_call(
        functools.partial(sum_kernel, sizes),
        out_shape=[
            jax.ShapeDtypeStruct((sizes.depth, hidden), jnp.float32),
            jax.ShapeDtypeStruct((classes, 1, sizes.depth_out), jnp.float32),
            jax.ShapeDtypeStruct((9, 1, hidden), jnp.float32),
        ],
        in_specs=[vmem] * 3,
        out_specs=[vmem] * 3,
        compiler_params=small,
        cost_estimate=pl.CostEstimate(
            flops=2 * parts.size, bytes_accessed=16 * parts.size, transcendentals=0
        ),
        name="sums",
    )(parts, far, edge)
    norms = pl.pallas_call(
        functools.partial(norm_kernel, chunks),
        out_shape=jax.ShapeDtypeStruct((2, 3), jnp.float32),
        in_specs=[vmem] * dp,
        out_specs=vmem,
        compiler_params=pltpu.CompilerParams(vmem_limit_bytes=4 * 1024 * 1024),
        name="norms",
    )(*lines)
    share_out = jnp.transpose(share_out, (1, 2, 0))
    return (share_in[None], jnp.transpose(total_taps, (1, 0, 2)), share_out, norms[None])


def general_sums(sizes, xrows, dpre, gout, small):
    g_in = jnp.dot(xrows.T, dpre, preferred_element_type=jnp.float32)
    g_out = gout[: sizes.classes].T
    g_taps = small[:9]
    share_in = lax.psum_scatter(g_in, "dp", scatter_dimension=0, tiled=True)
    share_out = lax.psum_scatter(g_out, "dp", scatter_dimension=0, tiled=True)
    local = jnp.stack([jnp.sum(g_in * g_in), jnp.sum(g_taps * g_taps), jnp.sum(g_out * g_out)])
    share_sq = jnp.stack([jnp.sum(share_in * share_in), jnp.sum(share_out * share_out)])
    total_taps, squares, share_total = lax.psum((g_taps, local, share_sq), "dp")
    totals = jnp.stack([share_total[0], jnp.sum(total_taps * total_taps), share_total[1]])
    norms = jnp.log(1e-12 + jnp.stack([squares, totals]))
    return (share_in[None], total_taps[None], share_out[None], norms[None])


def solution(mesh):
    dp, trials = mesh.shape["dp"], mesh.shape["trial"]
    placed = (
        P(("groups", "dp"), "trial", None, None),
        P(("groups", "dp")),
        P("trial"),
        P(("groups", "dp"), None),
        P("trial", None, None),
        P("trial", None, None),
        P("trial", None, None),
    )

    def step(*args):
        (wide, hidden), classes = args[4].shape[1:], args[6].shape[2]
        return per_device(Sizes(wide, hidden, classes, dp), dp, trials, *args)

    return jax.shard_map(
        step,
        mesh=mesh,
        in_specs=placed,
        out_specs=(
            P(("groups", "trial"), "dp", None),
            P(("groups", "trial"), None, None),
            P(("groups", "trial"), "dp", None),
            P(("groups", "trial"), None, None),
        ),
        check_vma=False,
    )
```

```python
import functools
import math

import jax
import jax.numpy as jnp
from jax import lax
from jax.experimental import pallas as pl
from jax.experimental.pallas import tpu as pltpu
from jax.sharding import PartitionSpec as P

PC = 37
LANES = 128
FORWARD_STEP = 64
BACKWARD_STEP = 64
REACH = 4
OFFSETS = [(a, b) for a in (-1, 0, 1) for b in (-1, 0, 1)]
X_LIMIT = 6.0
ROOM = 16384.0


def pieces(block, axis, size, source):
    width = block.shape[1] // 2
    if size != 4:
        block = jnp.where(lax.axis_index(axis) == source, block, jnp.zeros_like(block))
        block = lax.psum(block, axis)
        low, high = block[:, :width], block[:, width:]
        zero = jnp.int32(0)
        return zero + 1, zero, (width,), (low, low, high, high)
    me = lax.axis_index(axis)
    core = me % 2
    mate = [(0, 1), (1, 0), (2, 3), (3, 2)]
    across = [(0, 2), (2, 0), (1, 3), (3, 1)]
    here = ((source // 2) == (me // 2)).astype(jnp.int32)
    widths = split_width(width)
    got = lax.ppermute(jnp.where(core == 0, block[:, width:], block[:, :width]), axis, mate)
    values = []
    at = 0
    for piece in widths:
        low, high = block[:, at : at + piece], block[:, width + at : width + at + piece]
        kept = jnp.where(core == 0, low, high)
        held = jnp.where(source % 2 == core, kept, got[:, at : at + piece])
        other = lax.ppermute(held, axis, across)
        values += [held, other, lax.ppermute(held, axis, mate), lax.ppermute(other, axis, mate)]
        at += piece
    return here, core, widths, tuple(values)


def split_width(width):
    tiles = width // LANES
    last = max(tiles // 3, 1)
    return tuple(LANES * n for n in (tiles - last, last) if n > 0)


def gelu_parts(value):
    square = value * value
    half = 0.5 + 0.5 * jnp.tanh(value * (0.7978845608 + (0.7978845608 * 0.044715) * square))
    out_val = value * half
    rate = 2.0 * 0.7978845608 + (6.0 * 0.7978845608 * 0.044715) * square
    return (out_val, half + out_val * (1.0 - half) * rate)


def exponent(size):
    size = jnp.maximum(jnp.full((1, LANES), size, jnp.float32), 1e-30)
    return jnp.clip(jnp.floor(jnp.log(ROOM / size) * (1.0 / math.log(2.0))), -100.0, 100.0)


def head_kernel(
    sizes,
    widths,
    scalars,
    *refs,
):
    halves, refs = refs[: 4 * len(widths)], refs[4 * len(widths) :]
    weight_in, taps, weight_out, onehot, after, before = refs[:6]
    x_vmem, dpre_out, gout, small, first, early = refs[6:12]
    pre, dys, slope, hid, dlog, sem_in = refs[12:]
    rows = x_vmem.shape[0]
    width = x_vmem.shape[1] // 2
    hidden = weight_in.shape[1]
    chunks = hidden // LANES
    guard = REACH * (PC + 1)
    dil, here, core = scalars[0], scalars[1], scalars[2]

    def fetch(kind, index):
        column = (core if kind < 2 else 1 - core) * width + sum(widths[:index])
        target = x_vmem.at[:, pl.ds(pl.multiple_of(column, LANES), widths[index])]
        return pltpu.make_async_copy(halves[4 * index + kind], target, sem_in.at[index, kind // 2])

    for away in (0, 1):

        @pl.when(here == 1 - away)
        def _(away=away):
            for index in range(len(widths)):
                fetch(away, index).start()
                fetch(2 + away, index).start()

    for c in range(chunks):
        for ref in (pre, dys):
            ref[c, :guard, :] = jnp.zeros((guard, LANES), jnp.float32)
            ref[c, guard + rows :, :] = jnp.zeros((guard, LANES), jnp.float32)
    for index in range(len(widths)):
        fetch(0, index).wait()
        fetch(2, index).wait()

    for n in range(hidden // 256):
        value = jnp.dot(
            x_vmem[...], weight_in[:, 256 * n : 256 * n + 256], preferred_element_type=jnp.float32
        )
        for h in range(2):
            pre[2 * n + h, guard : guard + rows, :] = value[:, LANES * h : LANES * h + LANES]

    starts = [dil * (PC * a + b) for a, b in OFFSETS]

    def column_sums(source, c, row, count, sign):
        column = slice(LANES * c, LANES * c + LANES)
        sums = []
        for b in range(3):
            total = None
            for k in (b, 3 + b, 6 + b):
                at = guard + row + sign * starts[k]
                term = source[c, pl.ds(at, count), :] * taps[k, :, column]
                total = term if total is None else total + term
            sums.append(total)
        return sums

    def forward(row, count):
        low, high = after[pl.ds(row, count), :], before[pl.ds(row, count), :]
        for c in range(chunks):
            sums = column_sums(pre, c, row, count, 1)
            act, grad = gelu_parts(sums[1] + low * sums[0] + high * sums[2])
            slope[c, pl.ds(row, count), :] = grad
            hid[pl.ds(row, count), LANES * c : LANES * c + LANES] = act.astype(jnp.bfloat16)

    def run(step, body):
        whole = rows // step

        @pl.loop(0, whole)
        def _(i):
            body(pl.multiple_of(i * step, step), step)

        if rows > whole * step:
            body(whole * step, rows - whole * step)

    run(FORWARD_STEP, forward)

    logits = lax.dot_general(
        hid[...], weight_out[...], (((1,), (1,)), ((), ())), preferred_element_type=jnp.float32
    )
    lane = lax.broadcasted_iota(jnp.int32, logits.shape, 1)
    logits = jnp.where(lane < sizes.classes, logits, -1e30)
    peak = jnp.max(logits, axis=1, keepdims=True)
    power = jnp.exp(logits - peak)
    prob = power / jnp.sum(power, axis=1, keepdims=True)
    dlog[...] = (prob - onehot[...].astype(jnp.float32)).astype(jnp.bfloat16)

    gout[...] = lax.dot_general(
        dlog[...], hid[...], (((0,), (0,)), ((), ())), preferred_element_type=jnp.float32
    )
    for n in range(hidden // 256):
        value = jnp.dot(
            dlog[...], weight_out[:, 256 * n : 256 * n + 256], preferred_element_type=jnp.float32
        )
        for h in range(2):
            c = 2 * n + h
            dys[c, guard : guard + rows, :] = value[:, LANES * h : LANES * h + LANES] * slope[c]

    def fold(value):
        return jnp.sum(value.reshape(-1, 8, LANES), axis=0)

    biggest = jnp.zeros((8, LANES), jnp.float32)
    taps_biggest = jnp.zeros((1, LANES), jnp.float32)
    small[...] = jnp.zeros(small.shape, jnp.float32)
    taps_square = jnp.zeros((1, LANES), jnp.float32)
    for c in range(chunks):
        column = slice(LANES * c, LANES * c + LANES)

        def backward(row, count, carry):
            sums, top = carry
            low, high = after[pl.ds(row, count), :], before[pl.ds(row, count), :]
            dy = dys[c, pl.ds(guard + row, count), :]
            masked = (dy * low, dy, dy * high)
            out = [
                sums[k] + fold(masked[k % 3] * pre[c, pl.ds(guard + row + starts[k], count), :])
                for k in range(9)
            ]
            back = column_sums(dys, c, row, count, -1)
            total = back[1] + high * back[0] + low * back[2]
            dpre_out[pl.ds(row, count), column] = total.astype(jnp.bfloat16)
            size = jnp.max(jnp.abs(total).reshape(-1, 8, LANES), axis=0)
            return tuple(out), jnp.maximum(top, size)

        zeros = tuple(jnp.zeros((8, LANES), jnp.float32) for _ in range(9))
        step = BACKWARD_STEP
        whole = rows // step
        carry = lax.fori_loop(
            0,
            whole,
            lambda i, carry, step=step: backward(pl.multiple_of(i * step, step), step, carry),
            (zeros, biggest),
        )
        if rows > whole * step:
            carry = backward(whole * step, rows - whole * step, carry)
        sums, biggest = carry
        for k in range(9):
            value = jnp.sum(sums[k], axis=0, keepdims=True)
            taps_square = taps_square + value * value
            taps_biggest = jnp.maximum(taps_biggest, jnp.abs(value))
            small[k : k + 1, column] = value
    powers = (
        exponent(jnp.max(biggest) * (X_LIMIT * rows)),
        exponent(jnp.max(jnp.abs(gout[...]))),
        exponent(jnp.max(taps_biggest)),
    )
    for c in range(chunks):
        for i, power in enumerate(powers):
            small[9 + i : 10 + i, LANES * c : LANES * c + LANES] = power
    small[16:17, :LANES] = taps_square
    small[17:18, :] = jnp.sum(gout[...] * gout[...], axis=0, keepdims=True)
    if first.shape[0] == sizes.message:
        norm = message(sizes, scalars[3], x_vmem, dpre_out, gout, small, first, True)
        norm = norm + message(sizes, scalars[4], x_vmem, dpre_out, gout, small, early, True)
        small[18:19, :LANES] = norm


def message(sizes, place, x, dpre, gout, small, out, scaled):
    depth, depth_out = sizes.depth, sizes.depth_out
    column = pl.multiple_of(place * depth, LANES)
    block = lax.dot_general(
        x[:, pl.ds(column, depth)], dpre[...], (((0,), (0,)), ((), ())), preferred_element_type=jnp.float32
    )
    hidden = block.shape[1]
    chunks = hidden // LANES
    norm = jnp.sum(block * block, axis=0, keepdims=True)
    norm = sum(norm[:, LANES * c : LANES * c + LANES] for c in range(chunks))
    factors = [jnp.exp2(small[9 + i : 10 + i, :]) if scaled else 1.0 for i in range(3)]
    out[:depth, :] = block * factors[0]
    out[depth:, :] = jnp.zeros((out.shape[0] - depth, hidden), jnp.float32)
    column = pl.multiple_of(place * depth_out, LANES)
    for start, group in sizes.groups:
        value = gout[start : start + group, pl.ds(column, depth_out)]
        lane = start // sizes.group * LANES
        factor = factors[1][:, :LANES] if scaled else 1.0
        out[depth : depth + group, lane : lane + LANES] = value * factor
    row = depth + sizes.group
    out[row : row + 9, :] = small[0:9, :] * factors[2]
    if scaled:
        out[row + 9 : row + 12, :] = small[9:12, :]
    return norm


class Sizes:
    def __init__(self, wide, hidden, classes, dp):
        self.classes = classes
        self.depth = wide // dp
        self.depth_out = hidden // dp
        self.chunks = hidden // LANES
        self.class_rows = (classes + 7) // 8 * 8
        self.group = (self.class_rows // self.chunks + 7) // 8 * 8
        self.groups = [
            (at, min(self.group, self.class_rows - at)) for at in range(0, self.class_rows, self.group)
        ]
        self.message = self.depth + self.group + 16
        self.staged = dp == 4 and self.depth % LANES == 0 and self.depth_out == LANES


def head_backward(sizes, widths, scalars, halves, onehot, weight_in, taps, weight_out, masks):
    rows = onehot.shape[0]
    wide, hidden = weight_in.shape
    chunks = hidden // LANES
    vmem = pl.BlockSpec(memory_space=pltpu.VMEM)
    anywhere = pl.BlockSpec(memory_space=pl.ANY)
    span = 2 * REACH * (PC + 1) + rows
    return pl.pallas_call(
        functools.partial(head_kernel, sizes, widths),
        out_shape=[
            jax.ShapeDtypeStruct((rows, wide), jnp.bfloat16),
            jax.ShapeDtypeStruct((rows, hidden), jnp.bfloat16),
            jax.ShapeDtypeStruct((256, hidden), jnp.float32),
            jax.ShapeDtypeStruct((24, hidden), jnp.float32),
        ]
        + [jax.ShapeDtypeStruct((sizes.message if sizes.staged else 8, hidden), jnp.float32)] * 2,
        in_specs=[pl.BlockSpec(memory_space=pltpu.SMEM)] + [anywhere] * len(halves) + [vmem] * 6,
        out_specs=[vmem] * 6,
        scratch_shapes=[
            pltpu.VMEM((chunks, span, LANES), jnp.float32),
            pltpu.VMEM((chunks, span, LANES), jnp.float32),
            pltpu.VMEM((chunks, rows, LANES), jnp.float32),
            pltpu.VMEM((rows, hidden), jnp.bfloat16),
            pltpu.VMEM((rows, 256), jnp.bfloat16),
            pltpu.SemaphoreType.DMA((len(widths), 2)),
        ],
        compiler_params=pltpu.CompilerParams(vmem_limit_bytes=24 * 1024 * 1024),
        name="head",
    )(scalars, *halves, weight_in, taps, weight_out, onehot, *masks)


def blocks_kernel(sizes, scalars, x, dpre, gout, small, late, own, stats):
    norm = message(sizes, scalars[5], x, dpre, gout, small, late, True)
    norm = norm + message(sizes, scalars[6], x, dpre, gout, small, own, False)
    stats[...] = jnp.zeros(stats.shape, jnp.float32)
    stats[0:1, :] = norm + small[18:19, :LANES]
    stats[1:2, :] = small[16:17, :LANES]
    for c in range(sizes.chunks):
        stats[2 + c : 3 + c, :] = small[17:18, LANES * c : LANES * c + LANES]


def totals(sizes, parts, last):
    mark = sizes.depth + sizes.group
    spans = ((0, sizes.depth), (sizes.depth, mark), (mark, mark + 9))
    return [
        parts[start:stop, :] + last[start:stop, :] * jnp.exp2(-last[mark + 9 + i : mark + 10 + i, :])
        for i, (start, stop) in enumerate(spans)
    ]


def line_kernel(sizes, parts, last, stats, line):
    def fold(value):
        value = jnp.sum(value.reshape(-1, 8, value.shape[1]), axis=0)
        return sum(value[:, LANES * c : LANES * c + LANES] for c in range(sizes.chunks))

    sum_in, sum_out, sum_taps = totals(sizes, parts, last)
    line[0:8, :] = fold(sum_in * sum_in)
    line[8:16, :] = fold(sum_out * sum_out)
    line[16:24, :] = stats[...]
    line[24:32, :] = jnp.zeros((8, LANES), jnp.float32)
    square = jnp.sum(sum_taps * sum_taps, axis=0, keepdims=True)
    line[24:25, :] = sum(square[:, LANES * c : LANES * c + LANES] for c in range(sizes.chunks))


def sum_kernel(sizes, parts, last, share_in, share_out, taps_out):
    sum_in, sum_out, sum_taps = totals(sizes, parts, last)
    share_in[...] = sum_in
    for start, group in sizes.groups:
        lane = start // sizes.group * LANES
        count = min(group, sizes.classes - start)
        share_out[start : start + count, 0, :] = sum_out[:count, lane : lane + LANES]
    for k in range(9):
        taps_out[k, :, :] = sum_taps[k : k + 1, :]


def norm_kernel(chunks, *refs):
    lines, out = refs[:-1], refs[-1]
    total = sum(line[...] for line in lines)
    line = lines[0]
    values = [
        jnp.sum(total[16:17, :]),
        jnp.sum(total[17:18, :]),
        jnp.sum(total[18 : 18 + chunks, :]),
        jnp.sum(total[0:8, :]),
        jnp.sum(line[24:25, :]),
        jnp.sum(total[8:16, :]),
    ]
    row = lax.broadcasted_iota(jnp.int32, (8, LANES), 0)
    lane = lax.broadcasted_iota(jnp.int32, (8, LANES), 1)
    spread = jnp.zeros((8, LANES), jnp.float32)
    for i, value in enumerate(values):
        spread = jnp.where((row == i // 3) & (lane == i % 3), value, spread)
    out[...] = jnp.log(1e-12 + spread)[:2, :3]


def permute(value, pairs):
    return lax.ppermute(value, "dp", pairs)


def add_kernel(sizes, scalars, mine, theirs, out):
    depth, group = sizes.depth, sizes.group
    mark = depth + group
    end = (scalars[6] == 0) | (scalars[6] == 3)

    @pl.when(end)
    def _():
        out[...] = mine[...]

    @pl.when(jnp.logical_not(end))
    def _():
        for i, (start, stop) in enumerate(((0, depth), (depth, mark), (mark, mark + 9))):
            at = mark + 9 + i
            a, b = mine[at : at + 1, :], theirs[at : at + 1, :]
            common = jnp.minimum(a, b)
            out[start:stop, :] = mine[start:stop, :] * jnp.exp2(common - a) + theirs[
                start:stop, :
            ] * jnp.exp2(common - b)
            out[at : at + 1, :] = common
        out[mark + 12 :, :] = mine[mark + 12 :, :]


def by_row(sizes, shape, three):
    row = lax.broadcasted_iota(jnp.int32, shape, 0)
    return jnp.where(
        row < sizes.depth, three[0], jnp.where(row < sizes.depth + sizes.group, three[1], three[2])
    )


def staged_sums(sizes, me, scalars, xrows, dpre, gout, small, first, early):
    vmem = pl.BlockSpec(memory_space=pltpu.VMEM)
    smem = pl.BlockSpec(memory_space=pltpu.SMEM)
    hidden = dpre.shape[1]
    shape = (sizes.message, hidden)
    full = jax.ShapeDtypeStruct(shape, jnp.float32)
    lines = jax.ShapeDtypeStruct((8, LANES), jnp.float32)
    half = jnp.float16
    near = permute(first.astype(half), [(0, 1), (1, 0), (2, 3), (3, 2)])
    early = early.astype(half)
    middle = permute(early, [(1, 2), (2, 1)])
    late, own, stats = pl.pallas_call(
        functools.partial(blocks_kernel, sizes),
        out_shape=[full, full, lines],
        in_specs=[smem] + [vmem] * 4,
        out_specs=[vmem] * 3,
        compiler_params=pltpu.CompilerParams(vmem_limit_bytes=16 * 1024 * 1024),
        cost_estimate=pl.CostEstimate(
            flops=4 * sizes.depth * dpre.shape[0] * hidden,
            bytes_accessed=2 * xrows.size + 2 * dpre.size + 8 * sizes.message * hidden,
            transcendentals=0,
        ),
        name="blocks",
    )(scalars, xrows, dpre, gout, small)
    end = (me == 0) | (me == 3)
    mark = sizes.depth + sizes.group + 9
    both = pl.pallas_call(
        functools.partial(add_kernel, sizes),
        out_shape=full,
        in_specs=[smem, vmem, vmem],
        out_specs=vmem,
        compiler_params=pltpu.CompilerParams(vmem_limit_bytes=8 * 1024 * 1024),
        name="add",
    )(scalars, late, near.astype(jnp.float32))
    both = both.astype(half)
    far = permute(both, [(0, 1), (3, 2), (1, 3), (2, 0)])
    early, _ = lax.optimization_barrier((early, both))
    near, middle, _ = lax.optimization_barrier((near, middle, both))
    skip = permute(early, [(0, 2), (3, 1)])

    def split(value):
        return [value[mark + i : mark + i + 1] for i in range(3)]


    def decode(value):
        value = value.astype(jnp.float32)
        return value * by_row(sizes, shape, [jnp.exp2(-v) for v in split(value)])

    parts = own + decode(jnp.where(end, near, middle)) + decode(skip)
    return parts, far.astype(jnp.float32), stats


def per_device(sizes, dp, trials, features, owner, dilation_index, labels, input_weight, taps, output_weight):
    here, core, widths, halves = pieces(features[0, 0], "trial", trials, owner[0])
    me = lax.axis_index("dp")
    dil = dilation_index[0] + 1
    rows = features.shape[2]
    onehot = (labels[0][:, None] == jnp.arange(256, dtype=jnp.int32)[None, :]).astype(jnp.bfloat16)
    column = lax.broadcasted_iota(jnp.int32, (rows, LANES), 0) % PC
    before = (column < PC - dil).astype(jnp.float32)
    after = (column >= dil).astype(jnp.float32)
    classes, chunks = sizes.classes, sizes.chunks
    weight_out = jnp.pad(output_weight[0].T, ((0, 256 - classes), (0, 0)))
    high = me >= 2
    odd = me % 2
    end = (me == 0) | (me == 3)
    step, jump = jnp.where(odd == 0, 1, 2), jnp.where(high, me - 2, me + 2)
    to = [3 * (1 - odd), jnp.where(end, jump, step), jnp.where(end, step, jump), me]
    scalars = jnp.stack([dil, here, core] + to).astype(jnp.int32)
    xrows, dpre, gout, small, first, early = head_backward(
        sizes,
        widths,
        scalars,
        halves,
        onehot,
        input_weight[0],
        taps[0][:, None, :],
        weight_out,
        (after, before),
    )
    if not sizes.staged:
        return general_sums(sizes, xrows, dpre, gout, small)
    parts, last, stats = staged_sums(sizes, me, scalars, xrows, dpre, gout, small, first, early)
    vmem = pl.BlockSpec(memory_space=pltpu.VMEM)
    hidden = dpre.shape[1]
    small = pltpu.CompilerParams(vmem_limit_bytes=8 * 1024 * 1024)
    line = pl.pallas_call(
        functools.partial(line_kernel, sizes),
        out_shape=jax.ShapeDtypeStruct((32, LANES), jnp.float32),
        in_specs=[vmem] * 3,
        out_specs=vmem,
        compiler_params=small,
        name="line",
    )(parts, last, stats)
    lines = [line] + [permute(line, [(i, i ^ s) for i in range(dp)]) for s in range(1, dp)]
    share_in, share_out, total_taps = pl.pallas_call(
        functools.partial(sum_kernel, sizes),
        out_shape=[
            jax.ShapeDtypeStruct((sizes.depth, hidden), jnp.float32),
            jax.ShapeDtypeStruct((classes, 1, sizes.depth_out), jnp.float32),
            jax.ShapeDtypeStruct((9, 1, hidden), jnp.float32),
        ],
        in_specs=[vmem] * 2,
        out_specs=[vmem] * 3,
        compiler_params=small,
        cost_estimate=pl.CostEstimate(
            flops=2 * parts.size, bytes_accessed=16 * parts.size, transcendentals=0
        ),
        name="sums",
    )(parts, last)
    norms = pl.pallas_call(
        functools.partial(norm_kernel, chunks),
        out_shape=jax.ShapeDtypeStruct((2, 3), jnp.float32),
        in_specs=[vmem] * dp,
        out_specs=vmem,
        compiler_params=pltpu.CompilerParams(vmem_limit_bytes=4 * 1024 * 1024),
        name="norms",
    )(*lines)
    share_out = jnp.transpose(share_out, (1, 2, 0))
    return (share_in[None], jnp.transpose(total_taps, (1, 0, 2)), share_out, norms[None])


def general_sums(sizes, xrows, dpre, gout, small):
    g_in = jnp.dot(xrows.T, dpre, preferred_element_type=jnp.float32)
    g_out = gout[: sizes.classes].T
    g_taps = small[:9]
    share_in = lax.psum_scatter(g_in, "dp", scatter_dimension=0, tiled=True)
    share_out = lax.psum_scatter(g_out, "dp", scatter_dimension=0, tiled=True)
    local = jnp.stack([jnp.sum(g_in * g_in), jnp.sum(g_taps * g_taps), jnp.sum(g_out * g_out)])
    share_sq = jnp.stack([jnp.sum(share_in * share_in), jnp.sum(share_out * share_out)])
    total_taps, squares, share_total = lax.psum((g_taps, local, share_sq), "dp")
    totals = jnp.stack([share_total[0], jnp.sum(total_taps * total_taps), share_total[1]])
    norms = jnp.log(1e-12 + jnp.stack([squares, totals]))
    return (share_in[None], total_taps[None], share_out[None], norms[None])


def solution(mesh):
    dp, trials = mesh.shape["dp"], mesh.shape["trial"]
    placed = (
        P(("groups", "dp"), "trial", None, None),
        P(("groups", "dp")),
        P("trial"),
        P(("groups", "dp"), None),
        P("trial", None, None),
        P("trial", None, None),
        P("trial", None, None),
    )

    def step(*args):
        (wide, hidden), classes = args[4].shape[1:], args[6].shape[2]
        return per_device(Sizes(wide, hidden, classes, dp), dp, trials, *args)

    return jax.shard_map(
        step,
        mesh=mesh,
        in_specs=placed,
        out_specs=(
            P(("groups", "trial"), "dp", None),
            P(("groups", "trial"), None, None),
            P(("groups", "trial"), "dp", None),
            P(("groups", "trial"), None, None),
        ),
        check_vma=False,
    )
```

```python
import functools
import math

import jax
import jax.numpy as jnp
from jax import lax
from jax.experimental import pallas as pl
from jax.experimental.pallas import tpu as pltpu
from jax.sharding import PartitionSpec as P

PC = 37
LANES = 128
FORWARD_STEP = 64
BACKWARD_STEP = 64
REACH = 4
OFFSETS = [(a, b) for a in (-1, 0, 1) for b in (-1, 0, 1)]
X_LIMIT = 6.0
ROOM = 16384.0


def pieces(block, axis, size, source):
    width = block.shape[1] // 2
    if size != 4:
        block = jnp.where(lax.axis_index(axis) == source, block, jnp.zeros_like(block))
        block = lax.psum(block, axis)
        low, high = block[:, :width], block[:, width:]
        zero = jnp.int32(0)
        return zero + 1, zero, (width,), (low, low, high, high)
    me = lax.axis_index(axis)
    core = me % 2
    mate = [(0, 1), (1, 0), (2, 3), (3, 2)]
    across = [(0, 2), (2, 0), (1, 3), (3, 1)]
    here = ((source // 2) == (me // 2)).astype(jnp.int32)
    widths = split_width(width)
    got = lax.ppermute(jnp.where(core == 0, block[:, width:], block[:, :width]), axis, mate)
    values = []
    at = 0
    for piece in widths:
        low, high = block[:, at : at + piece], block[:, width + at : width + at + piece]
        kept = jnp.where(core == 0, low, high)
        held = jnp.where(source % 2 == core, kept, got[:, at : at + piece])
        other = lax.ppermute(held, axis, across)
        values += [held, other, lax.ppermute(held, axis, mate), lax.ppermute(other, axis, mate)]
        at += piece
    return here, core, widths, tuple(values)


def split_width(width):
    tiles = width // LANES
    last = max(tiles // 3, 1)
    return tuple(LANES * n for n in (tiles - last, last) if n > 0)


def gelu_parts(value):
    square = value * value
    half = 0.5 + 0.5 * jnp.tanh(value * (0.7978845608 + (0.7978845608 * 0.044715) * square))
    out_val = value * half
    rate = 2.0 * 0.7978845608 + (6.0 * 0.7978845608 * 0.044715) * square
    return (out_val, half + out_val * (1.0 - half) * rate)


def exponent(size):
    size = jnp.maximum(jnp.full((1, LANES), size, jnp.float32), 1e-30)
    return jnp.clip(jnp.floor(jnp.log(ROOM / size) * (1.0 / math.log(2.0))), -100.0, 100.0)


def head_kernel(
    sizes,
    widths,
    scalars,
    *refs,
):
    halves, refs = refs[: 4 * len(widths)], refs[4 * len(widths) :]
    weight_in, taps, weight_out, onehot, after, before = refs[:6]
    x_vmem, dpre_out, gout, small, first, early = refs[6:12]
    pre, dys, slope, hid, dlog, sem_in = refs[12:]
    rows = x_vmem.shape[0]
    width = x_vmem.shape[1] // 2
    hidden = weight_in.shape[1]
    chunks = hidden // LANES
    guard = REACH * (PC + 1)
    dil, here, core = scalars[0], scalars[1], scalars[2]

    def fetch(kind, index):
        column = (core if kind < 2 else 1 - core) * width + sum(widths[:index])
        target = x_vmem.at[:, pl.ds(pl.multiple_of(column, LANES), widths[index])]
        return pltpu.make_async_copy(halves[4 * index + kind], target, sem_in.at[index, kind // 2])

    for away in (0, 1):

        @pl.when(here == 1 - away)
        def _(away=away):
            for index in range(len(widths)):
                fetch(away, index).start()
                fetch(2 + away, index).start()

    for c in range(chunks):
        for ref in (pre, dys):
            ref[c, :guard, :] = jnp.zeros((guard, LANES), jnp.float32)
            ref[c, guard + rows :, :] = jnp.zeros((guard, LANES), jnp.float32)
    for index in range(len(widths)):
        fetch(0, index).wait()
        fetch(2, index).wait()

    for n in range(hidden // 256):
        value = jnp.dot(
            x_vmem[...], weight_in[:, 256 * n : 256 * n + 256], preferred_element_type=jnp.float32
        )
        for h in range(2):
            pre[2 * n + h, guard : guard + rows, :] = value[:, LANES * h : LANES * h + LANES]

    starts = [dil * (PC * a + b) for a, b in OFFSETS]

    def column_sums(source, c, row, count, sign):
        column = slice(LANES * c, LANES * c + LANES)
        sums = []
        for b in range(3):
            total = None
            for k in (b, 3 + b, 6 + b):
                at = guard + row + sign * starts[k]
                term = source[c, pl.ds(at, count), :] * taps[k, :, column]
                total = term if total is None else total + term
            sums.append(total)
        return sums

    def forward(row, count):
        low, high = after[pl.ds(row, count), :], before[pl.ds(row, count), :]
        for c in range(chunks):
            sums = column_sums(pre, c, row, count, 1)
            act, grad = gelu_parts(sums[1] + low * sums[0] + high * sums[2])
            slope[c, pl.ds(row, count), :] = grad
            hid[pl.ds(row, count), LANES * c : LANES * c + LANES] = act.astype(jnp.bfloat16)

    def run(step, body):
        whole = rows // step

        @pl.loop(0, whole)
        def _(i):
            body(pl.multiple_of(i * step, step), step)

        if rows > whole * step:
            body(whole * step, rows - whole * step)

    run(FORWARD_STEP, forward)

    logits = lax.dot_general(
        hid[...], weight_out[...], (((1,), (1,)), ((), ())), preferred_element_type=jnp.float32
    )
    lane = lax.broadcasted_iota(jnp.int32, logits.shape, 1)
    logits = jnp.where(lane < sizes.classes, logits, -1e30)
    peak = jnp.max(logits, axis=1, keepdims=True)
    power = jnp.exp(logits - peak)
    prob = power / jnp.sum(power, axis=1, keepdims=True)
    dlog[...] = (prob - onehot[...].astype(jnp.float32)).astype(jnp.bfloat16)

    gout[...] = lax.dot_general(
        dlog[...], hid[...], (((0,), (0,)), ((), ())), preferred_element_type=jnp.float32
    )
    for n in range(hidden // 256):
        value = jnp.dot(
            dlog[...], weight_out[:, 256 * n : 256 * n + 256], preferred_element_type=jnp.float32
        )
        for h in range(2):
            c = 2 * n + h
            dys[c, guard : guard + rows, :] = value[:, LANES * h : LANES * h + LANES] * slope[c]

    def fold(value):
        return jnp.sum(value.reshape(-1, 8, LANES), axis=0)

    biggest = jnp.zeros((8, LANES), jnp.float32)
    taps_biggest = jnp.zeros((1, LANES), jnp.float32)
    small[...] = jnp.zeros(small.shape, jnp.float32)
    taps_square = jnp.zeros((1, LANES), jnp.float32)
    for c in range(chunks):
        column = slice(LANES * c, LANES * c + LANES)

        def backward(row, count, carry):
            sums, top = carry
            low, high = after[pl.ds(row, count), :], before[pl.ds(row, count), :]
            dy = dys[c, pl.ds(guard + row, count), :]
            masked = (dy * low, dy, dy * high)
            out = [
                sums[k] + fold(masked[k % 3] * pre[c, pl.ds(guard + row + starts[k], count), :])
                for k in range(9)
            ]
            back = column_sums(dys, c, row, count, -1)
            total = back[1] + high * back[0] + low * back[2]
            dpre_out[pl.ds(row, count), column] = total.astype(jnp.bfloat16)
            size = jnp.max(jnp.abs(total).reshape(-1, 8, LANES), axis=0)
            return tuple(out), jnp.maximum(top, size)

        zeros = tuple(jnp.zeros((8, LANES), jnp.float32) for _ in range(9))
        step = BACKWARD_STEP
        whole = rows // step
        carry = lax.fori_loop(
            0,
            whole,
            lambda i, carry, step=step: backward(pl.multiple_of(i * step, step), step, carry),
            (zeros, biggest),
        )
        if rows > whole * step:
            carry = backward(whole * step, rows - whole * step, carry)
        sums, biggest = carry
        for k in range(9):
            value = jnp.sum(sums[k], axis=0, keepdims=True)
            taps_square = taps_square + value * value
            taps_biggest = jnp.maximum(taps_biggest, jnp.abs(value))
            small[k : k + 1, column] = value
    powers = (
        exponent(jnp.max(biggest) * (X_LIMIT * rows)),
        exponent(jnp.max(jnp.abs(gout[...]))),
        exponent(jnp.max(taps_biggest)),
    )
    for c in range(chunks):
        for i, power in enumerate(powers):
            small[9 + i : 10 + i, LANES * c : LANES * c + LANES] = power
    small[16:17, :LANES] = taps_square
    small[17:18, :] = jnp.sum(gout[...] * gout[...], axis=0, keepdims=True)
    if first.shape[0] == sizes.message:
        norm = message(sizes, scalars[3], x_vmem, dpre_out, gout, small, first, True)
        norm = norm + message(sizes, scalars[4], x_vmem, dpre_out, gout, small, early, True)
        small[18:19, :LANES] = norm


def message(sizes, place, x, dpre, gout, small, out, scaled):
    depth, depth_out = sizes.depth, sizes.depth_out
    column = pl.multiple_of(place * depth, LANES)
    block = lax.dot_general(
        x[:, pl.ds(column, depth)], dpre[...], (((0,), (0,)), ((), ())), preferred_element_type=jnp.float32
    )
    hidden = block.shape[1]
    chunks = hidden // LANES
    norm = jnp.sum(block * block, axis=0, keepdims=True)
    norm = sum(norm[:, LANES * c : LANES * c + LANES] for c in range(chunks))
    factors = [jnp.exp2(small[9 + i : 10 + i, :]) if scaled else 1.0 for i in range(3)]
    out[:depth, :] = block * factors[0]
    out[depth:, :] = jnp.zeros((out.shape[0] - depth, hidden), jnp.float32)
    column = pl.multiple_of(place * depth_out, LANES)
    for start, group in sizes.groups:
        value = gout[start : start + group, pl.ds(column, depth_out)]
        lane = start // sizes.group * LANES
        factor = factors[1][:, :LANES] if scaled else 1.0
        out[depth : depth + group, lane : lane + LANES] = value * factor
    row = depth + sizes.group
    out[row : row + 9, :] = small[0:9, :] * factors[2]
    if scaled:
        out[row + 9 : row + 12, :] = small[9:12, :]
    return norm


class Sizes:
    def __init__(self, wide, hidden, classes, dp):
        self.classes = classes
        self.depth = wide // dp
        self.depth_out = hidden // dp
        self.chunks = hidden // LANES
        self.class_rows = (classes + 7) // 8 * 8
        self.group = (self.class_rows // self.chunks + 7) // 8 * 8
        self.groups = [
            (at, min(self.group, self.class_rows - at)) for at in range(0, self.class_rows, self.group)
        ]
        self.message = self.depth + self.group + 16
        self.staged = dp == 4 and self.depth % LANES == 0 and self.depth_out == LANES


def head_backward(sizes, widths, scalars, halves, onehot, weight_in, taps, weight_out, masks):
    rows = onehot.shape[0]
    wide, hidden = weight_in.shape
    chunks = hidden // LANES
    vmem = pl.BlockSpec(memory_space=pltpu.VMEM)
    anywhere = pl.BlockSpec(memory_space=pl.ANY)
    span = 2 * REACH * (PC + 1) + rows
    return pl.pallas_call(
        functools.partial(head_kernel, sizes, widths),
        out_shape=[
            jax.ShapeDtypeStruct((rows, wide), jnp.bfloat16),
            jax.ShapeDtypeStruct((rows, hidden), jnp.bfloat16),
            jax.ShapeDtypeStruct((256, hidden), jnp.float32),
            jax.ShapeDtypeStruct((24, hidden), jnp.float32),
        ]
        + [jax.ShapeDtypeStruct((sizes.message if sizes.staged else 8, hidden), jnp.float32)] * 2,
        in_specs=[pl.BlockSpec(memory_space=pltpu.SMEM)] + [anywhere] * len(halves) + [vmem] * 6,
        out_specs=[vmem] * 6,
        scratch_shapes=[
            pltpu.VMEM((chunks, span, LANES), jnp.float32),
            pltpu.VMEM((chunks, span, LANES), jnp.float32),
            pltpu.VMEM((chunks, rows, LANES), jnp.float32),
            pltpu.VMEM((rows, hidden), jnp.bfloat16),
            pltpu.VMEM((rows, 256), jnp.bfloat16),
            pltpu.SemaphoreType.DMA((len(widths), 2)),
        ],
        compiler_params=pltpu.CompilerParams(vmem_limit_bytes=24 * 1024 * 1024),
        name="head",
    )(scalars, *halves, weight_in, taps, weight_out, onehot, *masks)


def blocks_kernel(sizes, scalars, x, dpre, gout, small, late, own, stats):
    norm = message(sizes, scalars[5], x, dpre, gout, small, late, True)
    norm = norm + message(sizes, scalars[6], x, dpre, gout, small, own, False)
    stats[...] = jnp.zeros(stats.shape, jnp.float32)
    stats[0:1, :] = norm + small[18:19, :LANES]
    stats[1:2, :] = small[16:17, :LANES]
    for c in range(sizes.chunks):
        stats[2 + c : 3 + c, :] = small[17:18, LANES * c : LANES * c + LANES]


def totals(sizes, parts, last):
    mark = sizes.depth + sizes.group
    spans = ((0, sizes.depth), (sizes.depth, mark), (mark, mark + 9))
    return [
        parts[start:stop, :] + last[start:stop, :] * jnp.exp2(-last[mark + 9 + i : mark + 10 + i, :])
        for i, (start, stop) in enumerate(spans)
    ]


def line_kernel(sizes, parts, last, stats, line):
    def fold(value):
        value = jnp.sum(value.reshape(-1, 8, value.shape[1]), axis=0)
        return sum(value[:, LANES * c : LANES * c + LANES] for c in range(sizes.chunks))

    sum_in, sum_out, sum_taps = totals(sizes, parts, last)
    line[0:8, :] = fold(sum_in * sum_in)
    line[8:16, :] = fold(sum_out * sum_out)
    line[16:24, :] = stats[...]
    line[24:32, :] = jnp.zeros((8, LANES), jnp.float32)
    square = jnp.sum(sum_taps * sum_taps, axis=0, keepdims=True)
    line[24:25, :] = sum(square[:, LANES * c : LANES * c + LANES] for c in range(sizes.chunks))


def sum_kernel(sizes, parts, last, share_in, share_out, taps_out):
    sum_in, sum_out, sum_taps = totals(sizes, parts, last)
    share_in[...] = sum_in
    for start, group in sizes.groups:
        lane = start // sizes.group * LANES
        count = min(group, sizes.classes - start)
        share_out[start : start + count, 0, :] = sum_out[:count, lane : lane + LANES]
    for k in range(9):
        taps_out[k, :, :] = sum_taps[k : k + 1, :]


def norm_kernel(chunks, *refs):
    lines, out = refs[:-1], refs[-1]
    total = sum(line[...] for line in lines)
    line = lines[0]
    values = [
        jnp.sum(total[16:17, :]),
        jnp.sum(total[17:18, :]),
        jnp.sum(total[18 : 18 + chunks, :]),
        jnp.sum(total[0:8, :]),
        jnp.sum(line[24:25, :]),
        jnp.sum(total[8:16, :]),
    ]
    row = lax.broadcasted_iota(jnp.int32, (8, LANES), 0)
    lane = lax.broadcasted_iota(jnp.int32, (8, LANES), 1)
    spread = jnp.zeros((8, LANES), jnp.float32)
    for i, value in enumerate(values):
        spread = jnp.where((row == i // 3) & (lane == i % 3), value, spread)
    out[...] = jnp.log(1e-12 + spread)[:2, :3]


def permute(value, pairs):
    return lax.ppermute(value, "dp", pairs)


def add_kernel(sizes, scalars, mine, theirs, out):
    depth, group = sizes.depth, sizes.group
    mark = depth + group
    end = (scalars[6] == 0) | (scalars[6] == 3)

    @pl.when(end)
    def _():
        out[...] = mine[...]

    @pl.when(jnp.logical_not(end))
    def _():
        for i, (start, stop) in enumerate(((0, depth), (depth, mark), (mark, mark + 9))):
            at = mark + 9 + i
            a, b = mine[at : at + 1, :], theirs[at : at + 1, :]
            common = jnp.minimum(a, b)
            out[start:stop, :] = mine[start:stop, :] * jnp.exp2(common - a) + theirs[
                start:stop, :
            ] * jnp.exp2(common - b)
            out[at : at + 1, :] = common
        out[mark + 12 :, :] = mine[mark + 12 :, :]


def by_row(sizes, shape, three):
    row = lax.broadcasted_iota(jnp.int32, shape, 0)
    return jnp.where(
        row < sizes.depth, three[0], jnp.where(row < sizes.depth + sizes.group, three[1], three[2])
    )


def staged_sums(sizes, me, scalars, xrows, dpre, gout, small, first, early):
    vmem = pl.BlockSpec(memory_space=pltpu.VMEM)
    smem = pl.BlockSpec(memory_space=pltpu.SMEM)
    hidden = dpre.shape[1]
    shape = (sizes.message, hidden)
    full = jax.ShapeDtypeStruct(shape, jnp.float32)
    lines = jax.ShapeDtypeStruct((8, LANES), jnp.float32)
    half = jnp.float16
    near = permute(first.astype(half), [(0, 1), (1, 0), (2, 3), (3, 2)])
    early = early.astype(half)
    middle = permute(early, [(1, 2), (2, 1)])
    late, own, stats = pl.pallas_call(
        functools.partial(blocks_kernel, sizes),
        out_shape=[full, full, lines],
        in_specs=[smem] + [vmem] * 4,
        out_specs=[vmem] * 3,
        compiler_params=pltpu.CompilerParams(vmem_limit_bytes=16 * 1024 * 1024),
        cost_estimate=pl.CostEstimate(
            flops=4 * sizes.depth * dpre.shape[0] * hidden,
            bytes_accessed=2 * xrows.size + 2 * dpre.size + 8 * sizes.message * hidden,
            transcendentals=0,
        ),
        name="blocks",
    )(scalars, xrows, dpre, gout, small)
    end = (me == 0) | (me == 3)
    mark = sizes.depth + sizes.group + 9
    both = pl.pallas_call(
        functools.partial(add_kernel, sizes),
        out_shape=full,
        in_specs=[smem, vmem, vmem],
        out_specs=vmem,
        compiler_params=pltpu.CompilerParams(vmem_limit_bytes=8 * 1024 * 1024),
        name="add",
    )(scalars, late, near.astype(jnp.float32))
    both = both.astype(half)
    far = permute(both, [(0, 1), (3, 2), (1, 3), (2, 0)])
    early, _ = lax.optimization_barrier((early, both))
    near, middle, _ = lax.optimization_barrier((near, middle, both))
    skip = permute(early, [(0, 2), (3, 1)])

    def split(value):
        return [value[mark + i : mark + i + 1] for i in range(3)]


    def decode(value):
        value = value.astype(jnp.float32)
        return value * by_row(sizes, shape, [jnp.exp2(-v) for v in split(value)])

    parts = own + decode(jnp.where(end, near, middle)) + decode(skip)
    return parts, far.astype(jnp.float32), stats


def per_device(sizes, dp, trials, features, owner, dilation_index, labels, input_weight, taps, output_weight):
    here, core, widths, halves = pieces(features[0, 0], "trial", trials, owner[0])
    me = lax.axis_index("dp")
    dil = dilation_index[0] + 1
    rows = features.shape[2]
    onehot = (labels[0][:, None] == jnp.arange(256, dtype=jnp.int32)[None, :]).astype(jnp.bfloat16)
    column = lax.broadcasted_iota(jnp.int32, (rows, LANES), 0) % PC
    before = (column < PC - dil).astype(jnp.float32)
    after = (column >= dil).astype(jnp.float32)
    classes, chunks = sizes.classes, sizes.chunks
    weight_out = jnp.pad(output_weight[0].T, ((0, 256 - classes), (0, 0)))
    high = me >= 2
    odd = me % 2
    end = (me == 0) | (me == 3)
    step, jump = jnp.where(odd == 0, 1, 2), jnp.where(high, me - 2, me + 2)
    to = [3 * (1 - odd), jnp.where(end, jump, step), jnp.where(end, step, jump), me]
    scalars = jnp.stack([dil, here, core] + to).astype(jnp.int32)
    xrows, dpre, gout, small, first, early = head_backward(
        sizes,
        widths,
        scalars,
        halves,
        onehot,
        input_weight[0],
        taps[0][:, None, :],
        weight_out,
        (after, before),
    )
    if not sizes.staged:
        return general_sums(sizes, xrows, dpre, gout, small)
    parts, last, stats = staged_sums(sizes, me, scalars, xrows, dpre, gout, small, first, early)
    vmem = pl.BlockSpec(memory_space=pltpu.VMEM)
    hidden = dpre.shape[1]
    small = pltpu.CompilerParams(vmem_limit_bytes=8 * 1024 * 1024)
    line = pl.pallas_call(
        functools.partial(line_kernel, sizes),
        out_shape=jax.ShapeDtypeStruct((32, LANES), jnp.float32),
        in_specs=[vmem] * 3,
        out_specs=vmem,
        compiler_params=small,
        name="line",
    )(parts, last, stats)
    lines = [line] + [permute(line, [(i, i ^ s) for i in range(dp)]) for s in (3, 2, 1)]
    share_in, share_out, total_taps = pl.pallas_call(
        functools.partial(sum_kernel, sizes),
        out_shape=[
            jax.ShapeDtypeStruct((sizes.depth, hidden), jnp.float32),
            jax.ShapeDtypeStruct((classes, 1, sizes.depth_out), jnp.float32),
            jax.ShapeDtypeStruct((9, 1, hidden), jnp.float32),
        ],
        in_specs=[vmem] * 2,
        out_specs=[vmem] * 3,
        compiler_params=small,
        cost_estimate=pl.CostEstimate(
            flops=2 * parts.size, bytes_accessed=16 * parts.size, transcendentals=0
        ),
        name="sums",
    )(parts, last)
    norms = pl.pallas_call(
        functools.partial(norm_kernel, chunks),
        out_shape=jax.ShapeDtypeStruct((2, 3), jnp.float32),
        in_specs=[vmem] * dp,
        out_specs=vmem,
        compiler_params=pltpu.CompilerParams(vmem_limit_bytes=4 * 1024 * 1024),
        name="norms",
    )(*lines)
    share_out = jnp.transpose(share_out, (1, 2, 0))
    return (share_in[None], jnp.transpose(total_taps, (1, 0, 2)), share_out, norms[None])


def general_sums(sizes, xrows, dpre, gout, small):
    g_in = jnp.dot(xrows.T, dpre, preferred_element_type=jnp.float32)
    g_out = gout[: sizes.classes].T
    g_taps = small[:9]
    share_in = lax.psum_scatter(g_in, "dp", scatter_dimension=0, tiled=True)
    share_out = lax.psum_scatter(g_out, "dp", scatter_dimension=0, tiled=True)
    local = jnp.stack([jnp.sum(g_in * g_in), jnp.sum(g_taps * g_taps), jnp.sum(g_out * g_out)])
    share_sq = jnp.stack([jnp.sum(share_in * share_in), jnp.sum(share_out * share_out)])
    total_taps, squares, share_total = lax.psum((g_taps, local, share_sq), "dp")
    totals = jnp.stack([share_total[0], jnp.sum(total_taps * total_taps), share_total[1]])
    norms = jnp.log(1e-12 + jnp.stack([squares, totals]))
    return (share_in[None], total_taps[None], share_out[None], norms[None])


def solution(mesh):
    dp, trials = mesh.shape["dp"], mesh.shape["trial"]
    placed = (
        P(("groups", "dp"), "trial", None, None),
        P(("groups", "dp")),
        P("trial"),
        P(("groups", "dp"), None),
        P("trial", None, None),
        P("trial", None, None),
        P("trial", None, None),
    )

    def step(*args):
        (wide, hidden), classes = args[4].shape[1:], args[6].shape[2]
        return per_device(Sizes(wide, hidden, classes, dp), dp, trials, *args)

    return jax.shard_map(
        step,
        mesh=mesh,
        in_specs=placed,
        out_specs=(
            P(("groups", "trial"), "dp", None),
            P(("groups", "trial"), None, None),
            P(("groups", "trial"), "dp", None),
            P(("groups", "trial"), None, None),
        ),
        check_vma=False,
    )
```

```python
import functools
import math

import jax
import jax.numpy as jnp
from jax import lax
from jax.experimental import pallas as pl
from jax.experimental.pallas import tpu as pltpu
from jax.sharding import PartitionSpec as P

PC = 37
LANES = 128
FORWARD_STEP = 64
BACKWARD_STEP = 64
REACH = 4
OFFSETS = [(a, b) for a in (-1, 0, 1) for b in (-1, 0, 1)]
X_LIMIT = 6.0
OTHER_REFS = 18
ROOM = 16384.0


def pieces(block, axis, size, source):
    wide = block.shape[1]
    if size != 4:
        block = jnp.where(lax.axis_index(axis) == source, block, jnp.zeros_like(block))
        block = lax.psum(block, axis)
        low, high = block[:, : wide // 2], block[:, wide // 2 :]
        zero = jnp.int32(0)
        return zero, zero, (wide // 2,), (low, low, high, high)
    me = lax.axis_index(axis)
    core = me % 2
    mate = [(0, 1), (1, 0), (2, 3), (3, 2)]
    across = [(0, 2), (2, 0), (1, 3), (3, 1)]
    widths, width = split_width(wide)
    shared = block[:, 2 * width :]
    shared_other = lax.ppermute(shared, axis, across)
    got = lax.ppermute(jnp.where(core == 0, block[:, width : 2 * width], block[:, :width]), axis, mate)
    values = []
    at = 0
    for piece in widths:
        if at:
            block, shared_other, _ = lax.optimization_barrier((block, shared_other, values[0]))
        low, high = block[:, at : at + piece], block[:, width + at : width + at + piece]
        kept = jnp.where(core == 0, low, high)
        held = jnp.where(source % 2 == core, kept, got[:, at : at + piece])
        other = lax.ppermute(held, axis, across)
        values += [held, other, lax.ppermute(held, axis, mate), lax.ppermute(other, axis, mate)]
        at += piece
    values += [shared, lax.ppermute(shared, axis, mate)]
    values += [shared_other, lax.ppermute(shared_other, axis, mate)]
    return (source ^ me).astype(jnp.int32), core, widths, tuple(values)


def split_width(wide):
    tiles = wide // LANES
    half = (tiles - 2) // 2
    last = max(half * 2 // 5, 1)
    return tuple(LANES * n for n in (half - last, last) if n > 0), LANES * half


def gelu_parts(value):
    square = value * value
    half = 0.5 + 0.5 * jnp.tanh(value * (0.7978845608 + (0.7978845608 * 0.044715) * square))
    out_val = value * half
    rate = 2.0 * 0.7978845608 + (6.0 * 0.7978845608 * 0.044715) * square
    return (out_val, half + out_val * (1.0 - half) * rate)


def exponent(size):
    size = jnp.maximum(jnp.full((1, LANES), size, jnp.float32), 1e-30)
    return jnp.clip(jnp.floor(jnp.log(ROOM / size) * (1.0 / math.log(2.0))), -100.0, 100.0)


def head_kernel(
    sizes,
    widths,
    scalars,
    *refs,
):
    count = len(refs) - OTHER_REFS
    halves, refs = refs[:count], refs[count:]
    shared = halves[4 * len(widths) :]
    weight_in, taps, weight_out, onehot, after, before = refs[:6]
    x_vmem, dpre_out, gout, small, first, early = refs[6:12]
    pre, dys, slope, hid, dlog, sem_in = refs[12:]
    rows = x_vmem.shape[0]
    width = sum(widths)
    hidden = weight_in.shape[1]
    chunks = hidden // LANES
    guard = REACH * (PC + 1)
    dil, where, core = scalars[0], scalars[1], scalars[2]

    def fetch(kind, index):
        column = (core if kind < 2 else 1 - core) * width + sum(widths[:index])
        target = x_vmem.at[:, pl.ds(pl.multiple_of(column, LANES), widths[index])]
        return pltpu.make_async_copy(halves[4 * index + kind], target, sem_in.at[index, kind // 2])

    def fetch_shared(kind):
        return pltpu.make_async_copy(shared[kind], x_vmem.at[:, 2 * width :], sem_in.at[len(widths), 0])

    for kind in range(4):

        @pl.when(where == kind)
        def _(kind=kind):
            for index in range(len(widths)):
                fetch(kind // 2, index).start()
                fetch(2 + kind // 2, index).start()
            if shared:
                fetch_shared(kind).start()

    for c in range(chunks):
        for ref in (pre, dys):
            ref[c, :guard, :] = jnp.zeros((guard, LANES), jnp.float32)
            ref[c, guard + rows :, :] = jnp.zeros((guard, LANES), jnp.float32)
    for index in range(len(widths)):
        fetch(0, index).wait()
        fetch(2, index).wait()
    if shared:
        fetch_shared(0).wait()

    for n in range(hidden // 256):
        value = jnp.dot(
            x_vmem[...], weight_in[:, 256 * n : 256 * n + 256], preferred_element_type=jnp.float32
        )
        for h in range(2):
            pre[2 * n + h, guard : guard + rows, :] = value[:, LANES * h : LANES * h + LANES]

    starts = [dil * (PC * a + b) for a, b in OFFSETS]

    def column_sums(source, c, row, count, sign):
        column = slice(LANES * c, LANES * c + LANES)
        sums = []
        for b in range(3):
            total = None
            for k in (b, 3 + b, 6 + b):
                at = guard + row + sign * starts[k]
                term = source[c, pl.ds(at, count), :] * taps[k, :, column]
                total = term if total is None else total + term
            sums.append(total)
        return sums

    def forward(row, count):
        low, high = after[pl.ds(row, count), :], before[pl.ds(row, count), :]
        for c in range(chunks):
            sums = column_sums(pre, c, row, count, 1)
            act, grad = gelu_parts(sums[1] + low * sums[0] + high * sums[2])
            slope[c, pl.ds(row, count), :] = grad
            hid[pl.ds(row, count), LANES * c : LANES * c + LANES] = act.astype(jnp.bfloat16)

    def run(step, body):
        whole = rows // step

        @pl.loop(0, whole)
        def _(i):
            body(pl.multiple_of(i * step, step), step)

        if rows > whole * step:
            body(whole * step, rows - whole * step)

    run(FORWARD_STEP, forward)

    logits = lax.dot_general(
        hid[...], weight_out[...], (((1,), (1,)), ((), ())), preferred_element_type=jnp.float32
    )
    lane = lax.broadcasted_iota(jnp.int32, logits.shape, 1)
    logits = jnp.where(lane < sizes.classes, logits, -1e30)
    peak = jnp.max(logits, axis=1, keepdims=True)
    power = jnp.exp(logits - peak)
    prob = power / jnp.sum(power, axis=1, keepdims=True)
    dlog[...] = (prob - onehot[...].astype(jnp.float32)).astype(jnp.bfloat16)

    gout[...] = lax.dot_general(
        dlog[...], hid[...], (((0,), (0,)), ((), ())), preferred_element_type=jnp.float32
    )
    for n in range(hidden // 256):
        value = jnp.dot(
            dlog[...], weight_out[:, 256 * n : 256 * n + 256], preferred_element_type=jnp.float32
        )
        for h in range(2):
            c = 2 * n + h
            dys[c, guard : guard + rows, :] = value[:, LANES * h : LANES * h + LANES] * slope[c]

    def fold(value):
        return jnp.sum(value.reshape(-1, 8, LANES), axis=0)

    biggest = jnp.zeros((8, LANES), jnp.float32)
    taps_biggest = jnp.zeros((1, LANES), jnp.float32)
    small[...] = jnp.zeros(small.shape, jnp.float32)
    taps_square = jnp.zeros((1, LANES), jnp.float32)
    for c in range(chunks):
        column = slice(LANES * c, LANES * c + LANES)

        def backward(row, count, carry):
            sums, top = carry
            low, high = after[pl.ds(row, count), :], before[pl.ds(row, count), :]
            dy = dys[c, pl.ds(guard + row, count), :]
            masked = (dy * low, dy, dy * high)
            out = [
                sums[k] + fold(masked[k % 3] * pre[c, pl.ds(guard + row + starts[k], count), :])
                for k in range(9)
            ]
            back = column_sums(dys, c, row, count, -1)
            total = back[1] + high * back[0] + low * back[2]
            dpre_out[pl.ds(row, count), column] = total.astype(jnp.bfloat16)
            size = jnp.max(jnp.abs(total).reshape(-1, 8, LANES), axis=0)
            return tuple(out), jnp.maximum(top, size)

        zeros = tuple(jnp.zeros((8, LANES), jnp.float32) for _ in range(9))
        step = BACKWARD_STEP
        whole = rows // step
        carry = lax.fori_loop(
            0,
            whole,
            lambda i, carry, step=step: backward(pl.multiple_of(i * step, step), step, carry),
            (zeros, biggest),
        )
        if rows > whole * step:
            carry = backward(whole * step, rows - whole * step, carry)
        sums, biggest = carry
        for k in range(9):
            value = jnp.sum(sums[k], axis=0, keepdims=True)
            taps_square = taps_square + value * value
            taps_biggest = jnp.maximum(taps_biggest, jnp.abs(value))
            small[k : k + 1, column] = value
    powers = (
        exponent(jnp.max(biggest) * (X_LIMIT * rows)),
        exponent(jnp.max(jnp.abs(gout[...]))),
        exponent(jnp.max(taps_biggest)),
    )
    for c in range(chunks):
        for i, power in enumerate(powers):
            small[9 + i : 10 + i, LANES * c : LANES * c + LANES] = power
    small[16:17, :LANES] = taps_square
    small[17:18, :] = jnp.sum(gout[...] * gout[...], axis=0, keepdims=True)
    if first.shape[0] == sizes.message:
        norm = message(sizes, scalars[3], x_vmem, dpre_out, gout, small, first, True)
        norm = norm + message(sizes, scalars[4], x_vmem, dpre_out, gout, small, early, True)
        small[18:19, :LANES] = norm


def message(sizes, place, x, dpre, gout, small, out, scaled):
    depth, depth_out = sizes.depth, sizes.depth_out
    column = pl.multiple_of(place * depth, LANES)
    block = lax.dot_general(
        x[:, pl.ds(column, depth)], dpre[...], (((0,), (0,)), ((), ())), preferred_element_type=jnp.float32
    )
    hidden = block.shape[1]
    chunks = hidden // LANES
    norm = jnp.sum(block * block, axis=0, keepdims=True)
    norm = sum(norm[:, LANES * c : LANES * c + LANES] for c in range(chunks))
    factors = [jnp.exp2(small[9 + i : 10 + i, :]) if scaled else 1.0 for i in range(3)]
    out[:depth, :] = block * factors[0]
    out[depth:, :] = jnp.zeros((out.shape[0] - depth, hidden), jnp.float32)
    column = pl.multiple_of(place * depth_out, LANES)
    for start, group in sizes.groups:
        value = gout[start : start + group, pl.ds(column, depth_out)]
        lane = start // sizes.group * LANES
        factor = factors[1][:, :LANES] if scaled else 1.0
        out[depth : depth + group, lane : lane + LANES] = value * factor
    row = depth + sizes.group
    out[row : row + 9, :] = small[0:9, :] * factors[2]
    if scaled:
        out[row + 9 : row + 12, :] = small[9:12, :]
    return norm


class Sizes:
    def __init__(self, wide, hidden, classes, dp):
        self.classes = classes
        self.depth = wide // dp
        self.depth_out = hidden // dp
        self.chunks = hidden // LANES
        self.class_rows = (classes + 7) // 8 * 8
        self.group = (self.class_rows // self.chunks + 7) // 8 * 8
        self.groups = [
            (at, min(self.group, self.class_rows - at)) for at in range(0, self.class_rows, self.group)
        ]
        self.message = self.depth + self.group + 16
        self.staged = dp == 4 and self.depth % LANES == 0 and self.depth_out == LANES


def head_backward(sizes, widths, scalars, halves, onehot, weight_in, taps, weight_out, masks):
    rows = onehot.shape[0]
    wide, hidden = weight_in.shape
    chunks = hidden // LANES
    vmem = pl.BlockSpec(memory_space=pltpu.VMEM)
    anywhere = pl.BlockSpec(memory_space=pl.ANY)
    span = 2 * REACH * (PC + 1) + rows
    return pl.pallas_call(
        functools.partial(head_kernel, sizes, widths),
        out_shape=[
            jax.ShapeDtypeStruct((rows, wide), jnp.bfloat16),
            jax.ShapeDtypeStruct((rows, hidden), jnp.bfloat16),
            jax.ShapeDtypeStruct((256, hidden), jnp.float32),
            jax.ShapeDtypeStruct((24, hidden), jnp.float32),
        ]
        + [jax.ShapeDtypeStruct((sizes.message if sizes.staged else 8, hidden), jnp.float32)] * 2,
        in_specs=[pl.BlockSpec(memory_space=pltpu.SMEM)] + [anywhere] * len(halves) + [vmem] * 6,
        out_specs=[vmem] * 6,
        scratch_shapes=[
            pltpu.VMEM((chunks, span, LANES), jnp.float32),
            pltpu.VMEM((chunks, span, LANES), jnp.float32),
            pltpu.VMEM((chunks, rows, LANES), jnp.float32),
            pltpu.VMEM((rows, hidden), jnp.bfloat16),
            pltpu.VMEM((rows, 256), jnp.bfloat16),
            pltpu.SemaphoreType.DMA((len(widths) + 1, 2)),
        ],
        compiler_params=pltpu.CompilerParams(vmem_limit_bytes=24 * 1024 * 1024),
        name="head",
    )(scalars, *halves, weight_in, taps, weight_out, onehot, *masks)


def blocks_kernel(sizes, scalars, x, dpre, gout, small, late, own, stats):
    norm = message(sizes, scalars[5], x, dpre, gout, small, late, True)
    norm = norm + message(sizes, scalars[6], x, dpre, gout, small, own, False)
    stats[...] = jnp.zeros(stats.shape, jnp.float32)
    stats[0:1, :] = norm + small[18:19, :LANES]
    stats[1:2, :] = small[16:17, :LANES]
    for c in range(sizes.chunks):
        stats[2 + c : 3 + c, :] = small[17:18, LANES * c : LANES * c + LANES]


def totals(sizes, parts, last):
    mark = sizes.depth + sizes.group
    spans = ((0, sizes.depth), (sizes.depth, mark), (mark, mark + 9))
    return [
        parts[start:stop, :] + last[start:stop, :] * jnp.exp2(-last[mark + 9 + i : mark + 10 + i, :])
        for i, (start, stop) in enumerate(spans)
    ]


def line_kernel(sizes, parts, last, stats, line):
    def fold(value):
        value = jnp.sum(value.reshape(-1, 8, value.shape[1]), axis=0)
        return sum(value[:, LANES * c : LANES * c + LANES] for c in range(sizes.chunks))

    sum_in, sum_out, sum_taps = totals(sizes, parts, last)
    line[0:8, :] = fold(sum_in * sum_in)
    line[8:16, :] = fold(sum_out * sum_out)
    line[16:24, :] = stats[...]
    line[24:32, :] = jnp.zeros((8, LANES), jnp.float32)
    square = jnp.sum(sum_taps * sum_taps, axis=0, keepdims=True)
    line[24:25, :] = sum(square[:, LANES * c : LANES * c + LANES] for c in range(sizes.chunks))


def sum_kernel(sizes, parts, last, share_in, share_out, taps_out):
    sum_in, sum_out, sum_taps = totals(sizes, parts, last)
    share_in[...] = sum_in
    for start, group in sizes.groups:
        lane = start // sizes.group * LANES
        count = min(group, sizes.classes - start)
        share_out[start : start + count, 0, :] = sum_out[:count, lane : lane + LANES]
    for k in range(9):
        taps_out[k, :, :] = sum_taps[k : k + 1, :]


def norm_kernel(chunks, *refs):
    lines, out = refs[:-1], refs[-1]
    total = sum(line[...] for line in lines)
    line = lines[0]
    values = [
        jnp.sum(total[16:17, :]),
        jnp.sum(total[17:18, :]),
        jnp.sum(total[18 : 18 + chunks, :]),
        jnp.sum(total[0:8, :]),
        jnp.sum(line[24:25, :]),
        jnp.sum(total[8:16, :]),
    ]
    row = lax.broadcasted_iota(jnp.int32, (8, LANES), 0)
    lane = lax.broadcasted_iota(jnp.int32, (8, LANES), 1)
    spread = jnp.zeros((8, LANES), jnp.float32)
    for i, value in enumerate(values):
        spread = jnp.where((row == i // 3) & (lane == i % 3), value, spread)
    out[...] = jnp.log(1e-12 + spread)[:2, :3]


def permute(value, pairs):
    return lax.ppermute(value, "dp", pairs)


def add_kernel(sizes, scalars, mine, theirs, out):
    depth, group = sizes.depth, sizes.group
    mark = depth + group
    end = (scalars[6] == 0) | (scalars[6] == 3)

    @pl.when(end)
    def _():
        out[...] = mine[...]

    @pl.when(jnp.logical_not(end))
    def _():
        for i, (start, stop) in enumerate(((0, depth), (depth, mark), (mark, mark + 9))):
            at = mark + 9 + i
            a, b = mine[at : at + 1, :], theirs[at : at + 1, :]
            common = jnp.minimum(a, b)
            out[start:stop, :] = mine[start:stop, :] * jnp.exp2(common - a) + theirs[
                start:stop, :
            ] * jnp.exp2(common - b)
            out[at : at + 1, :] = common
        out[mark + 12 :, :] = mine[mark + 12 :, :]


def by_row(sizes, shape, three):
    row = lax.broadcasted_iota(jnp.int32, shape, 0)
    return jnp.where(
        row < sizes.depth, three[0], jnp.where(row < sizes.depth + sizes.group, three[1], three[2])
    )


def staged_sums(sizes, me, scalars, xrows, dpre, gout, small, first, early):
    vmem = pl.BlockSpec(memory_space=pltpu.VMEM)
    smem = pl.BlockSpec(memory_space=pltpu.SMEM)
    hidden = dpre.shape[1]
    shape = (sizes.message, hidden)
    full = jax.ShapeDtypeStruct(shape, jnp.float32)
    lines = jax.ShapeDtypeStruct((8, LANES), jnp.float32)
    half = jnp.float16
    near = permute(first.astype(half), [(0, 1), (1, 0), (2, 3), (3, 2)])
    early = early.astype(half)
    middle = permute(early, [(1, 2), (2, 1)])
    late, own, stats = pl.pallas_call(
        functools.partial(blocks_kernel, sizes),
        out_shape=[full, full, lines],
        in_specs=[smem] + [vmem] * 4,
        out_specs=[vmem] * 3,
        compiler_params=pltpu.CompilerParams(vmem_limit_bytes=16 * 1024 * 1024),
        cost_estimate=pl.CostEstimate(
            flops=4 * sizes.depth * dpre.shape[0] * hidden,
            bytes_accessed=2 * xrows.size + 2 * dpre.size + 8 * sizes.message * hidden,
            transcendentals=0,
        ),
        name="blocks",
    )(scalars, xrows, dpre, gout, small)
    end = (me == 0) | (me == 3)
    mark = sizes.depth + sizes.group + 9
    both = pl.pallas_call(
        functools.partial(add_kernel, sizes),
        out_shape=full,
        in_specs=[smem, vmem, vmem],
        out_specs=vmem,
        compiler_params=pltpu.CompilerParams(vmem_limit_bytes=8 * 1024 * 1024),
        name="add",
    )(scalars, late, near.astype(jnp.float32))
    both = both.astype(half)
    far = permute(both, [(0, 1), (3, 2), (1, 3), (2, 0)])
    early, _ = lax.optimization_barrier((early, both))
    near, middle, _ = lax.optimization_barrier((near, middle, both))
    skip = permute(early, [(0, 2), (3, 1)])

    def split(value):
        return [value[mark + i : mark + i + 1] for i in range(3)]


    def decode(value):
        value = value.astype(jnp.float32)
        return value * by_row(sizes, shape, [jnp.exp2(-v) for v in split(value)])

    parts = own + decode(jnp.where(end, near, middle)) + decode(skip)
    return parts, far.astype(jnp.float32), stats


def per_device(sizes, dp, trials, features, owner, dilation_index, labels, input_weight, taps, output_weight):
    where, core, widths, halves = pieces(features[0, 0], "trial", trials, owner[0])
    me = lax.axis_index("dp")
    dil = dilation_index[0] + 1
    rows = features.shape[2]
    onehot = (labels[0][:, None] == jnp.arange(256, dtype=jnp.int32)[None, :]).astype(jnp.bfloat16)
    column = lax.broadcasted_iota(jnp.int32, (rows, LANES), 0) % PC
    before = (column < PC - dil).astype(jnp.float32)
    after = (column >= dil).astype(jnp.float32)
    classes, chunks = sizes.classes, sizes.chunks
    weight_out = jnp.pad(output_weight[0].T, ((0, 256 - classes), (0, 0)))
    high = me >= 2
    odd = me % 2
    end = (me == 0) | (me == 3)
    step, jump = jnp.where(odd == 0, 1, 2), jnp.where(high, me - 2, me + 2)
    to = [3 * (1 - odd), jnp.where(end, jump, step), jnp.where(end, step, jump), me]
    scalars = jnp.stack([dil, where, core] + to).astype(jnp.int32)
    xrows, dpre, gout, small, first, early = head_backward(
        sizes,
        widths,
        scalars,
        halves,
        onehot,
        input_weight[0],
        taps[0][:, None, :],
        weight_out,
        (after, before),
    )
    if not sizes.staged:
        return general_sums(sizes, xrows, dpre, gout, small)
    parts, last, stats = staged_sums(sizes, me, scalars, xrows, dpre, gout, small, first, early)
    vmem = pl.BlockSpec(memory_space=pltpu.VMEM)
    hidden = dpre.shape[1]
    small = pltpu.CompilerParams(vmem_limit_bytes=8 * 1024 * 1024)
    line = pl.pallas_call(
        functools.partial(line_kernel, sizes),
        out_shape=jax.ShapeDtypeStruct((32, LANES), jnp.float32),
        in_specs=[vmem] * 3,
        out_specs=vmem,
        compiler_params=small,
        name="line",
    )(parts, last, stats)
    lines = [line] + [permute(line, [(i, i ^ s) for i in range(dp)]) for s in (3, 2, 1)]
    share_in, share_out, total_taps = pl.pallas_call(
        functools.partial(sum_kernel, sizes),
        out_shape=[
            jax.ShapeDtypeStruct((sizes.depth, hidden), jnp.float32),
            jax.ShapeDtypeStruct((classes, 1, sizes.depth_out), jnp.float32),
            jax.ShapeDtypeStruct((9, 1, hidden), jnp.float32),
        ],
        in_specs=[vmem] * 2,
        out_specs=[vmem] * 3,
        compiler_params=small,
        cost_estimate=pl.CostEstimate(
            flops=2 * parts.size, bytes_accessed=16 * parts.size, transcendentals=0
        ),
        name="sums",
    )(parts, last)
    norms = pl.pallas_call(
        functools.partial(norm_kernel, chunks),
        out_shape=jax.ShapeDtypeStruct((2, 3), jnp.float32),
        in_specs=[vmem] * dp,
        out_specs=vmem,
        compiler_params=pltpu.CompilerParams(vmem_limit_bytes=4 * 1024 * 1024),
        name="norms",
    )(*lines)
    share_out = jnp.transpose(share_out, (1, 2, 0))
    return (share_in[None], jnp.transpose(total_taps, (1, 0, 2)), share_out, norms[None])


def general_sums(sizes, xrows, dpre, gout, small):
    g_in = jnp.dot(xrows.T, dpre, preferred_element_type=jnp.float32)
    g_out = gout[: sizes.classes].T
    g_taps = small[:9]
    share_in = lax.psum_scatter(g_in, "dp", scatter_dimension=0, tiled=True)
    share_out = lax.psum_scatter(g_out, "dp", scatter_dimension=0, tiled=True)
    local = jnp.stack([jnp.sum(g_in * g_in), jnp.sum(g_taps * g_taps), jnp.sum(g_out * g_out)])
    share_sq = jnp.stack([jnp.sum(share_in * share_in), jnp.sum(share_out * share_out)])
    total_taps, squares, share_total = lax.psum((g_taps, local, share_sq), "dp")
    totals = jnp.stack([share_total[0], jnp.sum(total_taps * total_taps), share_total[1]])
    norms = jnp.log(1e-12 + jnp.stack([squares, totals]))
    return (share_in[None], total_taps[None], share_out[None], norms[None])


def solution(mesh):
    dp, trials = mesh.shape["dp"], mesh.shape["trial"]
    placed = (
        P(("groups", "dp"), "trial", None, None),
        P(("groups", "dp")),
        P("trial"),
        P(("groups", "dp"), None),
        P("trial", None, None),
        P("trial", None, None),
        P("trial", None, None),
    )

    def step(*args):
        (wide, hidden), classes = args[4].shape[1:], args[6].shape[2]
        return per_device(Sizes(wide, hidden, classes, dp), dp, trials, *args)

    return jax.shard_map(
        step,
        mesh=mesh,
        in_specs=placed,
        out_specs=(
            P(("groups", "trial"), "dp", None),
            P(("groups", "trial"), None, None),
            P(("groups", "trial"), "dp", None),
            P(("groups", "trial"), None, None),
        ),
        check_vma=False,
    )
```

```python
import functools
import math

import jax
import jax.numpy as jnp
from jax import lax
from jax.experimental import pallas as pl
from jax.experimental.pallas import tpu as pltpu
from jax.sharding import PartitionSpec as P

PC = 37
LANES = 128
FORWARD_STEP = 64
BACKWARD_STEP = 64
REACH = 4
OFFSETS = [(a, b) for a in (-1, 0, 1) for b in (-1, 0, 1)]
X_LIMIT = 6.0
OTHER_REFS = 18
ROOM = 16384.0


def pieces(block, axis, size, source):
    wide = block.shape[1]
    if size != 4:
        block = jnp.where(lax.axis_index(axis) == source, block, jnp.zeros_like(block))
        block = lax.psum(block, axis)
        low, high = block[:, : wide // 2], block[:, wide // 2 :]
        zero = jnp.int32(0)
        return zero, zero, (wide // 2,), (low, low, high, high)
    me = lax.axis_index(axis)
    core = me % 2
    mate = [(0, 1), (1, 0), (2, 3), (3, 2)]
    across = [(0, 2), (2, 0), (1, 3), (3, 1)]
    widths, width = split_width(wide)
    shared = block[:, 2 * width :]
    shared_other = lax.ppermute(shared, axis, across)
    got = lax.ppermute(jnp.where(core == 0, block[:, width : 2 * width], block[:, :width]), axis, mate)
    values = []
    at = 0
    for piece in widths:
        if at:
            block, shared_other, _ = lax.optimization_barrier((block, shared_other, values[0]))
        low, high = block[:, at : at + piece], block[:, width + at : width + at + piece]
        kept = jnp.where(core == 0, low, high)
        held = jnp.where(source % 2 == core, kept, got[:, at : at + piece])
        other = lax.ppermute(held, axis, across)
        values += [held, other, lax.ppermute(held, axis, mate), lax.ppermute(other, axis, mate)]
        at += piece
    values += [shared, lax.ppermute(shared, axis, mate)]
    values += [shared_other, lax.ppermute(shared_other, axis, mate)]
    return (source ^ me).astype(jnp.int32), core, widths, tuple(values)


def split_width(wide):
    tiles = wide // LANES
    half = (tiles - 2) // 2
    last = max(half * 2 // 5, 1)
    return tuple(LANES * n for n in (half - last, last) if n > 0), LANES * half


def gelu_parts(value):
    square = value * value
    half = 0.5 + 0.5 * jnp.tanh(value * (0.7978845608 + (0.7978845608 * 0.044715) * square))
    out_val = value * half
    rate = 2.0 * 0.7978845608 + (6.0 * 0.7978845608 * 0.044715) * square
    return (out_val, half + out_val * (1.0 - half) * rate)


def exponent(size):
    size = jnp.maximum(jnp.full((1, LANES), size, jnp.float32), 1e-30)
    return jnp.clip(jnp.floor(jnp.log(ROOM / size) * (1.0 / math.log(2.0))), -100.0, 100.0)


def head_kernel(
    sizes,
    widths,
    scalars,
    *refs,
):
    count = len(refs) - OTHER_REFS
    halves, refs = refs[:count], refs[count:]
    shared = halves[4 * len(widths) :]
    weight_in, taps, weight_out, onehot, after, before = refs[:6]
    x_vmem, dpre_out, gout, small, first, early = refs[6:12]
    pre, dys, slope, hid, dlog, sem_in = refs[12:]
    rows = x_vmem.shape[0]
    width = sum(widths)
    hidden = weight_in.shape[1]
    chunks = hidden // LANES
    guard = REACH * (PC + 1)
    dil, where, core = scalars[0], scalars[1], scalars[2]

    def fetch(kind, index):
        column = (core if kind < 2 else 1 - core) * width + sum(widths[:index])
        target = x_vmem.at[:, pl.ds(pl.multiple_of(column, LANES), widths[index])]
        return pltpu.make_async_copy(halves[4 * index + kind], target, sem_in.at[index, kind // 2])

    def fetch_shared(kind):
        return pltpu.make_async_copy(shared[kind], x_vmem.at[:, 2 * width :], sem_in.at[len(widths), 0])

    for kind in range(4):

        @pl.when(where == kind)
        def _(kind=kind):
            for index in range(len(widths)):
                fetch(kind // 2, index).start()
                fetch(2 + kind // 2, index).start()
            if shared:
                fetch_shared(kind).start()

    for c in range(chunks):
        for ref in (pre, dys):
            ref[c, :guard, :] = jnp.zeros((guard, LANES), jnp.float32)
            ref[c, guard + rows :, :] = jnp.zeros((guard, LANES), jnp.float32)
    for index in range(len(widths)):
        fetch(0, index).wait()
        fetch(2, index).wait()
    if shared:
        fetch_shared(0).wait()

    for n in range(hidden // 256):
        value = jnp.dot(
            x_vmem[...], weight_in[:, 256 * n : 256 * n + 256], preferred_element_type=jnp.float32
        )
        for h in range(2):
            pre[2 * n + h, guard : guard + rows, :] = value[:, LANES * h : LANES * h + LANES]

    starts = [dil * (PC * a + b) for a, b in OFFSETS]

    def column_sums(source, c, row, count, sign):
        column = slice(LANES * c, LANES * c + LANES)
        sums = []
        for b in range(3):
            total = None
            for k in (b, 3 + b, 6 + b):
                at = guard + row + sign * starts[k]
                term = source[c, pl.ds(at, count), :] * taps[k, :, column]
                total = term if total is None else total + term
            sums.append(total)
        return sums

    def forward(row, count):
        low, high = after[pl.ds(row, count), :], before[pl.ds(row, count), :]
        for c in range(chunks):
            sums = column_sums(pre, c, row, count, 1)
            act, grad = gelu_parts(sums[1] + low * sums[0] + high * sums[2])
            slope[c, pl.ds(row, count), :] = grad
            hid[pl.ds(row, count), LANES * c : LANES * c + LANES] = act.astype(jnp.bfloat16)

    def run(step, body):
        whole = rows // step

        @pl.loop(0, whole)
        def _(i):
            body(pl.multiple_of(i * step, step), step)

        if rows > whole * step:
            body(whole * step, rows - whole * step)

    run(FORWARD_STEP, forward)

    logits = lax.dot_general(
        hid[...], weight_out[...], (((1,), (1,)), ((), ())), preferred_element_type=jnp.float32
    )
    lane = lax.broadcasted_iota(jnp.int32, logits.shape, 1)
    logits = jnp.where(lane < sizes.classes, logits, -1e30)
    peak = jnp.max(logits, axis=1, keepdims=True)
    power = jnp.exp(logits - peak)
    prob = power / jnp.sum(power, axis=1, keepdims=True)
    dlog[...] = (prob - onehot[...].astype(jnp.float32)).astype(jnp.bfloat16)

    gout[...] = lax.dot_general(
        dlog[...], hid[...], (((0,), (0,)), ((), ())), preferred_element_type=jnp.float32
    )
    for n in range(hidden // 256):
        value = jnp.dot(
            dlog[...], weight_out[:, 256 * n : 256 * n + 256], preferred_element_type=jnp.float32
        )
        for h in range(2):
            c = 2 * n + h
            dys[c, guard : guard + rows, :] = value[:, LANES * h : LANES * h + LANES] * slope[c]

    def fold(value):
        return jnp.sum(value.reshape(-1, 8, LANES), axis=0)

    biggest = jnp.zeros((8, LANES), jnp.float32)
    taps_biggest = jnp.zeros((1, LANES), jnp.float32)
    small[...] = jnp.zeros(small.shape, jnp.float32)
    taps_square = jnp.zeros((1, LANES), jnp.float32)
    for c in range(chunks):
        column = slice(LANES * c, LANES * c + LANES)

        def backward(row, count, carry):
            sums, top = carry
            low, high = after[pl.ds(row, count), :], before[pl.ds(row, count), :]
            dy = dys[c, pl.ds(guard + row, count), :]
            masked = (dy * low, dy, dy * high)
            out = [
                sums[k] + fold(masked[k % 3] * pre[c, pl.ds(guard + row + starts[k], count), :])
                for k in range(9)
            ]
            back = column_sums(dys, c, row, count, -1)
            total = back[1] + high * back[0] + low * back[2]
            dpre_out[pl.ds(row, count), column] = total.astype(jnp.bfloat16)
            size = jnp.max(jnp.abs(total).reshape(-1, 8, LANES), axis=0)
            return tuple(out), jnp.maximum(top, size)

        zeros = tuple(jnp.zeros((8, LANES), jnp.float32) for _ in range(9))
        step = BACKWARD_STEP
        whole = rows // step
        carry = lax.fori_loop(
            0,
            whole,
            lambda i, carry, step=step: backward(pl.multiple_of(i * step, step), step, carry),
            (zeros, biggest),
        )
        if rows > whole * step:
            carry = backward(whole * step, rows - whole * step, carry)
        sums, biggest = carry
        for k in range(9):
            value = jnp.sum(sums[k], axis=0, keepdims=True)
            taps_square = taps_square + value * value
            taps_biggest = jnp.maximum(taps_biggest, jnp.abs(value))
            small[k : k + 1, column] = value
    powers = (
        exponent(jnp.max(biggest) * (X_LIMIT * rows)),
        exponent(jnp.max(jnp.abs(gout[...]))),
        exponent(jnp.max(taps_biggest)),
    )
    for c in range(chunks):
        for i, power in enumerate(powers):
            small[9 + i : 10 + i, LANES * c : LANES * c + LANES] = power
    small[16:17, :LANES] = taps_square
    small[17:18, :] = jnp.sum(gout[...] * gout[...], axis=0, keepdims=True)
    if first.shape[0] == sizes.message:
        norm = message(sizes, scalars[3], x_vmem, dpre_out, gout, small, first, True)
        norm = norm + message(sizes, scalars[4], x_vmem, dpre_out, gout, small, early, True)
        small[18:19, :LANES] = norm


def message(sizes, place, x, dpre, gout, small, out, scaled):
    depth, depth_out = sizes.depth, sizes.depth_out
    column = pl.multiple_of(place * depth, LANES)
    block = lax.dot_general(
        x[:, pl.ds(column, depth)], dpre[...], (((0,), (0,)), ((), ())), preferred_element_type=jnp.float32
    )
    hidden = block.shape[1]
    chunks = hidden // LANES
    norm = jnp.sum(block * block, axis=0, keepdims=True)
    norm = sum(norm[:, LANES * c : LANES * c + LANES] for c in range(chunks))
    factors = [jnp.exp2(small[9 + i : 10 + i, :]) if scaled else 1.0 for i in range(3)]
    out[:depth, :] = block * factors[0]
    out[depth:, :] = jnp.zeros((out.shape[0] - depth, hidden), jnp.float32)
    column = pl.multiple_of(place * depth_out, LANES)
    for start, group in sizes.groups:
        value = gout[start : start + group, pl.ds(column, depth_out)]
        lane = start // sizes.group * LANES
        factor = factors[1][:, :LANES] if scaled else 1.0
        out[depth : depth + group, lane : lane + LANES] = value * factor
    row = depth + sizes.group
    out[row : row + 9, :] = small[0:9, :] * factors[2]
    if scaled:
        out[row + 9 : row + 12, :] = small[9:12, :]
    return norm


class Sizes:
    def __init__(self, wide, hidden, classes, dp):
        self.classes = classes
        self.depth = wide // dp
        self.depth_out = hidden // dp
        self.chunks = hidden // LANES
        self.class_rows = (classes + 7) // 8 * 8
        self.group = (self.class_rows // self.chunks + 7) // 8 * 8
        self.groups = [
            (at, min(self.group, self.class_rows - at)) for at in range(0, self.class_rows, self.group)
        ]
        self.message = self.depth + self.group + 16
        self.staged = dp == 4 and self.depth % LANES == 0 and self.depth_out == LANES


def head_backward(sizes, widths, scalars, halves, onehot, weight_in, taps, weight_out, masks):
    rows = onehot.shape[0]
    wide, hidden = weight_in.shape
    chunks = hidden // LANES
    vmem = pl.BlockSpec(memory_space=pltpu.VMEM)
    anywhere = pl.BlockSpec(memory_space=pl.ANY)
    span = 2 * REACH * (PC + 1) + rows
    return pl.pallas_call(
        functools.partial(head_kernel, sizes, widths),
        out_shape=[
            jax.ShapeDtypeStruct((rows, wide), jnp.bfloat16),
            jax.ShapeDtypeStruct((rows, hidden), jnp.bfloat16),
            jax.ShapeDtypeStruct((256, hidden), jnp.float32),
            jax.ShapeDtypeStruct((24, hidden), jnp.float32),
        ]
        + [jax.ShapeDtypeStruct((sizes.message if sizes.staged else 8, hidden), jnp.float32)] * 2,
        in_specs=[pl.BlockSpec(memory_space=pltpu.SMEM)] + [anywhere] * len(halves) + [vmem] * 6,
        out_specs=[vmem] * 6,
        scratch_shapes=[
            pltpu.VMEM((chunks, span, LANES), jnp.float32),
            pltpu.VMEM((chunks, span, LANES), jnp.float32),
            pltpu.VMEM((chunks, rows, LANES), jnp.float32),
            pltpu.VMEM((rows, hidden), jnp.bfloat16),
            pltpu.VMEM((rows, 256), jnp.bfloat16),
            pltpu.SemaphoreType.DMA((len(widths) + 1, 2)),
        ],
        compiler_params=pltpu.CompilerParams(vmem_limit_bytes=24 * 1024 * 1024),
        name="head",
    )(scalars, *halves, weight_in, taps, weight_out, onehot, *masks)


def blocks_kernel(sizes, scalars, x, dpre, gout, small, late, own, stats):
    norm = message(sizes, scalars[5], x, dpre, gout, small, late, True)
    norm = norm + message(sizes, scalars[6], x, dpre, gout, small, own, False)
    stats[...] = jnp.zeros(stats.shape, jnp.float32)
    stats[0:1, :] = norm + small[18:19, :LANES]
    stats[1:2, :] = small[16:17, :LANES]
    for c in range(sizes.chunks):
        stats[2 + c : 3 + c, :] = small[17:18, LANES * c : LANES * c + LANES]


def totals(sizes, parts, last):
    mark = sizes.depth + sizes.group
    spans = ((0, sizes.depth), (sizes.depth, mark), (mark, mark + 9))
    return [
        parts[start:stop, :] + last[start:stop, :] * jnp.exp2(-last[mark + 9 + i : mark + 10 + i, :])
        for i, (start, stop) in enumerate(spans)
    ]


def line_kernel(sizes, parts, last, stats, line):
    def fold(value):
        value = jnp.sum(value.reshape(-1, 8, value.shape[1]), axis=0)
        return sum(value[:, LANES * c : LANES * c + LANES] for c in range(sizes.chunks))

    sum_in, sum_out, sum_taps = totals(sizes, parts, last)
    line[0:8, :] = fold(sum_in * sum_in)
    line[8:16, :] = fold(sum_out * sum_out)
    line[16:24, :] = stats[...]
    line[24:32, :] = jnp.zeros((8, LANES), jnp.float32)
    square = jnp.sum(sum_taps * sum_taps, axis=0, keepdims=True)
    line[24:25, :] = sum(square[:, LANES * c : LANES * c + LANES] for c in range(sizes.chunks))


def sum_kernel(sizes, parts, last, share_in, share_out, taps_out):
    sum_in, sum_out, sum_taps = totals(sizes, parts, last)
    share_in[...] = sum_in
    for start, group in sizes.groups:
        lane = start // sizes.group * LANES
        count = min(group, sizes.classes - start)
        share_out[start : start + count, 0, :] = sum_out[:count, lane : lane + LANES]
    for k in range(9):
        taps_out[k, :, :] = sum_taps[k : k + 1, :]


def norm_kernel(chunks, line, total, out):
    values = [
        jnp.sum(total[16:17, :]),
        jnp.sum(total[17:18, :]),
        jnp.sum(total[18 : 18 + chunks, :]),
        jnp.sum(total[0:8, :]),
        jnp.sum(line[24:25, :]),
        jnp.sum(total[8:16, :]),
    ]
    row = lax.broadcasted_iota(jnp.int32, (8, LANES), 0)
    lane = lax.broadcasted_iota(jnp.int32, (8, LANES), 1)
    spread = jnp.zeros((8, LANES), jnp.float32)
    for i, value in enumerate(values):
        spread = jnp.where((row == i // 3) & (lane == i % 3), value, spread)
    out[...] = jnp.log(1e-12 + spread)[:2, :3]


def permute(value, pairs):
    return lax.ppermute(value, "dp", pairs)


def add_kernel(sizes, scalars, mine, theirs, out):
    depth, group = sizes.depth, sizes.group
    mark = depth + group
    end = (scalars[6] == 0) | (scalars[6] == 3)

    @pl.when(end)
    def _():
        out[...] = mine[...]

    @pl.when(jnp.logical_not(end))
    def _():
        for i, (start, stop) in enumerate(((0, depth), (depth, mark), (mark, mark + 9))):
            at = mark + 9 + i
            a, b = mine[at : at + 1, :], theirs[at : at + 1, :]
            common = jnp.minimum(a, b)
            out[start:stop, :] = mine[start:stop, :] * jnp.exp2(common - a) + theirs[
                start:stop, :
            ] * jnp.exp2(common - b)
            out[at : at + 1, :] = common
        out[mark + 12 :, :] = mine[mark + 12 :, :]


def by_row(sizes, shape, three):
    row = lax.broadcasted_iota(jnp.int32, shape, 0)
    return jnp.where(
        row < sizes.depth, three[0], jnp.where(row < sizes.depth + sizes.group, three[1], three[2])
    )


def staged_sums(sizes, me, scalars, xrows, dpre, gout, small, first, early):
    vmem = pl.BlockSpec(memory_space=pltpu.VMEM)
    smem = pl.BlockSpec(memory_space=pltpu.SMEM)
    hidden = dpre.shape[1]
    shape = (sizes.message, hidden)
    full = jax.ShapeDtypeStruct(shape, jnp.float32)
    lines = jax.ShapeDtypeStruct((8, LANES), jnp.float32)
    half = jnp.float16
    near = permute(first.astype(half), [(0, 1), (1, 0), (2, 3), (3, 2)])
    early = early.astype(half)
    middle = permute(early, [(1, 2), (2, 1)])
    late, own, stats = pl.pallas_call(
        functools.partial(blocks_kernel, sizes),
        out_shape=[full, full, lines],
        in_specs=[smem] + [vmem] * 4,
        out_specs=[vmem] * 3,
        compiler_params=pltpu.CompilerParams(vmem_limit_bytes=16 * 1024 * 1024),
        cost_estimate=pl.CostEstimate(
            flops=4 * sizes.depth * dpre.shape[0] * hidden,
            bytes_accessed=2 * xrows.size + 2 * dpre.size + 8 * sizes.message * hidden,
            transcendentals=0,
        ),
        name="blocks",
    )(scalars, xrows, dpre, gout, small)
    end = (me == 0) | (me == 3)
    mark = sizes.depth + sizes.group + 9
    both = pl.pallas_call(
        functools.partial(add_kernel, sizes),
        out_shape=full,
        in_specs=[smem, vmem, vmem],
        out_specs=vmem,
        compiler_params=pltpu.CompilerParams(vmem_limit_bytes=8 * 1024 * 1024),
        name="add",
    )(scalars, late, near.astype(jnp.float32))
    both = both.astype(half)
    far = permute(both, [(0, 1), (3, 2), (1, 3), (2, 0)])
    early, _ = lax.optimization_barrier((early, both))
    near, middle, _ = lax.optimization_barrier((near, middle, both))
    skip = permute(early, [(0, 2), (3, 1)])

    def split(value):
        return [value[mark + i : mark + i + 1] for i in range(3)]


    def decode(value):
        value = value.astype(jnp.float32)
        return value * by_row(sizes, shape, [jnp.exp2(-v) for v in split(value)])

    parts = own + decode(jnp.where(end, near, middle)) + decode(skip)
    return parts, far.astype(jnp.float32), stats


def per_device(sizes, dp, trials, features, owner, dilation_index, labels, input_weight, taps, output_weight):
    where, core, widths, halves = pieces(features[0, 0], "trial", trials, owner[0])
    me = lax.axis_index("dp")
    dil = dilation_index[0] + 1
    rows = features.shape[2]
    onehot = (labels[0][:, None] == jnp.arange(256, dtype=jnp.int32)[None, :]).astype(jnp.bfloat16)
    column = lax.broadcasted_iota(jnp.int32, (rows, LANES), 0) % PC
    before = (column < PC - dil).astype(jnp.float32)
    after = (column >= dil).astype(jnp.float32)
    classes, chunks = sizes.classes, sizes.chunks
    weight_out = jnp.pad(output_weight[0].T, ((0, 256 - classes), (0, 0)))
    high = me >= 2
    odd = me % 2
    end = (me == 0) | (me == 3)
    step, jump = jnp.where(odd == 0, 1, 2), jnp.where(high, me - 2, me + 2)
    to = [3 * (1 - odd), jnp.where(end, jump, step), jnp.where(end, step, jump), me]
    scalars = jnp.stack([dil, where, core] + to).astype(jnp.int32)
    xrows, dpre, gout, small, first, early = head_backward(
        sizes,
        widths,
        scalars,
        halves,
        onehot,
        input_weight[0],
        taps[0][:, None, :],
        weight_out,
        (after, before),
    )
    if not sizes.staged:
        return general_sums(sizes, xrows, dpre, gout, small)
    parts, last, stats = staged_sums(sizes, me, scalars, xrows, dpre, gout, small, first, early)
    vmem = pl.BlockSpec(memory_space=pltpu.VMEM)
    hidden = dpre.shape[1]
    small = pltpu.CompilerParams(vmem_limit_bytes=8 * 1024 * 1024)
    line = pl.pallas_call(
        functools.partial(line_kernel, sizes),
        out_shape=jax.ShapeDtypeStruct((32, LANES), jnp.float32),
        in_specs=[vmem] * 3,
        out_specs=vmem,
        compiler_params=small,
        name="line",
    )(parts, last, stats)
    total = line
    for step in (1, 2):
        total = total + permute(total, [(i, i ^ step) for i in range(dp)])
    share_in, share_out, total_taps = pl.pallas_call(
        functools.partial(sum_kernel, sizes),
        out_shape=[
            jax.ShapeDtypeStruct((sizes.depth, hidden), jnp.float32),
            jax.ShapeDtypeStruct((classes, 1, sizes.depth_out), jnp.float32),
            jax.ShapeDtypeStruct((9, 1, hidden), jnp.float32),
        ],
        in_specs=[vmem] * 2,
        out_specs=[vmem] * 3,
        compiler_params=small,
        cost_estimate=pl.CostEstimate(
            flops=2 * parts.size, bytes_accessed=16 * parts.size, transcendentals=0
        ),
        name="sums",
    )(parts, last)
    norms = pl.pallas_call(
        functools.partial(norm_kernel, chunks),
        out_shape=jax.ShapeDtypeStruct((2, 3), jnp.float32),
        in_specs=[vmem] * 2,
        out_specs=vmem,
        compiler_params=pltpu.CompilerParams(vmem_limit_bytes=4 * 1024 * 1024),
        name="norms",
    )(line, total)
    share_out = jnp.transpose(share_out, (1, 2, 0))
    return (share_in[None], jnp.transpose(total_taps, (1, 0, 2)), share_out, norms[None])


def general_sums(sizes, xrows, dpre, gout, small):
    g_in = jnp.dot(xrows.T, dpre, preferred_element_type=jnp.float32)
    g_out = gout[: sizes.classes].T
    g_taps = small[:9]
    share_in = lax.psum_scatter(g_in, "dp", scatter_dimension=0, tiled=True)
    share_out = lax.psum_scatter(g_out, "dp", scatter_dimension=0, tiled=True)
    local = jnp.stack([jnp.sum(g_in * g_in), jnp.sum(g_taps * g_taps), jnp.sum(g_out * g_out)])
    share_sq = jnp.stack([jnp.sum(share_in * share_in), jnp.sum(share_out * share_out)])
    total_taps, squares, share_total = lax.psum((g_taps, local, share_sq), "dp")
    totals = jnp.stack([share_total[0], jnp.sum(total_taps * total_taps), share_total[1]])
    norms = jnp.log(1e-12 + jnp.stack([squares, totals]))
    return (share_in[None], total_taps[None], share_out[None], norms[None])


def solution(mesh):
    dp, trials = mesh.shape["dp"], mesh.shape["trial"]
    placed = (
        P(("groups", "dp"), "trial", None, None),
        P(("groups", "dp")),
        P("trial"),
        P(("groups", "dp"), None),
        P("trial", None, None),
        P("trial", None, None),
        P("trial", None, None),
    )

    def step(*args):
        (wide, hidden), classes = args[4].shape[1:], args[6].shape[2]
        return per_device(Sizes(wide, hidden, classes, dp), dp, trials, *args)

    return jax.shard_map(
        step,
        mesh=mesh,
        in_specs=placed,
        out_specs=(
            P(("groups", "trial"), "dp", None),
            P(("groups", "trial"), None, None),
            P(("groups", "trial"), "dp", None),
            P(("groups", "trial"), None, None),
        ),
        check_vma=False,
    )
```

```python
import functools
import math

import jax
import jax.numpy as jnp
from jax import lax
from jax.experimental import pallas as pl
from jax.experimental.pallas import tpu as pltpu
from jax.sharding import PartitionSpec as P

PC = 37
LANES = 128
FORWARD_STEP = 64
BACKWARD_STEP = 64
REACH = 4
OFFSETS = [(a, b) for a in (-1, 0, 1) for b in (-1, 0, 1)]
X_LIMIT = 6.0
OTHER_REFS = 18
ROOM = 16384.0


def pieces(block, axis, size, source):
    wide = block.shape[1]
    if size != 4:
        block = jnp.where(lax.axis_index(axis) == source, block, jnp.zeros_like(block))
        block = lax.psum(block, axis)
        low, high = block[:, : wide // 2], block[:, wide // 2 :]
        zero = jnp.int32(0)
        return zero, zero, (wide // 2,), (low, low, high, high)
    me = lax.axis_index(axis)
    core = me % 2
    mate = [(0, 1), (1, 0), (2, 3), (3, 2)]
    across = [(0, 2), (2, 0), (1, 3), (3, 1)]
    widths, width = split_width(wide)
    shared = block[:, 2 * width :]
    block, shared = lax.optimization_barrier((block, shared))
    shared_other = lax.ppermute(shared, axis, across)
    got = lax.ppermute(jnp.where(core == 0, block[:, width : 2 * width], block[:, :width]), axis, mate)
    values = []
    at = 0
    for piece in widths:
        if at:
            block, shared_other, _ = lax.optimization_barrier((block, shared_other, values[0]))
        low, high = block[:, at : at + piece], block[:, width + at : width + at + piece]
        kept = jnp.where(core == 0, low, high)
        held = jnp.where(source % 2 == core, kept, got[:, at : at + piece])
        other = lax.ppermute(held, axis, across)
        values += [held, other, lax.ppermute(held, axis, mate), lax.ppermute(other, axis, mate)]
        at += piece
    values += [shared, lax.ppermute(shared, axis, mate)]
    values += [shared_other, lax.ppermute(shared_other, axis, mate)]
    return (source ^ me).astype(jnp.int32), core, widths, tuple(values)


def split_width(wide):
    tiles = wide // LANES
    half = (tiles - 2) // 2
    last = max(half * 2 // 5, 1)
    return tuple(LANES * n for n in (half - last, last) if n > 0), LANES * half


def gelu_parts(value):
    square = value * value
    half = 0.5 + 0.5 * jnp.tanh(value * (0.7978845608 + (0.7978845608 * 0.044715) * square))
    out_val = value * half
    rate = 2.0 * 0.7978845608 + (6.0 * 0.7978845608 * 0.044715) * square
    return (out_val, half + out_val * (1.0 - half) * rate)


def exponent(size):
    size = jnp.maximum(jnp.full((1, LANES), size, jnp.float32), 1e-30)
    return jnp.clip(jnp.floor(jnp.log(ROOM / size) * (1.0 / math.log(2.0))), -100.0, 100.0)


def head_kernel(
    sizes,
    widths,
    scalars,
    *refs,
):
    count = len(refs) - OTHER_REFS
    halves, refs = refs[:count], refs[count:]
    shared = halves[4 * len(widths) :]
    weight_in, taps, weight_out, onehot, after, before = refs[:6]
    x_vmem, dpre_out, gout, small, first, early = refs[6:12]
    pre, dys, slope, hid, dlog, sem_in = refs[12:]
    rows = x_vmem.shape[0]
    width = sum(widths)
    hidden = weight_in.shape[1]
    chunks = hidden // LANES
    guard = REACH * (PC + 1)
    dil, where, core = scalars[0], scalars[1], scalars[2]

    def fetch(kind, index):
        column = (core if kind < 2 else 1 - core) * width + sum(widths[:index])
        target = x_vmem.at[:, pl.ds(pl.multiple_of(column, LANES), widths[index])]
        return pltpu.make_async_copy(halves[4 * index + kind], target, sem_in.at[index, kind // 2])

    def fetch_shared(kind):
        return pltpu.make_async_copy(shared[kind], x_vmem.at[:, 2 * width :], sem_in.at[len(widths), 0])

    for kind in range(4):

        @pl.when(where == kind)
        def _(kind=kind):
            for index in range(len(widths)):
                fetch(kind // 2, index).start()
                fetch(2 + kind // 2, index).start()
            if shared:
                fetch_shared(kind).start()

    for c in range(chunks):
        for ref in (pre, dys):
            ref[c, :guard, :] = jnp.zeros((guard, LANES), jnp.float32)
            ref[c, guard + rows :, :] = jnp.zeros((guard, LANES), jnp.float32)
    for index in range(len(widths)):
        fetch(0, index).wait()
        fetch(2, index).wait()
    if shared:
        fetch_shared(0).wait()

    for n in range(hidden // 256):
        value = jnp.dot(
            x_vmem[...], weight_in[:, 256 * n : 256 * n + 256], preferred_element_type=jnp.float32
        )
        for h in range(2):
            pre[2 * n + h, guard : guard + rows, :] = value[:, LANES * h : LANES * h + LANES]

    starts = [dil * (PC * a + b) for a, b in OFFSETS]

    def column_sums(source, c, row, count, sign):
        column = slice(LANES * c, LANES * c + LANES)
        sums = []
        for b in range(3):
            total = None
            for k in (b, 3 + b, 6 + b):
                at = guard + row + sign * starts[k]
                term = source[c, pl.ds(at, count), :] * taps[k, :, column]
                total = term if total is None else total + term
            sums.append(total)
        return sums

    def forward(row, count):
        low, high = after[pl.ds(row, count), :], before[pl.ds(row, count), :]
        for c in range(chunks):
            sums = column_sums(pre, c, row, count, 1)
            act, grad = gelu_parts(sums[1] + low * sums[0] + high * sums[2])
            slope[c, pl.ds(row, count), :] = grad
            hid[pl.ds(row, count), LANES * c : LANES * c + LANES] = act.astype(jnp.bfloat16)

    def run(step, body):
        whole = rows // step

        @pl.loop(0, whole)
        def _(i):
            body(pl.multiple_of(i * step, step), step)

        if rows > whole * step:
            body(whole * step, rows - whole * step)

    run(FORWARD_STEP, forward)

    logits = lax.dot_general(
        hid[...], weight_out[...], (((1,), (1,)), ((), ())), preferred_element_type=jnp.float32
    )
    lane = lax.broadcasted_iota(jnp.int32, logits.shape, 1)
    logits = jnp.where(lane < sizes.classes, logits, -1e30)
    peak = jnp.max(logits, axis=1, keepdims=True)
    power = jnp.exp(logits - peak)
    prob = power / jnp.sum(power, axis=1, keepdims=True)
    dlog[...] = (prob - onehot[...].astype(jnp.float32)).astype(jnp.bfloat16)

    gout[...] = lax.dot_general(
        dlog[...], hid[...], (((0,), (0,)), ((), ())), preferred_element_type=jnp.float32
    )
    for n in range(hidden // 256):
        value = jnp.dot(
            dlog[...], weight_out[:, 256 * n : 256 * n + 256], preferred_element_type=jnp.float32
        )
        for h in range(2):
            c = 2 * n + h
            dys[c, guard : guard + rows, :] = value[:, LANES * h : LANES * h + LANES] * slope[c]

    def fold(value):
        return jnp.sum(value.reshape(-1, 8, LANES), axis=0)

    biggest = jnp.zeros((8, LANES), jnp.float32)
    taps_biggest = jnp.zeros((1, LANES), jnp.float32)
    small[...] = jnp.zeros(small.shape, jnp.float32)
    taps_square = jnp.zeros((1, LANES), jnp.float32)
    for c in range(chunks):
        column = slice(LANES * c, LANES * c + LANES)

        def backward(row, count, carry):
            sums, top = carry
            low, high = after[pl.ds(row, count), :], before[pl.ds(row, count), :]
            dy = dys[c, pl.ds(guard + row, count), :]
            masked = (dy * low, dy, dy * high)
            out = [
                sums[k] + fold(masked[k % 3] * pre[c, pl.ds(guard + row + starts[k], count), :])
                for k in range(9)
            ]
            back = column_sums(dys, c, row, count, -1)
            total = back[1] + high * back[0] + low * back[2]
            dpre_out[pl.ds(row, count), column] = total.astype(jnp.bfloat16)
            size = jnp.max(jnp.abs(total).reshape(-1, 8, LANES), axis=0)
            return tuple(out), jnp.maximum(top, size)

        zeros = tuple(jnp.zeros((8, LANES), jnp.float32) for _ in range(9))
        step = BACKWARD_STEP
        whole = rows // step
        carry = lax.fori_loop(
            0,
            whole,
            lambda i, carry, step=step: backward(pl.multiple_of(i * step, step), step, carry),
            (zeros, biggest),
        )
        if rows > whole * step:
            carry = backward(whole * step, rows - whole * step, carry)
        sums, biggest = carry
        for k in range(9):
            value = jnp.sum(sums[k], axis=0, keepdims=True)
            taps_square = taps_square + value * value
            taps_biggest = jnp.maximum(taps_biggest, jnp.abs(value))
            small[k : k + 1, column] = value
    powers = (
        exponent(jnp.max(biggest) * (X_LIMIT * rows)),
        exponent(jnp.max(jnp.abs(gout[...]))),
        exponent(jnp.max(taps_biggest)),
    )
    for c in range(chunks):
        for i, power in enumerate(powers):
            small[9 + i : 10 + i, LANES * c : LANES * c + LANES] = power
    small[16:17, :LANES] = taps_square
    small[17:18, :] = jnp.sum(gout[...] * gout[...], axis=0, keepdims=True)
    if first.shape[0] == sizes.message:
        norm = message(sizes, scalars[3], x_vmem, dpre_out, gout, small, first, True)
        norm = norm + message(sizes, scalars[4], x_vmem, dpre_out, gout, small, early, True)
        small[18:19, :LANES] = norm


def message(sizes, place, x, dpre, gout, small, out, scaled):
    depth, depth_out = sizes.depth, sizes.depth_out
    column = pl.multiple_of(place * depth, LANES)
    block = lax.dot_general(
        x[:, pl.ds(column, depth)], dpre[...], (((0,), (0,)), ((), ())), preferred_element_type=jnp.float32
    )
    hidden = block.shape[1]
    chunks = hidden // LANES
    norm = jnp.sum(block * block, axis=0, keepdims=True)
    norm = sum(norm[:, LANES * c : LANES * c + LANES] for c in range(chunks))
    factors = [jnp.exp2(small[9 + i : 10 + i, :]) if scaled else 1.0 for i in range(3)]
    out[:depth, :] = block * factors[0]
    out[depth:, :] = jnp.zeros((out.shape[0] - depth, hidden), jnp.float32)
    column = pl.multiple_of(place * depth_out, LANES)
    for start, group in sizes.groups:
        value = gout[start : start + group, pl.ds(column, depth_out)]
        lane = start // sizes.group * LANES
        factor = factors[1][:, :LANES] if scaled else 1.0
        out[depth : depth + group, lane : lane + LANES] = value * factor
    row = depth + sizes.group
    out[row : row + 9, :] = small[0:9, :] * factors[2]
    if scaled:
        out[row + 9 : row + 12, :] = small[9:12, :]
    return norm


class Sizes:
    def __init__(self, wide, hidden, classes, dp):
        self.classes = classes
        self.depth = wide // dp
        self.depth_out = hidden // dp
        self.chunks = hidden // LANES
        self.class_rows = (classes + 7) // 8 * 8
        self.group = (self.class_rows // self.chunks + 7) // 8 * 8
        self.groups = [
            (at, min(self.group, self.class_rows - at)) for at in range(0, self.class_rows, self.group)
        ]
        self.message = self.depth + self.group + 16
        self.staged = dp == 4 and self.depth % LANES == 0 and self.depth_out == LANES


def head_backward(sizes, widths, scalars, halves, onehot, weight_in, taps, weight_out, masks):
    rows = onehot.shape[0]
    wide, hidden = weight_in.shape
    chunks = hidden // LANES
    vmem = pl.BlockSpec(memory_space=pltpu.VMEM)
    anywhere = pl.BlockSpec(memory_space=pl.ANY)
    span = 2 * REACH * (PC + 1) + rows
    return pl.pallas_call(
        functools.partial(head_kernel, sizes, widths),
        out_shape=[
            jax.ShapeDtypeStruct((rows, wide), jnp.bfloat16),
            jax.ShapeDtypeStruct((rows, hidden), jnp.bfloat16),
            jax.ShapeDtypeStruct((256, hidden), jnp.float32),
            jax.ShapeDtypeStruct((24, hidden), jnp.float32),
        ]
        + [jax.ShapeDtypeStruct((sizes.message if sizes.staged else 8, hidden), jnp.float32)] * 2,
        in_specs=[pl.BlockSpec(memory_space=pltpu.SMEM)] + [anywhere] * len(halves) + [vmem] * 6,
        out_specs=[vmem] * 6,
        scratch_shapes=[
            pltpu.VMEM((chunks, span, LANES), jnp.float32),
            pltpu.VMEM((chunks, span, LANES), jnp.float32),
            pltpu.VMEM((chunks, rows, LANES), jnp.float32),
            pltpu.VMEM((rows, hidden), jnp.bfloat16),
            pltpu.VMEM((rows, 256), jnp.bfloat16),
            pltpu.SemaphoreType.DMA((len(widths) + 1, 2)),
        ],
        compiler_params=pltpu.CompilerParams(vmem_limit_bytes=24 * 1024 * 1024),
        name="head",
    )(scalars, *halves, weight_in, taps, weight_out, onehot, *masks)


def blocks_kernel(sizes, scalars, x, dpre, gout, small, late, own, stats):
    norm = message(sizes, scalars[5], x, dpre, gout, small, late, True)
    norm = norm + message(sizes, scalars[6], x, dpre, gout, small, own, False)
    stats[...] = jnp.zeros(stats.shape, jnp.float32)
    stats[0:1, :] = norm + small[18:19, :LANES]
    stats[1:2, :] = small[16:17, :LANES]
    for c in range(sizes.chunks):
        stats[2 + c : 3 + c, :] = small[17:18, LANES * c : LANES * c + LANES]


def totals(sizes, parts, last):
    mark = sizes.depth + sizes.group
    spans = ((0, sizes.depth), (sizes.depth, mark), (mark, mark + 9))
    return [
        parts[start:stop, :] + last[start:stop, :] * jnp.exp2(-last[mark + 9 + i : mark + 10 + i, :])
        for i, (start, stop) in enumerate(spans)
    ]


def line_kernel(sizes, parts, last, stats, line):
    def fold(value):
        value = jnp.sum(value.reshape(-1, 8, value.shape[1]), axis=0)
        return sum(value[:, LANES * c : LANES * c + LANES] for c in range(sizes.chunks))

    sum_in, sum_out, sum_taps = totals(sizes, parts, last)
    line[0:8, :] = fold(sum_in * sum_in)
    line[8:16, :] = fold(sum_out * sum_out)
    line[16:24, :] = stats[...]
    line[24:32, :] = jnp.zeros((8, LANES), jnp.float32)
    square = jnp.sum(sum_taps * sum_taps, axis=0, keepdims=True)
    line[24:25, :] = sum(square[:, LANES * c : LANES * c + LANES] for c in range(sizes.chunks))


def sum_kernel(sizes, parts, last, share_in, share_out, taps_out):
    sum_in, sum_out, sum_taps = totals(sizes, parts, last)
    share_in[...] = sum_in
    for start, group in sizes.groups:
        lane = start // sizes.group * LANES
        count = min(group, sizes.classes - start)
        share_out[start : start + count, 0, :] = sum_out[:count, lane : lane + LANES]
    for k in range(9):
        taps_out[k, :, :] = sum_taps[k : k + 1, :]


def norm_kernel(chunks, line, total, out):
    values = [
        jnp.sum(total[16:17, :]),
        jnp.sum(total[17:18, :]),
        jnp.sum(total[18 : 18 + chunks, :]),
        jnp.sum(total[0:8, :]),
        jnp.sum(line[24:25, :]),
        jnp.sum(total[8:16, :]),
    ]
    row = lax.broadcasted_iota(jnp.int32, (8, LANES), 0)
    lane = lax.broadcasted_iota(jnp.int32, (8, LANES), 1)
    spread = jnp.zeros((8, LANES), jnp.float32)
    for i, value in enumerate(values):
        spread = jnp.where((row == i // 3) & (lane == i % 3), value, spread)
    out[...] = jnp.log(1e-12 + spread)[:2, :3]


def permute(value, pairs):
    return lax.ppermute(value, "dp", pairs)


def add_kernel(sizes, scalars, mine, theirs, out):
    depth, group = sizes.depth, sizes.group
    mark = depth + group
    end = (scalars[6] == 0) | (scalars[6] == 3)

    @pl.when(end)
    def _():
        out[...] = mine[...]

    @pl.when(jnp.logical_not(end))
    def _():
        for i, (start, stop) in enumerate(((0, depth), (depth, mark), (mark, mark + 9))):
            at = mark + 9 + i
            a, b = mine[at : at + 1, :], theirs[at : at + 1, :]
            common = jnp.minimum(a, b)
            out[start:stop, :] = mine[start:stop, :] * jnp.exp2(common - a) + theirs[
                start:stop, :
            ] * jnp.exp2(common - b)
            out[at : at + 1, :] = common
        out[mark + 12 :, :] = mine[mark + 12 :, :]


def by_row(sizes, shape, three):
    row = lax.broadcasted_iota(jnp.int32, shape, 0)
    return jnp.where(
        row < sizes.depth, three[0], jnp.where(row < sizes.depth + sizes.group, three[1], three[2])
    )


def staged_sums(sizes, me, scalars, xrows, dpre, gout, small, first, early):
    vmem = pl.BlockSpec(memory_space=pltpu.VMEM)
    smem = pl.BlockSpec(memory_space=pltpu.SMEM)
    hidden = dpre.shape[1]
    shape = (sizes.message, hidden)
    full = jax.ShapeDtypeStruct(shape, jnp.float32)
    lines = jax.ShapeDtypeStruct((8, LANES), jnp.float32)
    half = jnp.float16
    near = permute(first.astype(half), [(0, 1), (1, 0), (2, 3), (3, 2)])
    early = early.astype(half)
    middle = permute(early, [(1, 2), (2, 1)])
    late, own, stats = pl.pallas_call(
        functools.partial(blocks_kernel, sizes),
        out_shape=[full, full, lines],
        in_specs=[smem] + [vmem] * 4,
        out_specs=[vmem] * 3,
        compiler_params=pltpu.CompilerParams(vmem_limit_bytes=16 * 1024 * 1024),
        cost_estimate=pl.CostEstimate(
            flops=4 * sizes.depth * dpre.shape[0] * hidden,
            bytes_accessed=2 * xrows.size + 2 * dpre.size + 8 * sizes.message * hidden,
            transcendentals=0,
        ),
        name="blocks",
    )(scalars, xrows, dpre, gout, small)
    end = (me == 0) | (me == 3)
    mark = sizes.depth + sizes.group + 9
    both = pl.pallas_call(
        functools.partial(add_kernel, sizes),
        out_shape=full,
        in_specs=[smem, vmem, vmem],
        out_specs=vmem,
        compiler_params=pltpu.CompilerParams(vmem_limit_bytes=8 * 1024 * 1024),
        name="add",
    )(scalars, late, near.astype(jnp.float32))
    both = both.astype(half)
    far = permute(both, [(0, 1), (3, 2), (1, 3), (2, 0)])
    early, _ = lax.optimization_barrier((early, near))
    near, middle, _ = lax.optimization_barrier((near, middle, both))
    skip = permute(early, [(0, 2), (3, 1)])

    def split(value):
        return [value[mark + i : mark + i + 1] for i in range(3)]


    def decode(value):
        value = value.astype(jnp.float32)
        return value * by_row(sizes, shape, [jnp.exp2(-v) for v in split(value)])

    parts = own + decode(jnp.where(end, near, middle)) + decode(skip)
    return parts, far.astype(jnp.float32), stats


def per_device(sizes, dp, trials, features, owner, dilation_index, labels, input_weight, taps, output_weight):
    where, core, widths, halves = pieces(features[0, 0], "trial", trials, owner[0])
    me = lax.axis_index("dp")
    dil = dilation_index[0] + 1
    rows = features.shape[2]
    onehot = (labels[0][:, None] == jnp.arange(256, dtype=jnp.int32)[None, :]).astype(jnp.bfloat16)
    column = lax.broadcasted_iota(jnp.int32, (rows, LANES), 0) % PC
    before = (column < PC - dil).astype(jnp.float32)
    after = (column >= dil).astype(jnp.float32)
    classes, chunks = sizes.classes, sizes.chunks
    weight_out = jnp.pad(output_weight[0].T, ((0, 256 - classes), (0, 0)))
    high = me >= 2
    odd = me % 2
    end = (me == 0) | (me == 3)
    step, jump = jnp.where(odd == 0, 1, 2), jnp.where(high, me - 2, me + 2)
    to = [3 * (1 - odd), jnp.where(end, jump, step), jnp.where(end, step, jump), me]
    scalars = jnp.stack([dil, where, core] + to).astype(jnp.int32)
    xrows, dpre, gout, small, first, early = head_backward(
        sizes,
        widths,
        scalars,
        halves,
        onehot,
        input_weight[0],
        taps[0][:, None, :],
        weight_out,
        (after, before),
    )
    if not sizes.staged:
        return general_sums(sizes, xrows, dpre, gout, small)
    parts, last, stats = staged_sums(sizes, me, scalars, xrows, dpre, gout, small, first, early)
    vmem = pl.BlockSpec(memory_space=pltpu.VMEM)
    hidden = dpre.shape[1]
    small = pltpu.CompilerParams(vmem_limit_bytes=8 * 1024 * 1024)
    line = pl.pallas_call(
        functools.partial(line_kernel, sizes),
        out_shape=jax.ShapeDtypeStruct((32, LANES), jnp.float32),
        in_specs=[vmem] * 3,
        out_specs=vmem,
        compiler_params=small,
        name="line",
    )(parts, last, stats)
    total = line
    for step in (1, 2):
        total = total + permute(total, [(i, i ^ step) for i in range(dp)])
    share_in, share_out, total_taps = pl.pallas_call(
        functools.partial(sum_kernel, sizes),
        out_shape=[
            jax.ShapeDtypeStruct((sizes.depth, hidden), jnp.float32),
            jax.ShapeDtypeStruct((classes, 1, sizes.depth_out), jnp.float32),
            jax.ShapeDtypeStruct((9, 1, hidden), jnp.float32),
        ],
        in_specs=[vmem] * 2,
        out_specs=[vmem] * 3,
        compiler_params=small,
        cost_estimate=pl.CostEstimate(
            flops=2 * parts.size, bytes_accessed=16 * parts.size, transcendentals=0
        ),
        name="sums",
    )(parts, last)
    norms = pl.pallas_call(
        functools.partial(norm_kernel, chunks),
        out_shape=jax.ShapeDtypeStruct((2, 3), jnp.float32),
        in_specs=[vmem] * 2,
        out_specs=vmem,
        compiler_params=pltpu.CompilerParams(vmem_limit_bytes=4 * 1024 * 1024),
        name="norms",
    )(line, total)
    share_out = jnp.transpose(share_out, (1, 2, 0))
    return (share_in[None], jnp.transpose(total_taps, (1, 0, 2)), share_out, norms[None])


def general_sums(sizes, xrows, dpre, gout, small):
    g_in = jnp.dot(xrows.T, dpre, preferred_element_type=jnp.float32)
    g_out = gout[: sizes.classes].T
    g_taps = small[:9]
    share_in = lax.psum_scatter(g_in, "dp", scatter_dimension=0, tiled=True)
    share_out = lax.psum_scatter(g_out, "dp", scatter_dimension=0, tiled=True)
    local = jnp.stack([jnp.sum(g_in * g_in), jnp.sum(g_taps * g_taps), jnp.sum(g_out * g_out)])
    share_sq = jnp.stack([jnp.sum(share_in * share_in), jnp.sum(share_out * share_out)])
    total_taps, squares, share_total = lax.psum((g_taps, local, share_sq), "dp")
    totals = jnp.stack([share_total[0], jnp.sum(total_taps * total_taps), share_total[1]])
    norms = jnp.log(1e-12 + jnp.stack([squares, totals]))
    return (share_in[None], total_taps[None], share_out[None], norms[None])


def solution(mesh):
    dp, trials = mesh.shape["dp"], mesh.shape["trial"]
    placed = (
        P(("groups", "dp"), "trial", None, None),
        P(("groups", "dp")),
        P("trial"),
        P(("groups", "dp"), None),
        P("trial", None, None),
        P("trial", None, None),
        P("trial", None, None),
    )

    def step(*args):
        (wide, hidden), classes = args[4].shape[1:], args[6].shape[2]
        return per_device(Sizes(wide, hidden, classes, dp), dp, trials, *args)

    return jax.shard_map(
        step,
        mesh=mesh,
        in_specs=placed,
        out_specs=(
            P(("groups", "trial"), "dp", None),
            P(("groups", "trial"), None, None),
            P(("groups", "trial"), "dp", None),
            P(("groups", "trial"), None, None),
        ),
        check_vma=False,
    )
```

```python
import functools
import math

import jax
import jax.numpy as jnp
from jax import lax
from jax.experimental import pallas as pl
from jax.experimental.pallas import tpu as pltpu
from jax.sharding import PartitionSpec as P

PC = 37
LANES = 128
FORWARD_STEP = 64
BACKWARD_STEP = 64
REACH = 4
OFFSETS = [(a, b) for a in (-1, 0, 1) for b in (-1, 0, 1)]
X_LIMIT = 6.0
OTHER_REFS = 17
ROOM = 16384.0


def pieces(block, axis, size, source):
    wide = block.shape[1]
    if size != 4:
        block = jnp.where(lax.axis_index(axis) == source, block, jnp.zeros_like(block))
        block = lax.psum(block, axis)
        low, high = block[:, : wide // 2], block[:, wide // 2 :]
        zero = jnp.int32(0)
        return zero, zero, (wide // 2,), (low, low, high, high)
    me = lax.axis_index(axis)
    core = me % 2
    mate = [(0, 1), (1, 0), (2, 3), (3, 2)]
    across = [(0, 2), (2, 0), (1, 3), (3, 1)]
    widths, width = split_width(wide)
    shared = block[:, 2 * width :]
    shared_other = lax.ppermute(shared, axis, across)
    got = lax.ppermute(jnp.where(core == 0, block[:, width : 2 * width], block[:, :width]), axis, mate)
    values = []
    at = 0
    for piece in widths:
        if at:
            block, shared_other, _ = lax.optimization_barrier((block, shared_other, values[0]))
        low, high = block[:, at : at + piece], block[:, width + at : width + at + piece]
        kept = jnp.where(core == 0, low, high)
        held = jnp.where(source % 2 == core, kept, got[:, at : at + piece])
        other = lax.ppermute(held, axis, across)
        values += [held, other, lax.ppermute(held, axis, mate), lax.ppermute(other, axis, mate)]
        at += piece
    values += [shared, lax.ppermute(shared, axis, mate)]
    values += [shared_other, lax.ppermute(shared_other, axis, mate)]
    return (source ^ me).astype(jnp.int32), core, widths, tuple(values)


def split_width(wide):
    tiles = wide // LANES
    half = (tiles - 2) // 2
    last = max(half * 2 // 5, 1)
    return tuple(LANES * n for n in (half - last, last) if n > 0), LANES * half


def gelu_parts(value):
    square = value * value
    half = 0.5 + 0.5 * jnp.tanh(value * (0.7978845608 + (0.7978845608 * 0.044715) * square))
    out_val = value * half
    rate = 2.0 * 0.7978845608 + (6.0 * 0.7978845608 * 0.044715) * square
    return (out_val, half + out_val * (1.0 - half) * rate)


def exponent(size):
    size = jnp.maximum(jnp.full((1, LANES), size, jnp.float32), 1e-30)
    return jnp.clip(jnp.floor(jnp.log(ROOM / size) * (1.0 / math.log(2.0))), -100.0, 100.0)


def head_kernel(
    sizes,
    widths,
    scalars,
    *refs,
):
    count = len(refs) - OTHER_REFS
    halves, refs = refs[:count], refs[count:]
    shared = halves[4 * len(widths) :]
    weight_in, taps, weight_out, onehot, after, before = refs[:6]
    x_vmem, dpre_out, gout, small, first = refs[6:11]
    pre, dys, slope, hid, dlog, sem_in = refs[11:]
    rows = x_vmem.shape[0]
    width = sum(widths)
    hidden = weight_in.shape[1]
    chunks = hidden // LANES
    guard = REACH * (PC + 1)
    dil, where, core = scalars[0], scalars[1], scalars[2]

    def fetch(kind, index):
        column = (core if kind < 2 else 1 - core) * width + sum(widths[:index])
        target = x_vmem.at[:, pl.ds(pl.multiple_of(column, LANES), widths[index])]
        return pltpu.make_async_copy(halves[4 * index + kind], target, sem_in.at[index, kind // 2])

    def fetch_shared(kind):
        return pltpu.make_async_copy(shared[kind], x_vmem.at[:, 2 * width :], sem_in.at[len(widths), 0])

    for kind in range(4):

        @pl.when(where == kind)
        def _(kind=kind):
            for index in range(len(widths)):
                fetch(kind // 2, index).start()
                fetch(2 + kind // 2, index).start()
            if shared:
                fetch_shared(kind).start()

    for c in range(chunks):
        for ref in (pre, dys):
            ref[c, :guard, :] = jnp.zeros((guard, LANES), jnp.float32)
            ref[c, guard + rows :, :] = jnp.zeros((guard, LANES), jnp.float32)
    for index in range(len(widths)):
        fetch(0, index).wait()
        fetch(2, index).wait()
    if shared:
        fetch_shared(0).wait()

    for n in range(hidden // 256):
        value = jnp.dot(
            x_vmem[...], weight_in[:, 256 * n : 256 * n + 256], preferred_element_type=jnp.float32
        )
        for h in range(2):
            pre[2 * n + h, guard : guard + rows, :] = value[:, LANES * h : LANES * h + LANES]

    starts = [dil * (PC * a + b) for a, b in OFFSETS]

    def column_sums(source, c, row, count, sign):
        column = slice(LANES * c, LANES * c + LANES)
        sums = []
        for b in range(3):
            total = None
            for k in (b, 3 + b, 6 + b):
                at = guard + row + sign * starts[k]
                term = source[c, pl.ds(at, count), :] * taps[k, :, column]
                total = term if total is None else total + term
            sums.append(total)
        return sums

    def forward(row, count):
        low, high = after[pl.ds(row, count), :], before[pl.ds(row, count), :]
        for c in range(chunks):
            sums = column_sums(pre, c, row, count, 1)
            act, grad = gelu_parts(sums[1] + low * sums[0] + high * sums[2])
            slope[c, pl.ds(row, count), :] = grad
            hid[pl.ds(row, count), LANES * c : LANES * c + LANES] = act.astype(jnp.bfloat16)

    def run(step, body):
        whole = rows // step

        @pl.loop(0, whole)
        def _(i):
            body(pl.multiple_of(i * step, step), step)

        if rows > whole * step:
            body(whole * step, rows - whole * step)

    run(FORWARD_STEP, forward)

    logits = lax.dot_general(
        hid[...], weight_out[...], (((1,), (1,)), ((), ())), preferred_element_type=jnp.float32
    )
    lane = lax.broadcasted_iota(jnp.int32, logits.shape, 1)
    logits = jnp.where(lane < sizes.classes, logits, -1e30)
    peak = jnp.max(logits, axis=1, keepdims=True)
    power = jnp.exp(logits - peak)
    prob = power / jnp.sum(power, axis=1, keepdims=True)
    dlog[...] = (prob - onehot[...].astype(jnp.float32)).astype(jnp.bfloat16)

    gout[...] = lax.dot_general(
        dlog[...], hid[...], (((0,), (0,)), ((), ())), preferred_element_type=jnp.float32
    )
    for n in range(hidden // 256):
        value = jnp.dot(
            dlog[...], weight_out[:, 256 * n : 256 * n + 256], preferred_element_type=jnp.float32
        )
        for h in range(2):
            c = 2 * n + h
            dys[c, guard : guard + rows, :] = value[:, LANES * h : LANES * h + LANES] * slope[c]

    def fold(value):
        return jnp.sum(value.reshape(-1, 8, LANES), axis=0)

    biggest = jnp.zeros((8, LANES), jnp.float32)
    taps_biggest = jnp.zeros((1, LANES), jnp.float32)
    small[...] = jnp.zeros(small.shape, jnp.float32)
    taps_square = jnp.zeros((1, LANES), jnp.float32)
    for c in range(chunks):
        column = slice(LANES * c, LANES * c + LANES)

        def backward(row, count, carry):
            sums, top = carry
            low, high = after[pl.ds(row, count), :], before[pl.ds(row, count), :]
            dy = dys[c, pl.ds(guard + row, count), :]
            masked = (dy * low, dy, dy * high)
            out = [
                sums[k] + fold(masked[k % 3] * pre[c, pl.ds(guard + row + starts[k], count), :])
                for k in range(9)
            ]
            back = column_sums(dys, c, row, count, -1)
            total = back[1] + high * back[0] + low * back[2]
            dpre_out[pl.ds(row, count), column] = total.astype(jnp.bfloat16)
            size = jnp.max(jnp.abs(total).reshape(-1, 8, LANES), axis=0)
            return tuple(out), jnp.maximum(top, size)

        zeros = tuple(jnp.zeros((8, LANES), jnp.float32) for _ in range(9))
        step = BACKWARD_STEP
        whole = rows // step
        carry = lax.fori_loop(
            0,
            whole,
            lambda i, carry, step=step: backward(pl.multiple_of(i * step, step), step, carry),
            (zeros, biggest),
        )
        if rows > whole * step:
            carry = backward(whole * step, rows - whole * step, carry)
        sums, biggest = carry
        for k in range(9):
            value = jnp.sum(sums[k], axis=0, keepdims=True)
            taps_square = taps_square + value * value
            taps_biggest = jnp.maximum(taps_biggest, jnp.abs(value))
            small[k : k + 1, column] = value
    powers = (
        exponent(jnp.max(biggest) * (X_LIMIT * rows)),
        exponent(jnp.max(jnp.abs(gout[...]))),
        exponent(jnp.max(taps_biggest)),
    )
    for c in range(chunks):
        for i, power in enumerate(powers):
            small[9 + i : 10 + i, LANES * c : LANES * c + LANES] = power
    small[16:17, :LANES] = taps_square
    small[17:18, :] = jnp.sum(gout[...] * gout[...], axis=0, keepdims=True)
    if first.shape[0] == sizes.message:
        norm = message(sizes, scalars[3], x_vmem, dpre_out, gout, small, first, True)
        small[18:19, :LANES] = norm


def message(sizes, place, x, dpre, gout, small, out, scaled):
    depth, depth_out = sizes.depth, sizes.depth_out
    column = pl.multiple_of(place * depth, LANES)
    block = lax.dot_general(
        x[:, pl.ds(column, depth)], dpre[...], (((0,), (0,)), ((), ())), preferred_element_type=jnp.float32
    )
    hidden = block.shape[1]
    chunks = hidden // LANES
    norm = jnp.sum(block * block, axis=0, keepdims=True)
    norm = sum(norm[:, LANES * c : LANES * c + LANES] for c in range(chunks))
    factors = [jnp.exp2(small[9 + i : 10 + i, :]) if scaled else 1.0 for i in range(3)]
    out[:depth, :] = block * factors[0]
    out[depth:, :] = jnp.zeros((out.shape[0] - depth, hidden), jnp.float32)
    column = pl.multiple_of(place * depth_out, LANES)
    for start, group in sizes.groups:
        value = gout[start : start + group, pl.ds(column, depth_out)]
        lane = start // sizes.group * LANES
        factor = factors[1][:, :LANES] if scaled else 1.0
        out[depth : depth + group, lane : lane + LANES] = value * factor
    row = depth + sizes.group
    out[row : row + 9, :] = small[0:9, :] * factors[2]
    if scaled:
        out[row + 9 : row + 12, :] = small[9:12, :]
    return norm


class Sizes:
    def __init__(self, wide, hidden, classes, dp):
        self.classes = classes
        self.depth = wide // dp
        self.depth_out = hidden // dp
        self.chunks = hidden // LANES
        self.class_rows = (classes + 7) // 8 * 8
        self.group = (self.class_rows // self.chunks + 7) // 8 * 8
        self.groups = [
            (at, min(self.group, self.class_rows - at)) for at in range(0, self.class_rows, self.group)
        ]
        self.message = self.depth + self.group + 16
        self.staged = dp == 4 and self.depth % LANES == 0 and self.depth_out == LANES


def head_backward(sizes, widths, scalars, halves, onehot, weight_in, taps, weight_out, masks):
    rows = onehot.shape[0]
    wide, hidden = weight_in.shape
    chunks = hidden // LANES
    vmem = pl.BlockSpec(memory_space=pltpu.VMEM)
    anywhere = pl.BlockSpec(memory_space=pl.ANY)
    span = 2 * REACH * (PC + 1) + rows
    return pl.pallas_call(
        functools.partial(head_kernel, sizes, widths),
        out_shape=[
            jax.ShapeDtypeStruct((rows, wide), jnp.bfloat16),
            jax.ShapeDtypeStruct((rows, hidden), jnp.bfloat16),
            jax.ShapeDtypeStruct((256, hidden), jnp.float32),
            jax.ShapeDtypeStruct((24, hidden), jnp.float32),
        ]
        + [jax.ShapeDtypeStruct((sizes.message if sizes.staged else 8, hidden), jnp.float32)],
        in_specs=[pl.BlockSpec(memory_space=pltpu.SMEM)] + [anywhere] * len(halves) + [vmem] * 6,
        out_specs=[vmem] * 5,
        scratch_shapes=[
            pltpu.VMEM((chunks, span, LANES), jnp.float32),
            pltpu.VMEM((chunks, span, LANES), jnp.float32),
            pltpu.VMEM((chunks, rows, LANES), jnp.float32),
            pltpu.VMEM((rows, hidden), jnp.bfloat16),
            pltpu.VMEM((rows, 256), jnp.bfloat16),
            pltpu.SemaphoreType.DMA((len(widths) + 1, 2)),
        ],
        compiler_params=pltpu.CompilerParams(vmem_limit_bytes=24 * 1024 * 1024),
        name="head",
    )(scalars, *halves, weight_in, taps, weight_out, onehot, *masks)


def step_kernel(sizes, scalars, x, dpre, gout, small, early, norm):
    norm[...] = jnp.zeros(norm.shape, jnp.float32)
    norm[0:1, :] = message(sizes, scalars[4], x, dpre, gout, small, early, True)


def blocks_kernel(sizes, scalars, x, dpre, gout, small, step_norm, late, own, stats):
    norm = message(sizes, scalars[5], x, dpre, gout, small, late, True)
    norm = norm + message(sizes, scalars[6], x, dpre, gout, small, own, False)
    stats[...] = jnp.zeros(stats.shape, jnp.float32)
    stats[0:1, :] = norm + small[18:19, :LANES] + step_norm[0:1, :]
    stats[1:2, :] = small[16:17, :LANES]
    for c in range(sizes.chunks):
        stats[2 + c : 3 + c, :] = small[17:18, LANES * c : LANES * c + LANES]


def totals(sizes, parts, last):
    mark = sizes.depth + sizes.group
    spans = ((0, sizes.depth), (sizes.depth, mark), (mark, mark + 9))
    return [
        parts[start:stop, :] + last[start:stop, :] * jnp.exp2(-last[mark + 9 + i : mark + 10 + i, :])
        for i, (start, stop) in enumerate(spans)
    ]


def line_kernel(sizes, parts, last, stats, line):
    def fold(value):
        value = jnp.sum(value.reshape(-1, 8, value.shape[1]), axis=0)
        return sum(value[:, LANES * c : LANES * c + LANES] for c in range(sizes.chunks))

    sum_in, sum_out, sum_taps = totals(sizes, parts, last)
    line[0:8, :] = fold(sum_in * sum_in)
    line[8:16, :] = fold(sum_out * sum_out)
    line[16:24, :] = stats[...]
    line[24:32, :] = jnp.zeros((8, LANES), jnp.float32)
    square = jnp.sum(sum_taps * sum_taps, axis=0, keepdims=True)
    line[24:25, :] = sum(square[:, LANES * c : LANES * c + LANES] for c in range(sizes.chunks))


def sum_kernel(sizes, parts, last, share_in, share_out, taps_out):
    sum_in, sum_out, sum_taps = totals(sizes, parts, last)
    share_in[...] = sum_in
    for start, group in sizes.groups:
        lane = start // sizes.group * LANES
        count = min(group, sizes.classes - start)
        share_out[start : start + count, 0, :] = sum_out[:count, lane : lane + LANES]
    for k in range(9):
        taps_out[k, :, :] = sum_taps[k : k + 1, :]


def norm_kernel(chunks, line, total, out):
    values = [
        jnp.sum(total[16:17, :]),
        jnp.sum(total[17:18, :]),
        jnp.sum(total[18 : 18 + chunks, :]),
        jnp.sum(total[0:8, :]),
        jnp.sum(line[24:25, :]),
        jnp.sum(total[8:16, :]),
    ]
    row = lax.broadcasted_iota(jnp.int32, (8, LANES), 0)
    lane = lax.broadcasted_iota(jnp.int32, (8, LANES), 1)
    spread = jnp.zeros((8, LANES), jnp.float32)
    for i, value in enumerate(values):
        spread = jnp.where((row == i // 3) & (lane == i % 3), value, spread)
    out[...] = jnp.log(1e-12 + spread)[:2, :3]


def permute(value, pairs):
    return lax.ppermute(value, "dp", pairs)


def add_kernel(sizes, scalars, mine, theirs, out):
    depth, group = sizes.depth, sizes.group
    mark = depth + group
    end = (scalars[6] == 0) | (scalars[6] == 3)

    @pl.when(end)
    def _():
        out[...] = mine[...]

    @pl.when(jnp.logical_not(end))
    def _():
        for i, (start, stop) in enumerate(((0, depth), (depth, mark), (mark, mark + 9))):
            at = mark + 9 + i
            a, b = mine[at : at + 1, :], theirs[at : at + 1, :]
            common = jnp.minimum(a, b)
            out[start:stop, :] = mine[start:stop, :] * jnp.exp2(common - a) + theirs[
                start:stop, :
            ] * jnp.exp2(common - b)
            out[at : at + 1, :] = common
        out[mark + 12 :, :] = mine[mark + 12 :, :]


def by_row(sizes, shape, three):
    row = lax.broadcasted_iota(jnp.int32, shape, 0)
    return jnp.where(
        row < sizes.depth, three[0], jnp.where(row < sizes.depth + sizes.group, three[1], three[2])
    )


def staged_sums(sizes, me, scalars, xrows, dpre, gout, small, first):
    vmem = pl.BlockSpec(memory_space=pltpu.VMEM)
    smem = pl.BlockSpec(memory_space=pltpu.SMEM)
    hidden = dpre.shape[1]
    shape = (sizes.message, hidden)
    full = jax.ShapeDtypeStruct(shape, jnp.float32)
    lines = jax.ShapeDtypeStruct((8, LANES), jnp.float32)
    half = jnp.float16
    near = permute(first.astype(half), [(0, 1), (1, 0), (2, 3), (3, 2)])
    early, step_norm = pl.pallas_call(
        functools.partial(step_kernel, sizes),
        out_shape=[full, lines],
        in_specs=[smem] + [vmem] * 4,
        out_specs=[vmem] * 2,
        compiler_params=pltpu.CompilerParams(vmem_limit_bytes=16 * 1024 * 1024),
        cost_estimate=pl.CostEstimate(
            flops=2 * sizes.depth * dpre.shape[0] * hidden,
            bytes_accessed=2 * xrows.size + 2 * dpre.size + 4 * sizes.message * hidden,
            transcendentals=0,
        ),
        name="step",
    )(scalars, xrows, dpre, gout, small)
    early = early.astype(half)
    middle = permute(early, [(1, 2), (2, 1)])
    late, own, stats = pl.pallas_call(
        functools.partial(blocks_kernel, sizes),
        out_shape=[full, full, lines],
        in_specs=[smem] + [vmem] * 5,
        out_specs=[vmem] * 3,
        compiler_params=pltpu.CompilerParams(vmem_limit_bytes=16 * 1024 * 1024),
        cost_estimate=pl.CostEstimate(
            flops=4 * sizes.depth * dpre.shape[0] * hidden,
            bytes_accessed=2 * xrows.size + 2 * dpre.size + 8 * sizes.message * hidden,
            transcendentals=0,
        ),
        name="blocks",
    )(scalars, xrows, dpre, gout, small, step_norm)
    end = (me == 0) | (me == 3)
    mark = sizes.depth + sizes.group + 9
    both = pl.pallas_call(
        functools.partial(add_kernel, sizes),
        out_shape=full,
        in_specs=[smem, vmem, vmem],
        out_specs=vmem,
        compiler_params=pltpu.CompilerParams(vmem_limit_bytes=8 * 1024 * 1024),
        name="add",
    )(scalars, late, near.astype(jnp.float32))
    both = both.astype(half)
    far = permute(both, [(0, 1), (3, 2), (1, 3), (2, 0)])
    early, _ = lax.optimization_barrier((early, both))
    near, middle, _ = lax.optimization_barrier((near, middle, both))
    skip = permute(early, [(0, 2), (3, 1)])

    def split(value):
        return [value[mark + i : mark + i + 1] for i in range(3)]


    def decode(value):
        value = value.astype(jnp.float32)
        return value * by_row(sizes, shape, [jnp.exp2(-v) for v in split(value)])

    parts = own + decode(jnp.where(end, near, middle)) + decode(skip)
    return parts, far.astype(jnp.float32), stats


def per_device(sizes, dp, trials, features, owner, dilation_index, labels, input_weight, taps, output_weight):
    where, core, widths, halves = pieces(features[0, 0], "trial", trials, owner[0])
    me = lax.axis_index("dp")
    dil = dilation_index[0] + 1
    rows = features.shape[2]
    onehot = (labels[0][:, None] == jnp.arange(256, dtype=jnp.int32)[None, :]).astype(jnp.bfloat16)
    column = lax.broadcasted_iota(jnp.int32, (rows, LANES), 0) % PC
    before = (column < PC - dil).astype(jnp.float32)
    after = (column >= dil).astype(jnp.float32)
    classes, chunks = sizes.classes, sizes.chunks
    weight_out = jnp.pad(output_weight[0].T, ((0, 256 - classes), (0, 0)))
    high = me >= 2
    odd = me % 2
    end = (me == 0) | (me == 3)
    step, jump = jnp.where(odd == 0, 1, 2), jnp.where(high, me - 2, me + 2)
    to = [3 * (1 - odd), jnp.where(end, jump, step), jnp.where(end, step, jump), me]
    scalars = jnp.stack([dil, where, core] + to).astype(jnp.int32)
    xrows, dpre, gout, small, first = head_backward(
        sizes,
        widths,
        scalars,
        halves,
        onehot,
        input_weight[0],
        taps[0][:, None, :],
        weight_out,
        (after, before),
    )
    if not sizes.staged:
        return general_sums(sizes, xrows, dpre, gout, small)
    parts, last, stats = staged_sums(sizes, me, scalars, xrows, dpre, gout, small, first)
    vmem = pl.BlockSpec(memory_space=pltpu.VMEM)
    hidden = dpre.shape[1]
    small = pltpu.CompilerParams(vmem_limit_bytes=8 * 1024 * 1024)
    line = pl.pallas_call(
        functools.partial(line_kernel, sizes),
        out_shape=jax.ShapeDtypeStruct((32, LANES), jnp.float32),
        in_specs=[vmem] * 3,
        out_specs=vmem,
        compiler_params=small,
        name="line",
    )(parts, last, stats)
    total = line
    for step in (1, 2):
        total = total + permute(total, [(i, i ^ step) for i in range(dp)])
    share_in, share_out, total_taps = pl.pallas_call(
        functools.partial(sum_kernel, sizes),
        out_shape=[
            jax.ShapeDtypeStruct((sizes.depth, hidden), jnp.float32),
            jax.ShapeDtypeStruct((classes, 1, sizes.depth_out), jnp.float32),
            jax.ShapeDtypeStruct((9, 1, hidden), jnp.float32),
        ],
        in_specs=[vmem] * 2,
        out_specs=[vmem] * 3,
        compiler_params=small,
        cost_estimate=pl.CostEstimate(
            flops=2 * parts.size, bytes_accessed=16 * parts.size, transcendentals=0
        ),
        name="sums",
    )(parts, last)
    norms = pl.pallas_call(
        functools.partial(norm_kernel, chunks),
        out_shape=jax.ShapeDtypeStruct((2, 3), jnp.float32),
        in_specs=[vmem] * 2,
        out_specs=vmem,
        compiler_params=pltpu.CompilerParams(vmem_limit_bytes=4 * 1024 * 1024),
        name="norms",
    )(line, total)
    share_out = jnp.transpose(share_out, (1, 2, 0))
    return (share_in[None], jnp.transpose(total_taps, (1, 0, 2)), share_out, norms[None])


def general_sums(sizes, xrows, dpre, gout, small):
    g_in = jnp.dot(xrows.T, dpre, preferred_element_type=jnp.float32)
    g_out = gout[: sizes.classes].T
    g_taps = small[:9]
    share_in = lax.psum_scatter(g_in, "dp", scatter_dimension=0, tiled=True)
    share_out = lax.psum_scatter(g_out, "dp", scatter_dimension=0, tiled=True)
    local = jnp.stack([jnp.sum(g_in * g_in), jnp.sum(g_taps * g_taps), jnp.sum(g_out * g_out)])
    share_sq = jnp.stack([jnp.sum(share_in * share_in), jnp.sum(share_out * share_out)])
    total_taps, squares, share_total = lax.psum((g_taps, local, share_sq), "dp")
    totals = jnp.stack([share_total[0], jnp.sum(total_taps * total_taps), share_total[1]])
    norms = jnp.log(1e-12 + jnp.stack([squares, totals]))
    return (share_in[None], total_taps[None], share_out[None], norms[None])


def solution(mesh):
    dp, trials = mesh.shape["dp"], mesh.shape["trial"]
    placed = (
        P(("groups", "dp"), "trial", None, None),
        P(("groups", "dp")),
        P("trial"),
        P(("groups", "dp"), None),
        P("trial", None, None),
        P("trial", None, None),
        P("trial", None, None),
    )

    def step(*args):
        (wide, hidden), classes = args[4].shape[1:], args[6].shape[2]
        return per_device(Sizes(wide, hidden, classes, dp), dp, trials, *args)

    return jax.shard_map(
        step,
        mesh=mesh,
        in_specs=placed,
        out_specs=(
            P(("groups", "trial"), "dp", None),
            P(("groups", "trial"), None, None),
            P(("groups", "trial"), "dp", None),
            P(("groups", "trial"), None, None),
        ),
        check_vma=False,
    )
```

```python
import functools
import math

import jax
import jax.numpy as jnp
from jax import lax
from jax.experimental import pallas as pl
from jax.experimental.pallas import tpu as pltpu
from jax.sharding import PartitionSpec as P

PC = 37
LANES = 128
FORWARD_STEP = 64
BACKWARD_STEP = 64
REACH = 4
OFFSETS = [(a, b) for a in (-1, 0, 1) for b in (-1, 0, 1)]
X_LIMIT = 6.0
OTHER_REFS = 18
ROOM = 16384.0


def pieces(block, axis, size, source):
    wide = block.shape[1]
    if size != 4:
        block = jnp.where(lax.axis_index(axis) == source, block, jnp.zeros_like(block))
        block = lax.psum(block, axis)
        low, high = block[:, : wide // 2], block[:, wide // 2 :]
        zero = jnp.int32(0)
        return zero, zero, (wide // 2,), (low, low, high, high)
    me = lax.axis_index(axis)
    core = me % 2
    mate = [(0, 1), (1, 0), (2, 3), (3, 2)]
    across = [(0, 2), (2, 0), (1, 3), (3, 1)]
    widths, width = split_width(wide)
    shared = block[:, 2 * width :]
    shared_other = lax.ppermute(shared, axis, across)
    got = lax.ppermute(jnp.where(core == 0, block[:, width : 2 * width], block[:, :width]), axis, mate)
    values = []
    at = 0
    for piece in widths:
        if at:
            block, shared_other, _ = lax.optimization_barrier((block, shared_other, values[0]))
        low, high = block[:, at : at + piece], block[:, width + at : width + at + piece]
        kept = jnp.where(core == 0, low, high)
        held = jnp.where(source % 2 == core, kept, got[:, at : at + piece])
        other = lax.ppermute(held, axis, across)
        values += [held, other, lax.ppermute(held, axis, mate), lax.ppermute(other, axis, mate)]
        at += piece
    values += [shared, lax.ppermute(shared, axis, mate)]
    values += [shared_other, lax.ppermute(shared_other, axis, mate)]
    return (source ^ me).astype(jnp.int32), core, widths, tuple(values)


def split_width(wide):
    tiles = wide // LANES
    half = (tiles - 2) // 2
    last = max(half * 2 // 5, 1)
    return tuple(LANES * n for n in (half - last, last) if n > 0), LANES * half


def gelu_parts(value):
    square = value * value
    half = 0.5 + 0.5 * jnp.tanh(value * (0.7978845608 + (0.7978845608 * 0.044715) * square))
    out_val = value * half
    rate = 2.0 * 0.7978845608 + (6.0 * 0.7978845608 * 0.044715) * square
    return (out_val, half + out_val * (1.0 - half) * rate)


def exponent(size):
    size = jnp.maximum(jnp.full((1, LANES), size, jnp.float32), 1e-30)
    return jnp.clip(jnp.floor(jnp.log(ROOM / size) * (1.0 / math.log(2.0))), -100.0, 100.0)


def head_kernel(
    sizes,
    widths,
    scalars,
    *refs,
):
    count = len(refs) - OTHER_REFS
    halves, refs = refs[:count], refs[count:]
    shared = halves[4 * len(widths) :]
    weight_in, taps, weight_out, onehot, after, before = refs[:6]
    x_vmem, dpre_out, gout, small, first, early = refs[6:12]
    pre, dys, slope, hid, dlog, sem_in = refs[12:]
    rows = x_vmem.shape[0]
    width = sum(widths)
    hidden = weight_in.shape[1]
    chunks = hidden // LANES
    guard = REACH * (PC + 1)
    dil, where, core = scalars[0], scalars[1], scalars[2]

    def fetch(kind, index):
        column = (core if kind < 2 else 1 - core) * width + sum(widths[:index])
        target = x_vmem.at[:, pl.ds(pl.multiple_of(column, LANES), widths[index])]
        return pltpu.make_async_copy(halves[4 * index + kind], target, sem_in.at[index, kind // 2])

    def fetch_shared(kind):
        return pltpu.make_async_copy(shared[kind], x_vmem.at[:, 2 * width :], sem_in.at[len(widths), 0])

    for kind in range(4):

        @pl.when(where == kind)
        def _(kind=kind):
            for index in range(len(widths)):
                fetch(kind // 2, index).start()
                fetch(2 + kind // 2, index).start()
            if shared:
                fetch_shared(kind).start()

    for c in range(chunks):
        for ref in (pre, dys):
            ref[c, :guard, :] = jnp.zeros((guard, LANES), jnp.float32)
            ref[c, guard + rows :, :] = jnp.zeros((guard, LANES), jnp.float32)
    for index in range(len(widths)):
        fetch(0, index).wait()
        fetch(2, index).wait()
    if shared:
        fetch_shared(0).wait()

    for n in range(hidden // 256):
        value = jnp.dot(
            x_vmem[...], weight_in[:, 256 * n : 256 * n + 256], preferred_element_type=jnp.float32
        )
        for h in range(2):
            pre[2 * n + h, guard : guard + rows, :] = value[:, LANES * h : LANES * h + LANES]

    starts = [dil * (PC * a + b) for a, b in OFFSETS]

    def column_sums(source, c, row, count, sign):
        column = slice(LANES * c, LANES * c + LANES)
        sums = []
        for b in range(3):
            total = None
            for k in (b, 3 + b, 6 + b):
                at = guard + row + sign * starts[k]
                term = source[c, pl.ds(at, count), :] * taps[k, :, column]
                total = term if total is None else total + term
            sums.append(total)
        return sums

    def forward(row, count):
        low, high = after[pl.ds(row, count), :], before[pl.ds(row, count), :]
        for c in range(chunks):
            sums = column_sums(pre, c, row, count, 1)
            act, grad = gelu_parts(sums[1] + low * sums[0] + high * sums[2])
            slope[c, pl.ds(row, count), :] = grad
            hid[pl.ds(row, count), LANES * c : LANES * c + LANES] = act.astype(jnp.bfloat16)

    def run(step, body):
        whole = rows // step

        @pl.loop(0, whole)
        def _(i):
            body(pl.multiple_of(i * step, step), step)

        if rows > whole * step:
            body(whole * step, rows - whole * step)

    run(FORWARD_STEP, forward)

    logits = lax.dot_general(
        hid[...], weight_out[...], (((1,), (1,)), ((), ())), preferred_element_type=jnp.float32
    )
    lane = lax.broadcasted_iota(jnp.int32, logits.shape, 1)
    logits = jnp.where(lane < sizes.classes, logits, -1e30)
    peak = jnp.max(logits, axis=1, keepdims=True)
    power = jnp.exp(logits - peak)
    prob = power / jnp.sum(power, axis=1, keepdims=True)
    dlog[...] = (prob - onehot[...].astype(jnp.float32)).astype(jnp.bfloat16)

    gout[...] = lax.dot_general(
        dlog[...], hid[...], (((0,), (0,)), ((), ())), preferred_element_type=jnp.float32
    )
    for n in range(hidden // 256):
        value = jnp.dot(
            dlog[...], weight_out[:, 256 * n : 256 * n + 256], preferred_element_type=jnp.float32
        )
        for h in range(2):
            c = 2 * n + h
            dys[c, guard : guard + rows, :] = value[:, LANES * h : LANES * h + LANES] * slope[c]

    def fold(value):
        return jnp.sum(value.reshape(-1, 8, LANES), axis=0)

    biggest = jnp.zeros((8, LANES), jnp.float32)
    taps_biggest = jnp.zeros((1, LANES), jnp.float32)
    small[...] = jnp.zeros(small.shape, jnp.float32)
    taps_square = jnp.zeros((1, LANES), jnp.float32)
    for c in range(chunks):
        column = slice(LANES * c, LANES * c + LANES)

        def backward(row, count, carry):
            sums, top = carry
            low, high = after[pl.ds(row, count), :], before[pl.ds(row, count), :]
            dy = dys[c, pl.ds(guard + row, count), :]
            masked = (dy * low, dy, dy * high)
            out = [
                sums[k] + fold(masked[k % 3] * pre[c, pl.ds(guard + row + starts[k], count), :])
                for k in range(9)
            ]
            back = column_sums(dys, c, row, count, -1)
            total = back[1] + high * back[0] + low * back[2]
            dpre_out[pl.ds(row, count), column] = total.astype(jnp.bfloat16)
            size = jnp.max(jnp.abs(total).reshape(-1, 8, LANES), axis=0)
            return tuple(out), jnp.maximum(top, size)

        zeros = tuple(jnp.zeros((8, LANES), jnp.float32) for _ in range(9))
        step = BACKWARD_STEP
        whole = rows // step
        carry = lax.fori_loop(
            0,
            whole,
            lambda i, carry, step=step: backward(pl.multiple_of(i * step, step), step, carry),
            (zeros, biggest),
        )
        if rows > whole * step:
            carry = backward(whole * step, rows - whole * step, carry)
        sums, biggest = carry
        for k in range(9):
            value = jnp.sum(sums[k], axis=0, keepdims=True)
            taps_square = taps_square + value * value
            taps_biggest = jnp.maximum(taps_biggest, jnp.abs(value))
            small[k : k + 1, column] = value
    powers = (
        exponent(jnp.max(biggest) * (X_LIMIT * rows)),
        exponent(jnp.max(jnp.abs(gout[...]))),
        exponent(jnp.max(taps_biggest)),
    )
    for c in range(chunks):
        for i, power in enumerate(powers):
            small[9 + i : 10 + i, LANES * c : LANES * c + LANES] = power
    small[16:17, :LANES] = taps_square
    small[17:18, :] = jnp.sum(gout[...] * gout[...], axis=0, keepdims=True)
    if first.shape[0] == sizes.message:
        norm = message(sizes, scalars[3], x_vmem, dpre_out, gout, small, first, True)
        norm = norm + message(sizes, scalars[4], x_vmem, dpre_out, gout, small, early, True)
        small[18:19, :LANES] = norm


def message(sizes, place, x, dpre, gout, small, out, scaled):
    depth, depth_out = sizes.depth, sizes.depth_out
    column = pl.multiple_of(place * depth, LANES)
    block = lax.dot_general(
        x[:, pl.ds(column, depth)], dpre[...], (((0,), (0,)), ((), ())), preferred_element_type=jnp.float32
    )
    hidden = block.shape[1]
    chunks = hidden // LANES
    norm = jnp.sum(block * block, axis=0, keepdims=True)
    norm = sum(norm[:, LANES * c : LANES * c + LANES] for c in range(chunks))
    factors = [jnp.exp2(small[9 + i : 10 + i, :]) if scaled else 1.0 for i in range(3)]
    out[:depth, :] = block * factors[0]
    out[depth:, :] = jnp.zeros((out.shape[0] - depth, hidden), jnp.float32)
    column = pl.multiple_of(place * depth_out, LANES)
    for start, group in sizes.groups:
        value = gout[start : start + group, pl.ds(column, depth_out)]
        lane = start // sizes.group * LANES
        factor = factors[1][:, :LANES] if scaled else 1.0
        out[depth : depth + group, lane : lane + LANES] = value * factor
    row = depth + sizes.group
    out[row : row + 9, :] = small[0:9, :] * factors[2]
    if scaled:
        out[row + 9 : row + 12, :] = small[9:12, :]
    return norm


class Sizes:
    def __init__(self, wide, hidden, classes, dp):
        self.classes = classes
        self.depth = wide // dp
        self.depth_out = hidden // dp
        self.chunks = hidden // LANES
        self.class_rows = (classes + 7) // 8 * 8
        self.group = (self.class_rows // self.chunks + 7) // 8 * 8
        self.groups = [
            (at, min(self.group, self.class_rows - at)) for at in range(0, self.class_rows, self.group)
        ]
        self.message = self.depth + self.group + 16
        self.staged = dp == 4 and self.depth % LANES == 0 and self.depth_out == LANES


def head_backward(sizes, widths, scalars, halves, onehot, weight_in, taps, weight_out, masks):
    rows = onehot.shape[0]
    wide, hidden = weight_in.shape
    chunks = hidden // LANES
    vmem = pl.BlockSpec(memory_space=pltpu.VMEM)
    anywhere = pl.BlockSpec(memory_space=pl.ANY)
    span = 2 * REACH * (PC + 1) + rows
    return pl.pallas_call(
        functools.partial(head_kernel, sizes, widths),
        out_shape=[
            jax.ShapeDtypeStruct((rows, wide), jnp.bfloat16),
            jax.ShapeDtypeStruct((rows, hidden), jnp.bfloat16),
            jax.ShapeDtypeStruct((256, hidden), jnp.float32),
            jax.ShapeDtypeStruct((24, hidden), jnp.float32),
        ]
        + [jax.ShapeDtypeStruct((sizes.message if sizes.staged else 8, hidden), jnp.float32)] * 2,
        in_specs=[pl.BlockSpec(memory_space=pltpu.SMEM)] + [anywhere] * len(halves) + [vmem] * 6,
        out_specs=[vmem] * 6,
        scratch_shapes=[
            pltpu.VMEM((chunks, span, LANES), jnp.float32),
            pltpu.VMEM((chunks, span, LANES), jnp.float32),
            pltpu.VMEM((chunks, rows, LANES), jnp.float32),
            pltpu.VMEM((rows, hidden), jnp.bfloat16),
            pltpu.VMEM((rows, 256), jnp.bfloat16),
            pltpu.SemaphoreType.DMA((len(widths) + 1, 2)),
        ],
        compiler_params=pltpu.CompilerParams(vmem_limit_bytes=24 * 1024 * 1024),
        name="head",
    )(scalars, *halves, weight_in, taps, weight_out, onehot, *masks)


def blocks_kernel(sizes, scalars, x, dpre, gout, small, late, own, stats):
    norm = message(sizes, scalars[5], x, dpre, gout, small, late, True)
    norm = norm + message(sizes, scalars[6], x, dpre, gout, small, own, False)
    stats[...] = jnp.zeros(stats.shape, jnp.float32)
    stats[0:1, :] = norm + small[18:19, :LANES]
    stats[1:2, :] = small[16:17, :LANES]
    for c in range(sizes.chunks):
        stats[2 + c : 3 + c, :] = small[17:18, LANES * c : LANES * c + LANES]


def totals(sizes, parts, last):
    mark = sizes.depth + sizes.group
    spans = ((0, sizes.depth), (sizes.depth, mark), (mark, mark + 9))
    return [
        parts[start:stop, :] + last[start:stop, :] * jnp.exp2(-last[mark + 9 + i : mark + 10 + i, :])
        for i, (start, stop) in enumerate(spans)
    ]


def line_kernel(sizes, parts, last, stats, line):
    def fold(value):
        value = jnp.sum(value.reshape(-1, 8, value.shape[1]), axis=0)
        return sum(value[:, LANES * c : LANES * c + LANES] for c in range(sizes.chunks))

    sum_in, sum_out, sum_taps = totals(sizes, parts, last)
    line[0:8, :] = fold(sum_in * sum_in)
    line[8:16, :] = fold(sum_out * sum_out)
    line[16:24, :] = stats[...]
    line[24:32, :] = jnp.zeros((8, LANES), jnp.float32)
    square = jnp.sum(sum_taps * sum_taps, axis=0, keepdims=True)
    line[24:25, :] = sum(square[:, LANES * c : LANES * c + LANES] for c in range(sizes.chunks))


def sum_kernel(sizes, parts, last, share_in, share_out, taps_out):
    sum_in, sum_out, sum_taps = totals(sizes, parts, last)
    share_in[...] = sum_in
    for start, group in sizes.groups:
        lane = start // sizes.group * LANES
        count = min(group, sizes.classes - start)
        share_out[start : start + count, 0, :] = sum_out[:count, lane : lane + LANES]
    for k in range(9):
        taps_out[k, :, :] = sum_taps[k : k + 1, :]


def norm_kernel(chunks, line, total, out):
    values = [
        jnp.sum(total[16:17, :]),
        jnp.sum(total[17:18, :]),
        jnp.sum(total[18 : 18 + chunks, :]),
        jnp.sum(total[0:8, :]),
        jnp.sum(line[24:25, :]),
        jnp.sum(total[8:16, :]),
    ]
    row = lax.broadcasted_iota(jnp.int32, (8, LANES), 0)
    lane = lax.broadcasted_iota(jnp.int32, (8, LANES), 1)
    spread = jnp.zeros((8, LANES), jnp.float32)
    for i, value in enumerate(values):
        spread = jnp.where((row == i // 3) & (lane == i % 3), value, spread)
    out[...] = jnp.log(1e-12 + spread)[:2, :3]


def permute(value, pairs):
    return lax.ppermute(value, "dp", pairs)


def add_kernel(sizes, scalars, mine, theirs, out):
    depth, group = sizes.depth, sizes.group
    mark = depth + group
    end = (scalars[6] == 0) | (scalars[6] == 3)

    @pl.when(end)
    def _():
        out[...] = mine[...]

    @pl.when(jnp.logical_not(end))
    def _():
        for i, (start, stop) in enumerate(((0, depth), (depth, mark), (mark, mark + 9))):
            at = mark + 9 + i
            a, b = mine[at : at + 1, :], theirs[at : at + 1, :]
            common = jnp.minimum(a, b)
            out[start:stop, :] = mine[start:stop, :] * jnp.exp2(common - a) + theirs[
                start:stop, :
            ] * jnp.exp2(common - b)
            out[at : at + 1, :] = common
        out[mark + 12 :, :] = mine[mark + 12 :, :]


def by_row(sizes, shape, three):
    row = lax.broadcasted_iota(jnp.int32, shape, 0)
    return jnp.where(
        row < sizes.depth, three[0], jnp.where(row < sizes.depth + sizes.group, three[1], three[2])
    )


def staged_sums(sizes, me, scalars, xrows, dpre, gout, small, first, early):
    vmem = pl.BlockSpec(memory_space=pltpu.VMEM)
    smem = pl.BlockSpec(memory_space=pltpu.SMEM)
    hidden = dpre.shape[1]
    shape = (sizes.message, hidden)
    full = jax.ShapeDtypeStruct(shape, jnp.float32)
    lines = jax.ShapeDtypeStruct((8, LANES), jnp.float32)
    half = jnp.float16
    near = permute(first.astype(half), [(0, 1), (1, 0), (2, 3), (3, 2)])
    early = early.astype(half)
    middle = permute(early, [(1, 2), (2, 1)])
    late, own, stats = pl.pallas_call(
        functools.partial(blocks_kernel, sizes),
        out_shape=[full, full, lines],
        in_specs=[smem] + [vmem] * 4,
        out_specs=[vmem] * 3,
        compiler_params=pltpu.CompilerParams(vmem_limit_bytes=16 * 1024 * 1024),
        cost_estimate=pl.CostEstimate(
            flops=4 * sizes.depth * dpre.shape[0] * hidden,
            bytes_accessed=2 * xrows.size + 2 * dpre.size + 8 * sizes.message * hidden,
            transcendentals=0,
        ),
        name="blocks",
    )(scalars, xrows, dpre, gout, small)
    end = (me == 0) | (me == 3)
    mark = sizes.depth + sizes.group + 9
    both = pl.pallas_call(
        functools.partial(add_kernel, sizes),
        out_shape=full,
        in_specs=[smem, vmem, vmem],
        out_specs=vmem,
        compiler_params=pltpu.CompilerParams(vmem_limit_bytes=8 * 1024 * 1024),
        name="add",
    )(scalars, late, near.astype(jnp.float32))
    both = both.astype(half)
    far = permute(both, [(0, 1), (3, 2), (1, 3), (2, 0)])
    early, _ = lax.optimization_barrier((early, both))
    near, middle, _ = lax.optimization_barrier((near, middle, both))
    skip = permute(early, [(0, 2), (3, 1)])

    def split(value):
        return [value[mark + i : mark + i + 1] for i in range(3)]


    def decode(value):
        value = value.astype(jnp.float32)
        return value * by_row(sizes, shape, [jnp.exp2(-v) for v in split(value)])

    parts = lax.optimization_barrier(own + decode(jnp.where(end, near, middle)))
    parts = parts + decode(skip)
    return parts, far.astype(jnp.float32), stats


def per_device(sizes, dp, trials, features, owner, dilation_index, labels, input_weight, taps, output_weight):
    where, core, widths, halves = pieces(features[0, 0], "trial", trials, owner[0])
    me = lax.axis_index("dp")
    dil = dilation_index[0] + 1
    rows = features.shape[2]
    onehot = (labels[0][:, None] == jnp.arange(256, dtype=jnp.int32)[None, :]).astype(jnp.bfloat16)
    column = lax.broadcasted_iota(jnp.int32, (rows, LANES), 0) % PC
    before = (column < PC - dil).astype(jnp.float32)
    after = (column >= dil).astype(jnp.float32)
    classes, chunks = sizes.classes, sizes.chunks
    weight_out = jnp.pad(output_weight[0].T, ((0, 256 - classes), (0, 0)))
    high = me >= 2
    odd = me % 2
    end = (me == 0) | (me == 3)
    step, jump = jnp.where(odd == 0, 1, 2), jnp.where(high, me - 2, me + 2)
    to = [3 * (1 - odd), jnp.where(end, jump, step), jnp.where(end, step, jump), me]
    scalars = jnp.stack([dil, where, core] + to).astype(jnp.int32)
    xrows, dpre, gout, small, first, early = head_backward(
        sizes,
        widths,
        scalars,
        halves,
        onehot,
        input_weight[0],
        taps[0][:, None, :],
        weight_out,
        (after, before),
    )
    if not sizes.staged:
        return general_sums(sizes, xrows, dpre, gout, small)
    parts, last, stats = staged_sums(sizes, me, scalars, xrows, dpre, gout, small, first, early)
    vmem = pl.BlockSpec(memory_space=pltpu.VMEM)
    hidden = dpre.shape[1]
    small = pltpu.CompilerParams(vmem_limit_bytes=8 * 1024 * 1024)
    line = pl.pallas_call(
        functools.partial(line_kernel, sizes),
        out_shape=jax.ShapeDtypeStruct((32, LANES), jnp.float32),
        in_specs=[vmem] * 3,
        out_specs=vmem,
        compiler_params=small,
        name="line",
    )(parts, last, stats)
    total = line
    for step in (1, 2):
        total = total + permute(total, [(i, i ^ step) for i in range(dp)])
    share_in, share_out, total_taps = pl.pallas_call(
        functools.partial(sum_kernel, sizes),
        out_shape=[
            jax.ShapeDtypeStruct((sizes.depth, hidden), jnp.float32),
            jax.ShapeDtypeStruct((classes, 1, sizes.depth_out), jnp.float32),
            jax.ShapeDtypeStruct((9, 1, hidden), jnp.float32),
        ],
        in_specs=[vmem] * 2,
        out_specs=[vmem] * 3,
        compiler_params=small,
        cost_estimate=pl.CostEstimate(
            flops=2 * parts.size, bytes_accessed=16 * parts.size, transcendentals=0
        ),
        name="sums",
    )(parts, last)
    norms = pl.pallas_call(
        functools.partial(norm_kernel, chunks),
        out_shape=jax.ShapeDtypeStruct((2, 3), jnp.float32),
        in_specs=[vmem] * 2,
        out_specs=vmem,
        compiler_params=pltpu.CompilerParams(vmem_limit_bytes=4 * 1024 * 1024),
        name="norms",
    )(line, total)
    share_out = jnp.transpose(share_out, (1, 2, 0))
    return (share_in[None], jnp.transpose(total_taps, (1, 0, 2)), share_out, norms[None])


def general_sums(sizes, xrows, dpre, gout, small):
    g_in = jnp.dot(xrows.T, dpre, preferred_element_type=jnp.float32)
    g_out = gout[: sizes.classes].T
    g_taps = small[:9]
    share_in = lax.psum_scatter(g_in, "dp", scatter_dimension=0, tiled=True)
    share_out = lax.psum_scatter(g_out, "dp", scatter_dimension=0, tiled=True)
    local = jnp.stack([jnp.sum(g_in * g_in), jnp.sum(g_taps * g_taps), jnp.sum(g_out * g_out)])
    share_sq = jnp.stack([jnp.sum(share_in * share_in), jnp.sum(share_out * share_out)])
    total_taps, squares, share_total = lax.psum((g_taps, local, share_sq), "dp")
    totals = jnp.stack([share_total[0], jnp.sum(total_taps * total_taps), share_total[1]])
    norms = jnp.log(1e-12 + jnp.stack([squares, totals]))
    return (share_in[None], total_taps[None], share_out[None], norms[None])


def solution(mesh):
    dp, trials = mesh.shape["dp"], mesh.shape["trial"]
    placed = (
        P(("groups", "dp"), "trial", None, None),
        P(("groups", "dp")),
        P("trial"),
        P(("groups", "dp"), None),
        P("trial", None, None),
        P("trial", None, None),
        P("trial", None, None),
    )

    def step(*args):
        (wide, hidden), classes = args[4].shape[1:], args[6].shape[2]
        return per_device(Sizes(wide, hidden, classes, dp), dp, trials, *args)

    return jax.shard_map(
        step,
        mesh=mesh,
        in_specs=placed,
        out_specs=(
            P(("groups", "trial"), "dp", None),
            P(("groups", "trial"), None, None),
            P(("groups", "trial"), "dp", None),
            P(("groups", "trial"), None, None),
        ),
        check_vma=False,
    )
```
